128 devices in a mesh: az: 8 (over z_lo, y), col: 16 (over z_hi, x, core).
Axes of the slice: x: 4, y: 4, z: 4 (z_hi: 2, z_lo: 2; z = z_hi * 2 + z_lo), core: 2. Of those that a mesh axis runs over, the one named last changes fastest.
Arguments:
- phase_field: float32 [64, 1024, 2048], P(None, 'col', 'az'), may hold values from -1 to 1
- velocity: bfloat16 [2, 64, 1024, 2048], P(None, None, 'col', 'az'), may hold values from -4 to 4
- owned_modes: int32 [128, 4], replicated, may hold values from 0 to 511, as said below
- legendre: bfloat16 [512, 1024, 512], P(('az', 'col')), as said below
- radial_inverse: bfloat16 [512, 64, 64], replicated, as said below
Outputs:
- new_phase: float32 [64, 1024, 2048], P(None, 'col', 'az')
The draws below stay inside these ranges and needn't reach their ends.
Inputs may be any that keep to these rules, and one draw needn't show every extreme that they name: `owned_modes`: every order from 0 to 511 appears exactly once; the second half of each row is 511 minus its first half. legendre[q, t, l] is the orthonormal associated Legendre function of degree l and order m_q (owned_modes flattened at q) at cos(theta_t), normalized so that the integral of its square times sin(theta) over theta is 1, rounded to bfloat16; it is 0 for l < m_q. `radial_inverse`: one matrix for each degree.
All inputs are finite; a program needn't handle non-finite values.
Results may differ from the reference program's by a relative error of at most 0.0003.
Values sent between devices are 32-bit elements; how exact they have to be, the bound alone decides.
No kernel may reach another device: no remote copies, remote signals or barrier semaphores. Data moves between devices by JAX's collectives and lax.ppermute only.
A program may use at most 192 MiB of HBM per device.

```python
import math
import jax
import jax.numpy as jnp
from jax import lax

NP = 2048
NT = 1024
DEGREES = 512
SHELLS = 64
MODES_DEV = 4


def ownership(key):
    pair_key = jax.random.fold_in(key, 23)
    pair_count = DEGREES // 2
    pair_order = jax.random.permutation(pair_key, pair_count).astype(jnp.int32)
    first_half = pair_order.reshape(-1, MODES_DEV // 2)
    return jnp.concatenate([first_half, DEGREES - 1 - first_half], axis=1).astype(jnp.int32)


def draw_owned_modes(key, part):
    return ownership(key)


def draw_legendre(key, part):
    mode_list = ownership(key).reshape(-1)
    orders = mode_list.astype(jnp.float32)[:, None]
    row_index = jnp.arange(NT, dtype=jnp.float32)
    colatitude = math.pi * (row_index + 0.5) / NT
    cosine = jnp.cos(colatitude)[None, :]
    sine_row = jnp.sin(colatitude)[None, :]
    log_start = 0.5 * math.log(0.5) + 0.5 * (jax.scipy.special.gammaln(orders + 1.5) - jax.scipy.special.gammaln(jnp.float32(1.5)) - jax.scipy.special.gammaln(orders + 1.0)) + orders * jnp.log(sine_row)
    diagonal_start = jnp.exp(log_start)

    def advance(state_pair, degree_id):
        one_back, two_back = state_pair
        degree = degree_id.astype(jnp.float32)
        denominator = jnp.maximum(degree * degree - orders * orders, 1.0)
        scale_up = jnp.sqrt(jnp.maximum(4.0 * degree * degree - 1.0, 1.0) / denominator)
        lower = degree - 1.0
        scale_back = jnp.sqrt(jnp.maximum(lower * lower - orders * orders, 0.0) / jnp.maximum(4.0 * lower * lower - 1.0, 1.0))
        recurred = scale_up * (cosine * one_back - scale_back * two_back)
        first_step = jnp.sqrt(2.0 * orders + 3.0) * cosine * one_back
        current = jnp.where(degree < orders, 0.0, jnp.where(degree == orders, diagonal_start, jnp.where(degree == orders + 1.0, first_step, recurred)))
        return ((current, one_back), current)
    zeros_start = jnp.zeros((DEGREES, NT), jnp.float32)
    final_pair, stacked = lax.scan(advance, (zeros_start, zeros_start), jnp.arange(DEGREES, dtype=jnp.int32))
    return jnp.transpose(stacked, (1, 2, 0)).astype(jnp.bfloat16)


def draw_radial_inverse(key, part):
    base_key = jax.random.fold_in(key, 5)
    diag_key = jax.random.fold_in(base_key, 1)
    off_key = jax.random.fold_in(base_key, 2)
    degree_scale = jnp.arange(DEGREES, dtype=jnp.float32)[:, None, None] / DEGREES
    off_diag = 0.35 * jax.random.normal(off_key, (DEGREES, SHELLS, SHELLS), jnp.float32) / math.sqrt(SHELLS)
    strength = jax.random.uniform(diag_key, (DEGREES, 1, SHELLS), jnp.float32, 0.5, 1.0) / (1.0 + 2.0 * degree_scale)
    identity = jnp.eye(SHELLS, dtype=jnp.float32)[None, :, :]
    matrix = off_diag * (1.0 - identity) + identity * strength
    return matrix.astype(jnp.bfloat16)


def steps_of(rng, extent, split, smallest, largest):
    gain = 1.0
    for position, blocks in split:
        steps = jax.random.uniform(jax.random.fold_in(jax.random.fold_in(rng, 6), position), (blocks,), jnp.float32, smallest / len(split), largest / len(split))
        gain = gain * jnp.repeat(jnp.exp(steps), extent[position] // blocks).reshape((-1,) + (1,) * (len(extent) - 1 - position))
    return gain


def scatter_about(key, extent, scale, most, shards=(), held_as=jnp.bfloat16):
    entries = scale * jax.random.normal(key, extent, jnp.float32)
    if shards:
        entries = entries * steps_of(key, extent, shards, -0.22, 0.18)
    return jnp.clip(entries, -most, most).astype(held_as)


def setup_inputs(seed: int = 0) -> dict:
    arg_keys = jax.random.split(jax.random.key(seed), 6)
    phase_field = jnp.clip(jax.random.uniform(arg_keys[0], (SHELLS, NT, NP), jnp.float32, -1.0, 1.0) * steps_of(arg_keys[0], (SHELLS, NT, NP), ((1, 16), (2, 8)), -0.4, 0.0), -1.0, 1.0)
    velocity = scatter_about(arg_keys[1], (2, SHELLS, NT, NP), 1.0, 4.0, ((2, 16), (3, 8)))
    owned_modes = draw_owned_modes(jax.random.fold_in(arg_keys[5], 71), 0)
    legendre = draw_legendre(jax.random.fold_in(arg_keys[5], 71), 0)
    radial_inverse = draw_radial_inverse(jax.random.fold_in(arg_keys[5], 71), 0)
    return dict(phase_field=phase_field, velocity=velocity, owned_modes=owned_modes, legendre=legendre, radial_inverse=radial_inverse)


step_time = 2.0e-3
mobility_step = 4.0e-6
highest_precision = lax.Precision.HIGHEST


def shell_radii(shells):
    return 0.75 + 0.25 * (jnp.arange(shells, dtype=jnp.float32) + 0.5) / shells


def colat_weights(count):
    row_index = jnp.arange(count, dtype=jnp.int32)
    waves = jnp.arange(1, count // 2 + 1, dtype=jnp.int32)
    turns = ((2 * row_index[:, None] + 1) * waves[None, :]) % (2 * count)
    cosines = jnp.cos(turns.astype(jnp.float32) * (math.pi / count))
    wave_float = waves.astype(jnp.float32)
    coefs = 1.0 / (4.0 * wave_float * wave_float - 1.0)
    return (2.0 / count) * (1.0 - 2.0 * jnp.dot(cosines, coefs, precision=highest_precision))


def reference(phase_field, velocity, owned_modes, legendre, radial_inverse):
    shells, theta_count, phi_count = phase_field.shape
    mode_list = owned_modes.reshape(-1).astype(jnp.int32)
    mode_count = mode_list.shape[0]
    degree_count = legendre.shape[2]
    legendre_full = legendre.astype(jnp.float32)
    shell_radius = shell_radii(shells)
    east_cell = jnp.roll(phase_field, -1, axis=2)
    west_cell = jnp.roll(phase_field, 1, axis=2)
    padded = jnp.pad(phase_field, ((0, 0), (1, 1), (0, 0)))
    south_cell = padded[:, 2:, :]
    north_cell = padded[:, :-2, :]
    d_phi = (east_cell - west_cell) * (phi_count / (4.0 * math.pi))
    d_theta = (south_cell - north_cell) * (theta_count / (2.0 * math.pi))
    spin_rate = velocity[0].astype(jnp.float32)
    sweep_speed = velocity[1].astype(jnp.float32)
    advected = phase_field - step_time * (spin_rate * d_phi + sweep_speed / shell_radius[:, None, None] * d_theta)
    potential = phase_field * phase_field * phase_field - phase_field
    fields = jnp.stack([advected, potential])
    spectrum = jnp.fft.rfft(fields, axis=-1) / phi_count
    picked = spectrum[..., mode_list]
    real_imag = jnp.stack([jnp.real(picked), jnp.imag(picked)]).astype(jnp.float32)
    arranged = jnp.transpose(real_imag, (4, 3, 0, 1, 2)).reshape(mode_count, theta_count, 4 * shells)
    weights = colat_weights(theta_count)
    weighted = arranged * weights[None, :, None]
    coeffs = jnp.einsum("ktx,ktl->klx", weighted.astype(jnp.float32), legendre_full, precision=highest_precision)
    coeffs = coeffs.reshape(mode_count, degree_count, 2, 2, shells)
    degrees = jnp.arange(degree_count, dtype=jnp.float32)
    factor = mobility_step * (degrees * (degrees + 1.0))[:, None] / (shell_radius * shell_radius)[None, :]
    right_side = coeffs[:, :, :, 0, :] - factor[None, :, None, :] * coeffs[:, :, :, 1, :]
    solved = jnp.einsum("lrs,klqs->klqr", radial_inverse.astype(jnp.float32), right_side, precision=highest_precision)
    synthesis = jnp.einsum("ktl,klx->ktx", legendre_full, solved.reshape(mode_count, degree_count, 2 * shells), precision=highest_precision)
    synthesis = synthesis.reshape(mode_count, theta_count, 2, shells)
    natural = jnp.argsort(mode_list)
    ordered = synthesis[natural]
    real_part = jnp.transpose(ordered[:, :, 0, :], (2, 1, 0))
    imag_part = jnp.transpose(ordered[:, :, 1, :], (2, 1, 0))
    complex_modes = lax.complex(real_part, imag_part)
    padded_modes = jnp.pad(complex_modes, ((0, 0), (0, 0), (0, phi_count // 2 + 1 - mode_count)))
    new_phase = phi_count * jnp.fft.irfft(padded_modes, n=phi_count, axis=-1)
    return new_phase.astype(jnp.float32)
```

```python
import math

import jax
import jax.numpy as jnp
import numpy as np
from jax import lax
from jax.experimental import pallas as pl
from jax.experimental.pallas import tpu as pltpu
from jax.sharding import PartitionSpec as P

step_time = 0.002
mobility_step = 4e-06
f32 = jnp.float32
bf16 = jnp.bfloat16
everyone = ("az", "col")


def params(mib=48):
    return pltpu.CompilerParams(vmem_limit_bytes=mib * 1024 * 1024)


def colat_weights(count):
    theta = math.pi * (np.arange(count) + 0.5) / count
    waves = np.arange(1, count // 2 + 1)
    total = (np.cos(2.0 * waves[None, :] * theta[:, None]) / (4.0 * waves * waves - 1.0)).sum(1)
    return 2.0 / count * (1.0 - 2.0 * total)


def shell_radii(shells):
    return 0.75 + 0.25 * (np.arange(shells) + 0.5) / shells


def split(x):
    hi = x.astype(bf16)
    return hi, (x - hi.astype(f32)).astype(bf16)


def dot_nn(a, b):
    return lax.dot_general(a, b, (((1,), (0,)), ((), ())), preferred_element_type=f32)


def dot_nt(a, b):
    return lax.dot_general(a, b, (((1,), (1,)), ((), ())), preferred_element_type=f32)


def swap_halves(a, b):
    half = lax.broadcasted_iota(jnp.int32, a.shape, 1) < 64
    first = jnp.where(half, a, pltpu.roll(b, 64, 1))
    second = jnp.where(half, pltpu.roll(a, 64, 1), b)
    return first, second


def edges_kernel(c_ref, west_ref, east_ref, north_ref, south_ref):
    shells, rows, cols = c_ref.shape
    block = pl.program_id(0)
    lane = lax.broadcasted_iota(jnp.int32, (rows, 128), 1)
    west = jnp.where(block == 0, 0.0, west_ref[...])
    east = jnp.where(block == 0, 0.0, east_ref[...])
    for k in range(shells):
        at = block * shells + k
        west = jnp.where(lane == at, pltpu.roll(c_ref[k, :, :128], at, 1), west)
        east = jnp.where(lane == at, pltpu.roll(c_ref[k, :, cols - 128 :], at + 1, 1), east)
    west_ref[...] = west
    east_ref[...] = east
    north_ref[...] = c_ref[:, 0, :]
    south_ref[...] = c_ref[:, rows - 1, :]


def edges_stage(phase):
    shells, rows, cols = phase.shape
    kb = 16
    return pl.pallas_call(
        edges_kernel,
        grid=(shells // kb,),
        in_specs=[pl.BlockSpec((kb, rows, cols), lambda i: (i, 0, 0))],
        out_specs=[
            pl.BlockSpec((rows, 128), lambda i: (0, 0)),
            pl.BlockSpec((rows, 128), lambda i: (0, 0)),
            pl.BlockSpec((kb, cols), lambda i: (i, 0)),
            pl.BlockSpec((kb, cols), lambda i: (i, 0)),
        ],
        out_shape=[
            jax.ShapeDtypeStruct((rows, 128), f32),
            jax.ShapeDtypeStruct((rows, 128), f32),
            jax.ShapeDtypeStruct((shells, cols), f32),
            jax.ShapeDtypeStruct((shells, cols), f32),
        ],
        compiler_params=params(61),
        name="edges",
    )(phase)


def potential_kernel(c_ref, w_ref, out_ref):
    shells, rows, cols = c_ref.shape
    weights = w_ref[...]
    for k in range(shells):
        x = c_ref[k]
        y = (x * x * x - x) * weights
        for a in range(rows // 8):
            for h in range(cols // 128):
                out_ref[a, k, h] = y[8 * a : 8 * a + 8, 128 * h : 128 * h + 128]


def potential_stage(phase, weights):
    shells, rows, cols = phase.shape
    kb = 8
    return pl.pallas_call(
        potential_kernel,
        grid=(shells // kb,),
        in_specs=[
            pl.BlockSpec((kb, rows, cols), lambda i: (i, 0, 0)),
            pl.BlockSpec((rows, cols), lambda i: (0, 0)),
        ],
        out_specs=pl.BlockSpec((rows // 8, kb, cols // 128, 8, 128), lambda i: (0, i, 0, 0, 0)),
        out_shape=jax.ShapeDtypeStruct((rows // 8, shells, cols // 128, 8, 128), f32),
        compiler_params=params(61),
        name="potential",
    )(phase, weights)


def advect_kernel(scale_phi, scale_ref, c_ref, v_ref, w_ref, west_ref, east_ref, north_ref, south_ref, out_ref):
    shells, rows, cols = c_ref.shape
    block = pl.program_id(0)
    weights = w_ref[...]
    lane = lax.broadcasted_iota(jnp.int32, (rows, cols), 1)
    row = lax.broadcasted_iota(jnp.int32, (rows, cols), 0)
    turn = jnp.where(block == 0, 0, 128 - block * shells)
    west_all = pltpu.roll(west_ref[...], turn, 1)
    east_all = pltpu.roll(east_ref[...], turn, 1)
    for k in range(shells):
        x = c_ref[k]
        west_edge = jnp.broadcast_to(west_all[:, k : k + 1], (rows, cols))
        east_edge = jnp.broadcast_to(east_all[:, k : k + 1], (rows, cols))
        west = jnp.where(lane == 0, west_edge, pltpu.roll(x, 1, 1))
        east = jnp.where(lane == cols - 1, east_edge, pltpu.roll(x, cols - 1, 1))
        north = jnp.where(row == 0, north_ref[k : k + 1, :], pltpu.roll(x, 1, 0))
        south = jnp.where(row == rows - 1, south_ref[k : k + 1, :], pltpu.roll(x, rows - 1, 0))
        spin = v_ref[0, k].astype(f32)
        sweep = v_ref[1, k].astype(f32)
        scale_theta = scale_ref[block * shells + k]
        y = x - (spin * ((east - west) * scale_phi) + sweep * ((south - north) * scale_theta))
        y = y * weights
        for a in range(rows // 8):
            for h in range(cols // 128):
                out_ref[a, k, h] = y[8 * a : 8 * a + 8, 128 * h : 128 * h + 128]


def advect_stage(phase, velocity, weights, west, east, north, south, scale_phi, scale_theta):
    shells, rows, cols = phase.shape
    kb = 8

    def kernel(*refs):
        advect_kernel(scale_phi, *refs)

    return pl.pallas_call(
        kernel,
        grid=(shells // kb,),
        in_specs=[
            pl.BlockSpec(memory_space=pltpu.SMEM),
            pl.BlockSpec((kb, rows, cols), lambda i: (i, 0, 0)),
            pl.BlockSpec((2, kb, rows, cols), lambda i: (0, i, 0, 0)),
            pl.BlockSpec((rows, cols), lambda i: (0, 0)),
            pl.BlockSpec((rows, 128), lambda i: (0, 0)),
            pl.BlockSpec((rows, 128), lambda i: (0, 0)),
            pl.BlockSpec((kb, cols), lambda i: (i, 0)),
            pl.BlockSpec((kb, cols), lambda i: (i, 0)),
        ],
        out_specs=pl.BlockSpec((rows // 8, kb, cols // 128, 8, 128), lambda i: (0, i, 0, 0, 0)),
        out_shape=jax.ShapeDtypeStruct((rows // 8, shells, cols // 128, 8, 128), f32),
        compiler_params=params(61),
        name="advect",
    )(scale_theta, phase, velocity, weights, west, east, north, south)


def fourier_kernel(p_ref, table_ref, *rest):
    out_ref, xh, xl, ysc = rest[-4:]
    parts = p_ref.shape[0]
    half = parts // 2
    per = xh.shape[0] // 8
    tiles = xh.shape[1] // half // 128
    sign = jnp.where(pl.program_id(0) == 0, 1.0, -1.0).astype(f32)
    for a in range(half):
        for t in range(8):
            for j in range(tiles):
                strided = pl.ds(8 * j + t, per, stride=8 * tiles)
                x = p_ref[a, strided, :] + sign * p_ref[a + half, strided, :]
                h, l = split(x)
                lanes = slice((a * tiles + j) * 128, (a * tiles + j + 1) * 128)
                xh[t * per : (t + 1) * per, lanes] = h
                xl[t * per : (t + 1) * per, lanes] = l
    ph, plo = xh[...], xl[...]
    both = table_ref.shape[1] // 2
    count = both // 2
    y = dot_nt(table_ref[0], ph)
    y = y[:both] + (y[both:] + dot_nt(table_ref[0, :both], plo))
    for u in range(4):
        first, second = swap_halves(y[:count, 128 * u : 128 * u + 128], y[count:, 128 * u : 128 * u + 128])
        ysc[pl.ds(2 * u, count, stride=8), :] = first
        ysc[pl.ds(2 * u + 1, count, stride=8), :] = second
    owners = count // 2
    for s in range(2):
        out_ref[:, 0, 0, s] = ysc[s * owners * 8 : (s + 1) * owners * 8, :].reshape(owners, 8, 128)


def fourier_stage(rows_all, table, field, buffer):
    parts, shells, tiles, tb, _ = rows_all.shape
    half_phi = table.shape[2]
    modes2 = table.shape[1] // 2
    owners = modes2 // 4
    flat = rows_all.reshape(parts, shells * tiles * tb, 128)
    in_specs = [
        pl.BlockSpec((parts, shells * tiles * tb, 128), lambda i: (0, 0, 0)),
        pl.BlockSpec((1, 2 * modes2, half_phi), lambda i: (i, 0, 0)),
    ]
    args = [flat, table]
    aliases = {}
    if buffer is not None:
        in_specs.append(pl.BlockSpec(memory_space=pl.ANY))
        args.append(buffer)
        aliases = {2: 0}
    return pl.pallas_call(
        fourier_kernel,
        grid=(2,),
        in_specs=in_specs,
        out_specs=pl.BlockSpec((owners, 1, 1, 2, 8, 128), lambda i: (0, field, i, 0, 0, 0)),
        out_shape=jax.ShapeDtypeStruct((owners, 2, 2, 2, 8, 128), f32),
        scratch_shapes=[
            pltpu.VMEM((shells * tb, half_phi), bf16),
            pltpu.VMEM((shells * tb, half_phi), bf16),
            pltpu.VMEM((modes2 * 4, 128), f32),
        ],
        input_output_aliases=aliases,
        compiler_params=params(61),
        name="fourier" + str(field),
    )(*args)


def spectral_kernel(az, col, sel_ref, r_ref, legt_ref, leg_ref, rad_ref, fac_ref, out_ref, xh, xl, rhs, sol, radf):
    step = pl.program_id(0)
    degrees = legt_ref.shape[1]
    shells = rad_ref.shape[0]
    theta = legt_ref.shape[2]
    tb = az * 8

    @pl.when(step < 4)
    def _():
        for f in range(2):
            for c in range(col):
                x = jnp.concatenate([r_ref[a * col + c, f, 0, 0] for a in range(az)], axis=0)
                h, l = split(x)
                xh[c * tb : (c + 1) * tb, f * 128 : (f + 1) * 128] = h
                xl[c * tb : (c + 1) * tb, f * 128 : (f + 1) * 128] = l
        leg = legt_ref[0]
        coef = dot_nn(leg, xh[...]) + dot_nn(leg, xl[...])
        right = (coef[:, :128] - fac_ref[...] * coef[:, 128:]).T
        for q in range(4):

            @pl.when(step == q)
            def _():
                for i in range(2):
                    for lt in range(degrees // 128):
                        rhs[lt, pl.ds(2 * q + i, shells, stride=8), :] = right[
                            i * shells : (i + 1) * shells, lt * 128 : lt * 128 + 128
                        ]

    @pl.when(step == 3)
    def _():
        rb = 8

        def outer(block, carry):
            radf[...] = rad_ref[pl.ds(block * rb, rb)].astype(f32)
            for lt in range(degrees // 128):
                lanes = slice(lt * 128, lt * 128 + 128)
                acc = [jnp.zeros((8, 128), f32) for _ in range(rb)]
                for s in range(shells):
                    v = rhs[lt, 8 * s : 8 * s + 8, :]
                    for r in range(rb):
                        acc[r] = acc[r] + radf[r, s : s + 1, lanes] * v
                for r in range(rb):
                    sol[lt, pl.ds(pl.multiple_of((block * rb + r) * 8, 8), 8), :] = acc[r]
            return carry

        lax.fori_loop(0, shells // rb, outer, 0)

    for q in range(4):

        @pl.when(step == 4 + q)
        def _():
            gain = sel_ref[4 + q].astype(f32)
            x = jnp.concatenate(
                [
                    jnp.concatenate(
                        [sol[lt, pl.ds(2 * q + i, shells, stride=8), :] for lt in range(degrees // 128)], axis=1
                    )
                    for i in range(2)
                ],
                axis=0,
            )
            h, l = split(x * gain)
            leg = leg_ref[0]
            y = dot_nt(leg, h) + dot_nt(leg, l)
            for c in range(col):
                for a in range(az):
                    out_ref[a * col + c, 0] = y[c * tb + a * 8 : c * tb + a * 8 + 8]


def spectral_stage(received, legendre_t, legendre, radial, factor, select, az, col):
    owners = received.shape[0]
    modes, theta, degrees = legendre.shape
    shells = radial.shape[0]

    def first(i):
        return jnp.minimum(i, 3)

    def last(i):
        return jnp.maximum(i - 4, 0)

    def kernel(*refs):
        spectral_kernel(az, col, *refs)

    return pl.pallas_call(
        kernel,
        grid_spec=pltpu.PrefetchScalarGridSpec(
            num_scalar_prefetch=1,
            grid=(8,),
            in_specs=[
                pl.BlockSpec((owners, 2, 1, 1, 8, 128), lambda i, s: (0, 0, first(i) // 2, first(i) % 2, 0, 0)),
                pl.BlockSpec((1, degrees, theta), lambda i, s: (s[first(i)], 0, 0)),
                pl.BlockSpec((1, theta, degrees), lambda i, s: (s[last(i)], 0, 0)),
                pl.BlockSpec((shells, shells, degrees), lambda i, s: (0, 0, 0)),
                pl.BlockSpec((degrees, 2 * shells), lambda i, s: (0, 0)),
            ],
            out_specs=pl.BlockSpec((owners, 1, 8, 128), lambda i, s: (0, last(i), 0, 0)),
            scratch_shapes=[
                pltpu.VMEM((theta, 256), bf16),
                pltpu.VMEM((theta, 256), bf16),
                pltpu.VMEM((degrees // 128, 8 * shells, 128), f32),
                pltpu.VMEM((degrees // 128, 8 * shells, 128), f32),
                pltpu.VMEM((8, shells, degrees), f32),
            ],
        ),
        out_shape=jax.ShapeDtypeStruct((owners, 4, 8, 128), f32),
        compiler_params=params(61),
        name="spectral",
    )(select, received, legendre_t, legendre, radial, factor)


def inverse_kernel(z_ref, table_ref, out_ref, gh, gl):
    owners = z_ref.shape[0] // 32
    rows = gh.shape[1]
    per = rows // 8

    @pl.when(pl.program_id(0) == 0)
    def _():
        for par in range(2):
            halves = [[], []]
            for s in range(2):
                base = (par * 2 + s) * 8
                cos_u, sin_u = [], []
                for u in range(4):
                    a = z_ref[pl.ds(base + 2 * u, owners, stride=32), :]
                    b = z_ref[pl.ds(base + 2 * u + 1, owners, stride=32), :]
                    first, second = swap_halves(a, b)
                    cos_u.append(first)
                    sin_u.append(second)
                halves[0].append(jnp.concatenate(cos_u, axis=1))
                halves[1].append(jnp.concatenate(sin_u, axis=1))
            for i in range(2):
                for s in range(2):
                    h, l = split(halves[i][s].T)
                    at = (2 * i + s) * owners
                    gh[par, :, at : at + owners] = h
                    gl[par, :, at : at + owners] = l

    sums = []
    for par in range(2):
        both = table_ref.shape[1] // 2
        th, tl = table_ref[par, :both], table_ref[par, both:]
        h, l = gh[par], gl[par]
        sums.append(dot_nn(h, th) + (dot_nn(h, tl) + dot_nn(l, th)))
    near = sums[0] + sums[1]
    far = sums[0] - sums[1]
    tiles = near.shape[1] // 128
    for t in range(8):
        for j in range(tiles):
            lanes = slice(j * 128, j * 128 + 128)
            strided = pl.ds(8 * j + t, per, stride=8 * tiles)
            out_ref[0, 0, strided, :] = near[t * per : (t + 1) * per, lanes]
            out_ref[1, 0, strided, :] = far[t * per : (t + 1) * per, lanes]


def inverse_stage(received, table, shells, az):
    owners, _, tb, _ = received.shape
    half_phi = table.shape[2]
    modes2 = table.shape[1] // 2
    flat = received.reshape(owners * 4 * tb, 128)
    cols = 2 * half_phi // az
    rows = shells * tb
    out = pl.pallas_call(
        inverse_kernel,
        grid=(az // 2,),
        in_specs=[
            pl.BlockSpec((owners * 4 * tb, 128), lambda i: (0, 0)),
            pl.BlockSpec((2, 2 * modes2, cols), lambda i: (0, 0, i)),
        ],
        out_specs=pl.BlockSpec((2, 1, rows * cols // 128, 128), lambda i: (0, i, 0, 0)),
        out_shape=jax.ShapeDtypeStruct((2, az // 2, rows * cols // 128, 128), f32),
        scratch_shapes=[
            pltpu.VMEM((2, rows, modes2), bf16),
            pltpu.VMEM((2, rows, modes2), bf16),
        ],
        compiler_params=params(24),
        name="inverse",
    )(flat, table)
    return out.reshape(az, shells, cols // 128, tb, 128)


def gather_kernel(w_ref, out_ref):
    parts, shells = w_ref.shape[:2]
    for k in range(shells):
        for a in range(parts):
            for h in range(w_ref.shape[2]):
                out_ref[k, 8 * a : 8 * a + 8, 128 * h : 128 * h + 128] = w_ref[a, k, h]


def gather_stage(blocks):
    parts, shells, tiles, tb, _ = blocks.shape
    cols = tiles * 128
    kb = 8
    return pl.pallas_call(
        gather_kernel,
        grid=(shells // kb,),
        in_specs=[pl.BlockSpec((parts, kb, tiles, tb, 128), lambda i: (0, i, 0, 0, 0))],
        out_specs=pl.BlockSpec((kb, parts * tb, cols), lambda i: (i, 0, 0)),
        out_shape=jax.ShapeDtypeStruct((shells, parts * tb, cols), f32),
        compiler_params=params(16),
        name="gather",
    )(blocks)


def exchange(x, axes):
    return lax.all_to_all(x, axes, split_axis=0, concat_axis=0, tiled=True)


def wave_tables(owned_modes, phi_count):
    first_half = owned_modes[:, :2].T.reshape(-1)
    top = owned_modes.shape[0] * owned_modes.shape[1] - 1
    even = jnp.where(first_half % 2 == 0, first_half, top - first_half)
    modes = jnp.stack([even, top - even])
    phi_index = jnp.arange(phi_count // 2, dtype=jnp.int32)
    quarter = jnp.arange(2, dtype=jnp.int32) * (phi_count // 4)
    turns = modes[:, None, :, None] * phi_index + quarter[None, :, None, None]
    turns = turns % phi_count
    table = jnp.cos(turns.astype(f32) * (2.0 * math.pi / phi_count))
    table = table.reshape(2, -1, phi_count // 2)
    rounded = lax.reduce_precision(table, 8, 7)
    return jnp.concatenate([rounded.astype(bf16), (table - rounded).astype(bf16)], axis=1)


def body(phase_field, velocity, owned_modes, legendre, radial_inverse):
    shells, theta_local, phi_local = phase_field.shape
    az_count = lax.axis_size("az")
    col_count = lax.axis_size("col")
    az_here = lax.axis_index("az")
    col_here = lax.axis_index("col")
    phi_count = phi_local * az_count
    theta_count = theta_local * col_count
    degree_count = legendre.shape[2]
    radius = shell_radii(shells)

    weights = jnp.asarray((colat_weights(theta_count) / phi_count).astype(np.float32))
    weights = lax.dynamic_slice(weights, (col_here * theta_local,), (theta_local,))
    weights = jnp.broadcast_to(weights[:, None], (theta_local, phi_local))

    west_out, east_out, north_out, south_out = edges_stage(phase_field)
    forward_az = [(i, (i + 1) % az_count) for i in range(az_count)]
    backward_az = [(target, source) for source, target in forward_az]
    forward_col = [(i, i + 1) for i in range(col_count - 1)]
    backward_col = [(target, source) for source, target in forward_col]
    west = lax.ppermute(east_out, "az", forward_az)
    east = lax.ppermute(west_out, "az", backward_az)
    north = lax.ppermute(south_out, "col", forward_col)
    south = lax.ppermute(north_out, "col", backward_col)
    potential = potential_stage(phase_field, weights)
    potential, west, east, north, south = lax.optimization_barrier((potential, west, east, north, south))
    rows_potential = exchange(potential, "az")

    scale_phi = step_time * phi_count / (4.0 * math.pi)
    scale_theta = jnp.asarray((step_time * theta_count / (2.0 * math.pi) / radius).astype(np.float32))
    advected = advect_stage(
        phase_field, velocity, weights, west, east, north, south, scale_phi, scale_theta
    )
    table = wave_tables(owned_modes, phi_count)
    rows_advected = exchange(advected, "az")

    spectra = fourier_stage(rows_potential, table, 1, None)
    spectra = fourier_stage(rows_advected, table, 0, spectra)
    received = exchange(spectra, everyone)

    here = az_here * col_count + col_here
    mine = lax.dynamic_slice(owned_modes, (here, 0), (1, owned_modes.shape[1]))[0]
    odd = mine[:2] % 2
    slot = jnp.arange(2, dtype=jnp.int32)
    even_slot = slot + 2 * odd
    odd_slot = slot + 2 * (1 - odd)
    slots = jnp.concatenate([even_slot, odd_slot])
    top = owned_modes.shape[0] * owned_modes.shape[1] - 1
    even_mode = jnp.where(odd == 0, mine[:2], top - mine[:2])
    gains = jnp.concatenate([jnp.where(even_mode == 0, 1, 2), jnp.full((2,), 2, jnp.int32)])
    select = jnp.concatenate([slots, gains]).astype(jnp.int32)
    degrees = np.arange(degree_count)
    factor = mobility_step * (degrees * (degrees + 1.0))[:, None] / (radius * radius)[None, :]
    factor = jnp.asarray(np.concatenate([factor, factor], axis=1).astype(np.float32))
    legendre_t = jnp.transpose(legendre, (0, 2, 1))
    radial = jnp.transpose(radial_inverse, (1, 2, 0))
    synthesis = spectral_stage(
        received, legendre_t, legendre, radial, factor, select, az_count, col_count
    )
    grid_modes = exchange(synthesis, everyone)

    blocks = inverse_stage(grid_modes, table, shells, az_count)
    return gather_stage(exchange(blocks, "az"))


def solution(mesh):
    in_specs = (
        P(None, "col", "az"),
        P(None, None, "col", "az"),
        P(),
        P(("az", "col"), None, None),
        P(),
    )
    out_specs = P(None, "col", "az")
    return jax.shard_map(body, mesh=mesh, in_specs=in_specs, out_specs=out_specs, check_vma=False)
```

```python
import math

import jax
import jax.numpy as jnp
import numpy as np
from jax import lax
from jax.experimental import pallas as pl
from jax.experimental.pallas import tpu as pltpu
from jax.sharding import PartitionSpec as P

step_time = 0.002
mobility_step = 4e-06
f32 = jnp.float32
bf16 = jnp.bfloat16
everyone = ("az", "col")


def params(mib=48):
    return pltpu.CompilerParams(vmem_limit_bytes=mib * 1024 * 1024)


def colat_weights(count):
    theta = math.pi * (np.arange(count) + 0.5) / count
    waves = np.arange(1, count // 2 + 1)
    total = (np.cos(2.0 * waves[None, :] * theta[:, None]) / (4.0 * waves * waves - 1.0)).sum(1)
    return 2.0 / count * (1.0 - 2.0 * total)


def shell_radii(shells):
    return 0.75 + 0.25 * (np.arange(shells) + 0.5) / shells


def split(x):
    hi = x.astype(bf16)
    return hi, (x - hi.astype(f32)).astype(bf16)


def dot_nn(a, b):
    return lax.dot_general(a, b, (((1,), (0,)), ((), ())), preferred_element_type=f32)


def dot_nt(a, b):
    return lax.dot_general(a, b, (((1,), (1,)), ((), ())), preferred_element_type=f32)


def swap_halves(a, b):
    half = lax.broadcasted_iota(jnp.int32, a.shape, 1) < 64
    first = jnp.where(half, a, pltpu.roll(b, 64, 1))
    second = jnp.where(half, pltpu.roll(a, 64, 1), b)
    return first, second


def edges_kernel(c_ref, west_ref, east_ref, north_ref, south_ref):
    shells, rows, cols = c_ref.shape
    block = pl.program_id(0)
    lane = lax.broadcasted_iota(jnp.int32, (rows, 128), 1)
    west = jnp.where(block == 0, 0.0, west_ref[...])
    east = jnp.where(block == 0, 0.0, east_ref[...])
    for k in range(shells):
        at = block * shells + k
        west = jnp.where(lane == at, pltpu.roll(c_ref[k, :, :128], at, 1), west)
        east = jnp.where(lane == at, pltpu.roll(c_ref[k, :, cols - 128 :], at + 1, 1), east)
    west_ref[...] = west
    east_ref[...] = east
    north_ref[...] = c_ref[:, 0, :]
    south_ref[...] = c_ref[:, rows - 1, :]


def edges_stage(phase):
    shells, rows, cols = phase.shape
    kb = 16
    return pl.pallas_call(
        edges_kernel,
        grid=(shells // kb,),
        in_specs=[pl.BlockSpec((kb, rows, cols), lambda i: (i, 0, 0))],
        out_specs=[
            pl.BlockSpec((rows, 128), lambda i: (0, 0)),
            pl.BlockSpec((rows, 128), lambda i: (0, 0)),
            pl.BlockSpec((kb, cols), lambda i: (i, 0)),
            pl.BlockSpec((kb, cols), lambda i: (i, 0)),
        ],
        out_shape=[
            jax.ShapeDtypeStruct((rows, 128), f32),
            jax.ShapeDtypeStruct((rows, 128), f32),
            jax.ShapeDtypeStruct((shells, cols), f32),
            jax.ShapeDtypeStruct((shells, cols), f32),
        ],
        compiler_params=params(61),
        name="edges",
    )(phase)


def stencil_kernel(scale_phi, scale_ref, c_ref, v_ref, w_ref, west_ref, east_ref, north_ref, south_ref, out_ref):
    shells, rows, cols = c_ref.shape
    block = pl.program_id(0)
    weights = w_ref[...]
    lane = lax.broadcasted_iota(jnp.int32, (rows, cols), 1)
    row = lax.broadcasted_iota(jnp.int32, (rows, cols), 0)
    turn = jnp.where(block == 0, 0, 128 - block * shells)
    west_all = pltpu.roll(west_ref[...], turn, 1)
    east_all = pltpu.roll(east_ref[...], turn, 1)
    for k in range(shells):
        x = c_ref[k]
        west_edge = jnp.broadcast_to(west_all[:, k : k + 1], (rows, cols))
        east_edge = jnp.broadcast_to(east_all[:, k : k + 1], (rows, cols))
        west = jnp.where(lane == 0, west_edge, pltpu.roll(x, 1, 1))
        east = jnp.where(lane == cols - 1, east_edge, pltpu.roll(x, cols - 1, 1))
        north = jnp.where(row == 0, north_ref[k : k + 1, :], pltpu.roll(x, 1, 0))
        south = jnp.where(row == rows - 1, south_ref[k : k + 1, :], pltpu.roll(x, rows - 1, 0))
        spin = v_ref[0, k].astype(f32)
        sweep = v_ref[1, k].astype(f32)
        scale_theta = scale_ref[block * shells + k]
        y = x - (spin * ((east - west) * scale_phi) + sweep * ((south - north) * scale_theta))
        y = y * weights
        z = (x * x * x - x) * weights
        for a in range(rows // 8):
            for h in range(cols // 128):
                out_ref[a, 0, k, h] = y[8 * a : 8 * a + 8, 128 * h : 128 * h + 128]
                out_ref[a, 1, k, h] = z[8 * a : 8 * a + 8, 128 * h : 128 * h + 128]


def stencil_stage(phase, velocity, weights, west, east, north, south, scale_phi, scale_theta):
    shells, rows, cols = phase.shape
    kb = 8

    def kernel(*refs):
        stencil_kernel(scale_phi, *refs)

    return pl.pallas_call(
        kernel,
        grid=(shells // kb,),
        in_specs=[
            pl.BlockSpec(memory_space=pltpu.SMEM),
            pl.BlockSpec((kb, rows, cols), lambda i: (i, 0, 0)),
            pl.BlockSpec((2, kb, rows, cols), lambda i: (0, i, 0, 0)),
            pl.BlockSpec((rows, cols), lambda i: (0, 0)),
            pl.BlockSpec((rows, 128), lambda i: (0, 0)),
            pl.BlockSpec((rows, 128), lambda i: (0, 0)),
            pl.BlockSpec((kb, cols), lambda i: (i, 0)),
            pl.BlockSpec((kb, cols), lambda i: (i, 0)),
        ],
        out_specs=pl.BlockSpec((rows // 8, 2, kb, cols // 128, 8, 128), lambda i: (0, 0, i, 0, 0, 0)),
        out_shape=jax.ShapeDtypeStruct((rows // 8, 2, shells, cols // 128, 8, 128), f32),
        compiler_params=params(54),
        name="stencil",
    )(scale_theta, phase, velocity, weights, west, east, north, south)


def table_kernel(fine_ref, coarse_ref, out_ref):
    modes = fine_ref.shape[2]
    tiles = out_ref.shape[2] // 128
    fc, fs = fine_ref[0, 0], fine_ref[1, 0]
    for u in range(tiles):
        cc = jnp.broadcast_to(coarse_ref[0, 0, :, u : u + 1], (modes, 128))
        cs = jnp.broadcast_to(coarse_ref[1, 0, :, u : u + 1], (modes, 128))
        for i, value in enumerate((fc * cc - fs * cs, fs * cc + fc * cs)):
            h, l = split(value)
            lanes = slice(128 * u, 128 * u + 128)
            out_ref[0, i * modes : (i + 1) * modes, lanes] = h
            out_ref[0, (2 + i) * modes : (3 + i) * modes, lanes] = l


def wave_tables(owned_modes, phi_count):
    first_half = owned_modes[:, :2].T.reshape(-1)
    top = owned_modes.shape[0] * owned_modes.shape[1] - 1
    even = jnp.where(first_half % 2 == 0, first_half, top - first_half)
    modes = jnp.stack([even, top - even])
    count = modes.shape[1]
    half_phi = phi_count // 2

    def waves(step):
        quarter = jnp.arange(2, dtype=jnp.int32) * (phi_count // 4)
        lanes = jnp.arange(128, dtype=jnp.int32) * step
        turns = (modes[None, :, :, None] * lanes + quarter[:, None, None, None]) % phi_count
        return jnp.cos(turns.astype(f32) * (2.0 * math.pi / phi_count))

    return pl.pallas_call(
        table_kernel,
        grid=(2,),
        in_specs=[
            pl.BlockSpec((2, 1, count, 128), lambda i: (0, i, 0, 0)),
            pl.BlockSpec((2, 1, count, 128), lambda i: (0, i, 0, 0)),
        ],
        out_specs=pl.BlockSpec((1, 4 * count, half_phi), lambda i: (i, 0, 0)),
        out_shape=jax.ShapeDtypeStruct((2, 4 * count, half_phi), bf16),
        compiler_params=params(40),
        name="table",
    )(waves(1), waves(128))


def fourier_kernel(p_ref, table_ref, out_ref, xh, xl, ysc):
    parts = p_ref.shape[0]
    half = parts // 2
    per = xh.shape[0] // 8
    tiles = xh.shape[1] // half // 128
    sign = jnp.where(pl.program_id(1) == 0, 1.0, -1.0).astype(f32)
    for a in range(half):
        for t in range(8):
            for j in range(tiles):
                strided = pl.ds(8 * j + t, per, stride=8 * tiles)
                x = p_ref[a, 0, strided, :] + sign * p_ref[a + half, 0, strided, :]
                h, l = split(x)
                lanes = slice((a * tiles + j) * 128, (a * tiles + j + 1) * 128)
                xh[t * per : (t + 1) * per, lanes] = h
                xl[t * per : (t + 1) * per, lanes] = l
    ph, plo = xh[...], xl[...]
    both = table_ref.shape[1] // 2
    count = both // 2
    y = dot_nt(table_ref[0], ph)
    y = y[:both] + (y[both:] + dot_nt(table_ref[0, :both], plo))
    for u in range(4):
        first, second = swap_halves(y[:count, 128 * u : 128 * u + 128], y[count:, 128 * u : 128 * u + 128])
        ysc[pl.ds(2 * u, count, stride=8), :] = first
        ysc[pl.ds(2 * u + 1, count, stride=8), :] = second
    owners = count // 2
    for s in range(2):
        out_ref[:, 0, 0, s] = ysc[s * owners * 8 : (s + 1) * owners * 8, :].reshape(owners, 8, 128)


def fourier_stage(rows_all, table):
    parts, fields, shells, tiles, tb, _ = rows_all.shape
    half_phi = table.shape[2]
    modes2 = table.shape[1] // 2
    owners = modes2 // 4
    flat = rows_all.reshape(parts, fields, shells * tiles * tb, 128)
    return pl.pallas_call(
        fourier_kernel,
        grid=(fields, 2),
        in_specs=[
            pl.BlockSpec((parts, 1, shells * tiles * tb, 128), lambda f, i: (0, f, 0, 0)),
            pl.BlockSpec((1, 2 * modes2, half_phi), lambda f, i: (i, 0, 0)),
        ],
        out_specs=pl.BlockSpec((owners, 1, 1, 2, 8, 128), lambda f, i: (0, f, i, 0, 0, 0)),
        out_shape=jax.ShapeDtypeStruct((owners, fields, 2, 2, 8, 128), f32),
        scratch_shapes=[
            pltpu.VMEM((shells * tb, half_phi), bf16),
            pltpu.VMEM((shells * tb, half_phi), bf16),
            pltpu.VMEM((modes2 * 4, 128), f32),
        ],
        compiler_params=params(40),
        name="fourier",
    )(flat, table)


def spectral_kernel(az, col, sel_ref, r_ref, legt_ref, leg_ref, rad_ref, fac_ref, out_ref, xh, xl, rhs, sol, radf):
    step = pl.program_id(0)
    degrees = legt_ref.shape[1]
    shells = rad_ref.shape[0]
    theta = legt_ref.shape[2]
    tb = az * 8

    @pl.when(step < 4)
    def _():
        for f in range(2):
            for c in range(col):
                x = jnp.concatenate([r_ref[a * col + c, f, 0, 0] for a in range(az)], axis=0)
                h, l = split(x)
                xh[c * tb : (c + 1) * tb, f * 128 : (f + 1) * 128] = h
                xl[c * tb : (c + 1) * tb, f * 128 : (f + 1) * 128] = l
        leg = legt_ref[0]
        coef = dot_nn(leg, xh[...]) + dot_nn(leg, xl[...])
        right = (coef[:, :128] - fac_ref[...] * coef[:, 128:]).T
        for q in range(4):

            @pl.when(step == q)
            def _():
                for i in range(2):
                    for lt in range(degrees // 128):
                        rhs[lt, pl.ds(2 * q + i, shells, stride=8), :] = right[
                            i * shells : (i + 1) * shells, lt * 128 : lt * 128 + 128
                        ]

    @pl.when(step == 3)
    def _():
        rb = 8

        def outer(block, carry):
            radf[...] = rad_ref[pl.ds(block * rb, rb)].astype(f32)
            for lt in range(degrees // 128):
                lanes = slice(lt * 128, lt * 128 + 128)
                acc = [jnp.zeros((8, 128), f32) for _ in range(rb)]
                for s in range(shells):
                    v = rhs[lt, 8 * s : 8 * s + 8, :]
                    for r in range(rb):
                        acc[r] = acc[r] + radf[r, s : s + 1, lanes] * v
                for r in range(rb):
                    sol[lt, pl.ds(pl.multiple_of((block * rb + r) * 8, 8), 8), :] = acc[r]
            return carry

        lax.fori_loop(0, shells // rb, outer, 0)

    for q in range(4):

        @pl.when(step == 4 + q)
        def _():
            gain = sel_ref[4 + q].astype(f32)
            x = jnp.concatenate(
                [
                    jnp.concatenate(
                        [sol[lt, pl.ds(2 * q + i, shells, stride=8), :] for lt in range(degrees // 128)], axis=1
                    )
                    for i in range(2)
                ],
                axis=0,
            )
            h, l = split(x * gain)
            leg = leg_ref[0]
            y = dot_nt(leg, h) + dot_nt(leg, l)
            for c in range(col):
                for a in range(az):
                    out_ref[a * col + c, 0] = y[c * tb + a * 8 : c * tb + a * 8 + 8]


def spectral_stage(received, legendre_t, legendre, radial, factor, select, az, col):
    owners = received.shape[0]
    modes, theta, degrees = legendre.shape
    shells = radial.shape[0]

    def first(i):
        return jnp.minimum(i, 3)

    def last(i):
        return jnp.maximum(i - 4, 0)

    def kernel(*refs):
        spectral_kernel(az, col, *refs)

    return pl.pallas_call(
        kernel,
        grid_spec=pltpu.PrefetchScalarGridSpec(
            num_scalar_prefetch=1,
            grid=(8,),
            in_specs=[
                pl.BlockSpec((owners, 2, 1, 1, 8, 128), lambda i, s: (0, 0, first(i) // 2, first(i) % 2, 0, 0)),
                pl.BlockSpec((1, degrees, theta), lambda i, s: (s[first(i)], 0, 0)),
                pl.BlockSpec((1, theta, degrees), lambda i, s: (s[last(i)], 0, 0)),
                pl.BlockSpec((shells, shells, degrees), lambda i, s: (0, 0, 0)),
                pl.BlockSpec((degrees, 2 * shells), lambda i, s: (0, 0)),
            ],
            out_specs=pl.BlockSpec((owners, 1, 8, 128), lambda i, s: (0, last(i), 0, 0)),
            scratch_shapes=[
                pltpu.VMEM((theta, 256), bf16),
                pltpu.VMEM((theta, 256), bf16),
                pltpu.VMEM((degrees // 128, 8 * shells, 128), f32),
                pltpu.VMEM((degrees // 128, 8 * shells, 128), f32),
                pltpu.VMEM((8, shells, degrees), f32),
            ],
        ),
        out_shape=jax.ShapeDtypeStruct((owners, 4, 8, 128), f32),
        compiler_params=params(61),
        name="spectral",
    )(select, received, legendre_t, legendre, radial, factor)


def inverse_kernel(z_ref, table_ref, out_ref, gh, gl):
    owners = z_ref.shape[0] // 32
    rows = gh.shape[1]
    per = rows // 8

    @pl.when(pl.program_id(0) == 0)
    def _():
        for par in range(2):
            halves = [[], []]
            for s in range(2):
                base = (par * 2 + s) * 8
                cos_u, sin_u = [], []
                for u in range(4):
                    a = z_ref[pl.ds(base + 2 * u, owners, stride=32), :]
                    b = z_ref[pl.ds(base + 2 * u + 1, owners, stride=32), :]
                    first, second = swap_halves(a, b)
                    cos_u.append(first)
                    sin_u.append(second)
                halves[0].append(jnp.concatenate(cos_u, axis=1))
                halves[1].append(jnp.concatenate(sin_u, axis=1))
            for i in range(2):
                for s in range(2):
                    h, l = split(halves[i][s].T)
                    at = (2 * i + s) * owners
                    gh[par, :, at : at + owners] = h
                    gl[par, :, at : at + owners] = l

    sums = []
    for par in range(2):
        both = table_ref.shape[1] // 2
        th, tl = table_ref[par, :both], table_ref[par, both:]
        h, l = gh[par], gl[par]
        sums.append(dot_nn(h, th) + (dot_nn(h, tl) + dot_nn(l, th)))
    near = sums[0] + sums[1]
    far = sums[0] - sums[1]
    tiles = near.shape[1] // 128
    for t in range(8):
        for j in range(tiles):
            lanes = slice(j * 128, j * 128 + 128)
            strided = pl.ds(8 * j + t, per, stride=8 * tiles)
            out_ref[0, 0, strided, :] = near[t * per : (t + 1) * per, lanes]
            out_ref[1, 0, strided, :] = far[t * per : (t + 1) * per, lanes]


def inverse_stage(received, table, shells, az):
    owners, _, tb, _ = received.shape
    half_phi = table.shape[2]
    modes2 = table.shape[1] // 2
    flat = received.reshape(owners * 4 * tb, 128)
    cols = 2 * half_phi // az
    rows = shells * tb
    out = pl.pallas_call(
        inverse_kernel,
        grid=(az // 2,),
        in_specs=[
            pl.BlockSpec((owners * 4 * tb, 128), lambda i: (0, 0)),
            pl.BlockSpec((2, 2 * modes2, cols), lambda i: (0, 0, i)),
        ],
        out_specs=pl.BlockSpec((2, 1, rows * cols // 128, 128), lambda i: (0, i, 0, 0)),
        out_shape=jax.ShapeDtypeStruct((2, az // 2, rows * cols // 128, 128), f32),
        scratch_shapes=[
            pltpu.VMEM((2, rows, modes2), bf16),
            pltpu.VMEM((2, rows, modes2), bf16),
        ],
        compiler_params=params(24),
        name="inverse",
    )(flat, table)
    return out.reshape(az, shells, cols // 128, tb, 128)


def gather_kernel(w_ref, out_ref):
    parts, shells = w_ref.shape[:2]
    for k in range(shells):
        for a in range(parts):
            for h in range(w_ref.shape[2]):
                out_ref[k, 8 * a : 8 * a + 8, 128 * h : 128 * h + 128] = w_ref[a, k, h]


def gather_stage(blocks):
    parts, shells, tiles, tb, _ = blocks.shape
    cols = tiles * 128
    kb = 8
    return pl.pallas_call(
        gather_kernel,
        grid=(shells // kb,),
        in_specs=[pl.BlockSpec((parts, kb, tiles, tb, 128), lambda i: (0, i, 0, 0, 0))],
        out_specs=pl.BlockSpec((kb, parts * tb, cols), lambda i: (i, 0, 0)),
        out_shape=jax.ShapeDtypeStruct((shells, parts * tb, cols), f32),
        compiler_params=params(16),
        name="gather",
    )(blocks)


def exchange(x, axes):
    return lax.all_to_all(x, axes, split_axis=0, concat_axis=0, tiled=True)


def body(phase_field, velocity, owned_modes, legendre, radial_inverse):
    shells, theta_local, phi_local = phase_field.shape
    az_count = lax.axis_size("az")
    col_count = lax.axis_size("col")
    az_here = lax.axis_index("az")
    col_here = lax.axis_index("col")
    phi_count = phi_local * az_count
    theta_count = theta_local * col_count
    degree_count = legendre.shape[2]
    radius = shell_radii(shells)

    weights = jnp.asarray((colat_weights(theta_count) / phi_count).astype(np.float32))
    weights = lax.dynamic_slice(weights, (col_here * theta_local,), (theta_local,))
    weights = jnp.broadcast_to(weights[:, None], (theta_local, phi_local))

    west_out, east_out, north_out, south_out = edges_stage(phase_field)
    forward_az = [(i, (i + 1) % az_count) for i in range(az_count)]
    backward_az = [(target, source) for source, target in forward_az]
    forward_col = [(i, i + 1) for i in range(col_count - 1)]
    backward_col = [(target, source) for source, target in forward_col]
    west = lax.ppermute(east_out, "az", forward_az)
    east = lax.ppermute(west_out, "az", backward_az)
    north = lax.ppermute(south_out, "col", forward_col)
    south = lax.ppermute(north_out, "col", backward_col)

    here = az_here * col_count + col_here
    mine = lax.dynamic_slice(owned_modes, (here, 0), (1, owned_modes.shape[1]))[0]
    odd = mine[:2] % 2
    slot = jnp.arange(2, dtype=jnp.int32)
    even_slot = slot + 2 * odd
    odd_slot = slot + 2 * (1 - odd)
    slots = jnp.concatenate([even_slot, odd_slot])
    top = owned_modes.shape[0] * owned_modes.shape[1] - 1
    even_mode = jnp.where(odd == 0, mine[:2], top - mine[:2])
    gains = jnp.concatenate([jnp.where(even_mode == 0, 1, 2), jnp.full((2,), 2, jnp.int32)])
    select = jnp.concatenate([slots, gains]).astype(jnp.int32)
    degrees = np.arange(degree_count)
    factor = mobility_step * (degrees * (degrees + 1.0))[:, None] / (radius * radius)[None, :]
    factor = jnp.asarray(np.concatenate([factor, factor], axis=1).astype(np.float32))
    legendre_t = jnp.transpose(legendre, (0, 2, 1))
    radial = jnp.transpose(radial_inverse, (1, 2, 0))
    table = wave_tables(owned_modes, phi_count)

    scale_phi = step_time * phi_count / (4.0 * math.pi)
    scale_theta = jnp.asarray((step_time * theta_count / (2.0 * math.pi) / radius).astype(np.float32))
    fields = stencil_stage(
        phase_field, velocity, weights, west, east, north, south, scale_phi, scale_theta
    )
    fields, table, select, legendre_t = lax.optimization_barrier((fields, table, select, legendre_t))
    received = exchange(fourier_stage(exchange(fields, "az"), table), everyone)
    synthesis = spectral_stage(
        received, legendre_t, legendre, radial, factor, select, az_count, col_count
    )
    grid_modes = exchange(synthesis, everyone)

    blocks = inverse_stage(grid_modes, table, shells, az_count)
    return gather_stage(exchange(blocks, "az"))


def solution(mesh):
    in_specs = (
        P(None, "col", "az"),
        P(None, None, "col", "az"),
        P(),
        P(("az", "col"), None, None),
        P(),
    )
    out_specs = P(None, "col", "az")
    return jax.shard_map(body, mesh=mesh, in_specs=in_specs, out_specs=out_specs, check_vma=False)
```

```python
import math

import jax
import jax.numpy as jnp
import numpy as np
from jax import lax
from jax.experimental import pallas as pl
from jax.experimental.pallas import tpu as pltpu
from jax.sharding import PartitionSpec as P

step_time = 0.002
mobility_step = 4e-06
f32 = jnp.float32
bf16 = jnp.bfloat16
everyone = ("az", "col")


def params(mib=48):
    return pltpu.CompilerParams(vmem_limit_bytes=mib * 1024 * 1024)


def colat_weights(count):
    theta = math.pi * (np.arange(count) + 0.5) / count
    waves = np.arange(1, count // 2 + 1)
    total = (np.cos(2.0 * waves[None, :] * theta[:, None]) / (4.0 * waves * waves - 1.0)).sum(1)
    return 2.0 / count * (1.0 - 2.0 * total)


def shell_radii(shells):
    return 0.75 + 0.25 * (np.arange(shells) + 0.5) / shells


def split(x):
    hi = x.astype(bf16)
    return hi, (x - hi.astype(f32)).astype(bf16)


def dot_nn(a, b):
    return lax.dot_general(a, b, (((1,), (0,)), ((), ())), preferred_element_type=f32)


def dot_nt(a, b):
    return lax.dot_general(a, b, (((1,), (1,)), ((), ())), preferred_element_type=f32)


def swap_halves(a, b):
    half = lax.broadcasted_iota(jnp.int32, a.shape, 1) < 64
    first = jnp.where(half, a, pltpu.roll(b, 64, 1))
    second = jnp.where(half, pltpu.roll(a, 64, 1), b)
    return first, second


def edges_kernel(c_ref, west_ref, east_ref, north_ref, south_ref):
    shells, rows, cols = c_ref.shape
    block = pl.program_id(0)
    lane = lax.broadcasted_iota(jnp.int32, (rows, 128), 1)
    west = jnp.where(block == 0, 0.0, west_ref[...])
    east = jnp.where(block == 0, 0.0, east_ref[...])
    for k in range(shells):
        at = block * shells + k
        west = jnp.where(lane == at, pltpu.roll(c_ref[k, :, :128], at, 1), west)
        east = jnp.where(lane == at, pltpu.roll(c_ref[k, :, cols - 128 :], at + 1, 1), east)
    west_ref[...] = west
    east_ref[...] = east
    north_ref[...] = c_ref[:, 0, :]
    south_ref[...] = c_ref[:, rows - 1, :]


def edges_stage(phase):
    shells, rows, cols = phase.shape
    kb = 16
    return pl.pallas_call(
        edges_kernel,
        grid=(shells // kb,),
        in_specs=[pl.BlockSpec((kb, rows, cols), lambda i: (i, 0, 0))],
        out_specs=[
            pl.BlockSpec((rows, 128), lambda i: (0, 0)),
            pl.BlockSpec((rows, 128), lambda i: (0, 0)),
            pl.BlockSpec((kb, cols), lambda i: (i, 0)),
            pl.BlockSpec((kb, cols), lambda i: (i, 0)),
        ],
        out_shape=[
            jax.ShapeDtypeStruct((rows, 128), f32),
            jax.ShapeDtypeStruct((rows, 128), f32),
            jax.ShapeDtypeStruct((shells, cols), f32),
            jax.ShapeDtypeStruct((shells, cols), f32),
        ],
        compiler_params=params(61),
        name="edges",
    )(phase)


def stencil_kernel(scale_phi, where_ref, scale_ref, c_ref, v_ref, w_ref, west_ref, east_ref, north_ref, south_ref, out_ref):
    shells, rows, cols = c_ref.shape
    block = pl.program_id(0)
    weights = jnp.concatenate([w_ref[...]] * (cols // 128), axis=1)
    lane = lax.broadcasted_iota(jnp.int32, (rows, cols), 1)
    row = lax.broadcasted_iota(jnp.int32, (rows, cols), 0)
    turn = jnp.where(block == 0, 0, 128 - block * shells)
    west_all = pltpu.roll(west_ref[...], turn, 1)
    east_all = pltpu.roll(east_ref[...], turn, 1)
    for k in range(shells):
        x = c_ref[k]
        west_edge = jnp.broadcast_to(west_all[:, k : k + 1], (rows, cols))
        east_edge = jnp.broadcast_to(east_all[:, k : k + 1], (rows, cols))
        west = jnp.where(lane == 0, west_edge, pltpu.roll(x, 1, 1))
        east = jnp.where(lane == cols - 1, east_edge, pltpu.roll(x, cols - 1, 1))
        north = jnp.where(row == 0, north_ref[k : k + 1, :], pltpu.roll(x, 1, 0))
        south = jnp.where(row == rows - 1, south_ref[k : k + 1, :], pltpu.roll(x, rows - 1, 0))
        spin = v_ref[0, k].astype(f32)
        sweep = v_ref[1, k].astype(f32)
        scale_theta = scale_ref[block * shells + k]
        y = x - (spin * ((east - west) * scale_phi) + sweep * ((south - north) * scale_theta))
        y = y * weights
        z = (x * x * x - x) * weights
        for a in range(rows // 8):
            for h in range(cols // 128):
                out_ref[a, 0, k, h] = y[8 * a : 8 * a + 8, 128 * h : 128 * h + 128]
                out_ref[a, 1, k, h] = z[8 * a : 8 * a + 8, 128 * h : 128 * h + 128]


def stencil_stage(phase, velocity, weights, where, west, east, north, south, scale_phi, scale_theta):
    shells, rows, cols = phase.shape
    kb = 16

    def kernel(*refs):
        stencil_kernel(scale_phi, *refs)

    return pl.pallas_call(
        kernel,
        grid_spec=pltpu.PrefetchScalarGridSpec(
            num_scalar_prefetch=1,
            grid=(shells // kb,),
            in_specs=[
                pl.BlockSpec(memory_space=pltpu.SMEM),
                pl.BlockSpec((kb, rows, cols), lambda i, s: (i, 0, 0)),
                pl.BlockSpec((2, kb, rows, cols), lambda i, s: (0, i, 0, 0)),
                pl.BlockSpec((rows, 128), lambda i, s: (s[0], 0)),
                pl.BlockSpec((rows, 128), lambda i, s: (0, 0)),
                pl.BlockSpec((rows, 128), lambda i, s: (0, 0)),
                pl.BlockSpec((kb, cols), lambda i, s: (i, 0)),
                pl.BlockSpec((kb, cols), lambda i, s: (i, 0)),
            ],
            out_specs=pl.BlockSpec((rows // 8, 2, kb, cols // 128, 8, 128), lambda i, s: (0, 0, i, 0, 0, 0)),
        ),
        out_shape=jax.ShapeDtypeStruct((rows // 8, 2, shells, cols // 128, 8, 128), f32),
        compiler_params=params(48),
        name="stencil",
    )(where, scale_theta, phase, velocity, weights, west, east, north, south)


def table_kernel(fine_ref, coarse_ref, out_ref):
    modes = fine_ref.shape[2]
    tiles = out_ref.shape[2] // 128
    fc, fs = fine_ref[0, 0], fine_ref[1, 0]
    coarse = [coarse_ref[i, 0].T for i in range(2)]
    for u in range(tiles):
        cc = jnp.broadcast_to(coarse[0][:, u : u + 1], (modes, 128))
        cs = jnp.broadcast_to(coarse[1][:, u : u + 1], (modes, 128))
        for i, value in enumerate((fc * cc - fs * cs, fs * cc + fc * cs)):
            h, l = split(value)
            lanes = slice(128 * u, 128 * u + 128)
            out_ref[0, i * modes : (i + 1) * modes, lanes] = h
            out_ref[0, (2 + i) * modes : (3 + i) * modes, lanes] = l


def wave_tables(owned_modes, phi_count):
    first_half = owned_modes[:, :2].T.reshape(-1)
    top = owned_modes.shape[0] * owned_modes.shape[1] - 1
    even = jnp.where(first_half % 2 == 0, first_half, top - first_half)
    modes = jnp.stack([even, top - even])
    count = modes.shape[1]
    half_phi = phi_count // 2

    quarter = jnp.arange(2, dtype=jnp.int32) * (phi_count // 4)

    def waves(turns):
        turns = (turns + quarter[:, None, None, None]) % phi_count
        return jnp.cos(turns.astype(f32) * (2.0 * math.pi / phi_count))

    lanes = jnp.arange(128, dtype=jnp.int32)
    tiles = jnp.arange(half_phi // 128, dtype=jnp.int32) * 128
    fine = waves(modes[None, :, :, None] * lanes)
    coarse = waves(modes[None, :, None, :] * tiles[:, None])

    return pl.pallas_call(
        table_kernel,
        grid=(2,),
        in_specs=[
            pl.BlockSpec((2, 1, count, 128), lambda i: (0, i, 0, 0)),
            pl.BlockSpec((2, 1, half_phi // 128, count), lambda i: (0, i, 0, 0)),
        ],
        out_specs=pl.BlockSpec((1, 4 * count, half_phi), lambda i: (i, 0, 0)),
        out_shape=jax.ShapeDtypeStruct((2, 4 * count, half_phi), bf16),
        compiler_params=params(40),
        name="table",
    )(fine, coarse)


def fourier_kernel(p_ref, table_ref, out_ref, xh, xl, ysc):
    parts, fields = p_ref.shape[:2]
    half = parts // 2
    per = xh.shape[0] // 8
    tiles = xh.shape[1] // half // 128
    both = table_ref.shape[1] // 2
    count = both // 2
    owners = count // 2

    def one(index, carry):
        f, parity = index // 2, index % 2
        sign = jnp.where(parity == 0, 1.0, -1.0).astype(f32)
        for a in range(half):
            for t in range(8):
                for j in range(tiles):
                    strided = pl.ds(8 * j + t, per, stride=8 * tiles)
                    x = p_ref[a, f, strided, :] + sign * p_ref[a + half, f, strided, :]
                    h, l = split(x)
                    lanes = slice((a * tiles + j) * 128, (a * tiles + j + 1) * 128)
                    xh[t * per : (t + 1) * per, lanes] = h
                    xl[t * per : (t + 1) * per, lanes] = l
        y = dot_nt(table_ref[parity], xh[...])
        y = y[:both] + (y[both:] + dot_nt(table_ref[parity, :both], xl[...]))
        for u in range(4):
            first, second = swap_halves(y[:count, 128 * u : 128 * u + 128], y[count:, 128 * u : 128 * u + 128])
            ysc[pl.ds(2 * u, count, stride=8), :] = first
            ysc[pl.ds(2 * u + 1, count, stride=8), :] = second
        for s in range(2):
            out_ref[:, f, parity, s] = ysc[s * owners * 8 : (s + 1) * owners * 8, :].reshape(owners, 8, 128)
        return carry

    lax.fori_loop(0, 2 * fields, one, 0)


def fourier_stage(rows_all, table):
    parts, fields, shells, tiles, tb, _ = rows_all.shape
    half_phi = table.shape[2]
    modes2 = table.shape[1] // 2
    owners = modes2 // 4
    flat = rows_all.reshape(parts, fields, shells * tiles * tb, 128)
    whole = pl.BlockSpec(memory_space=pltpu.VMEM)
    return pl.pallas_call(
        fourier_kernel,
        in_specs=[whole, whole],
        out_specs=whole,
        out_shape=jax.ShapeDtypeStruct((owners, fields, 2, 2, 8, 128), f32),
        scratch_shapes=[
            pltpu.VMEM((shells * tb, half_phi), bf16),
            pltpu.VMEM((shells * tb, half_phi), bf16),
            pltpu.VMEM((modes2 * 4, 128), f32),
        ],
        compiler_params=params(32),
        name="fourier",
    )(flat, table)


def spectral_kernel(az, col, mode_ref, r_ref, leg, rad, fac_ref, out_ref, xh, xl, rhs, sol, radf):
    degrees = leg.shape[2]
    shells = rad.shape[0]
    tb = az * 8
    tiles = degrees // 128
    for q in range(4):
        parity = mode_ref[q] % 2
        for f in range(2):
            x = jnp.concatenate(
                [r_ref[a * col + c, f, parity, q % 2] for c in range(col) for a in range(az)], axis=0
            )
            h, l = split(x.T)
            xh[f * 128 : (f + 1) * 128, :] = h
            xl[f * 128 : (f + 1) * 128, :] = l
        coef = dot_nn(xh[...], leg[q]) + dot_nn(xl[...], leg[q])
        right = coef[:128] - fac_ref[...] * coef[128:]
        for i in range(2):
            for lt in range(tiles):
                rhs[lt, pl.ds(2 * q + i, shells, stride=8), :] = right[
                    i * shells : (i + 1) * shells, lt * 128 : lt * 128 + 128
                ]

    rb = 8

    def outer(block, carry):
        radf[...] = rad[pl.ds(block * rb, rb)].astype(f32)
        for lt in range(tiles):
            lanes = slice(lt * 128, lt * 128 + 128)
            acc = [jnp.zeros((8, 128), f32) for _ in range(rb)]
            for s in range(shells):
                v = rhs[lt, 8 * s : 8 * s + 8, :]
                for r in range(rb):
                    acc[r] = acc[r] + radf[r, s : s + 1, lanes] * v
            for r in range(rb):
                sol[lt, pl.ds(pl.multiple_of((block * rb + r) * 8, 8), 8), :] = acc[r]
        return carry

    lax.fori_loop(0, shells // rb, outer, 0)

    for q in range(4):
        parity = mode_ref[q] % 2
        gain = jnp.where(mode_ref[q] == 0, 1.0, 2.0).astype(f32)
        x = jnp.concatenate(
            [
                jnp.concatenate([sol[lt, pl.ds(2 * q + i, shells, stride=8), :] for lt in range(tiles)], axis=1)
                for i in range(2)
            ],
            axis=0,
        )
        h, l = split(x * gain)
        y = dot_nt(leg[q], h) + dot_nt(leg[q], l)
        for c in range(col):
            for a in range(az):
                out_ref[a * col + c, 2 * parity + q % 2] = y[c * tb + a * 8 : c * tb + a * 8 + 8]


def spectral_stage(received, legendre, radial, factor, own, az, col):
    owners = received.shape[0]
    modes, theta, degrees = legendre.shape
    shells = radial.shape[0]

    def kernel(*refs):
        spectral_kernel(az, col, *refs)

    whole = pl.BlockSpec(memory_space=pltpu.VMEM)
    return pl.pallas_call(
        kernel,
        in_specs=[pl.BlockSpec(memory_space=pltpu.SMEM), whole, whole, whole, whole],
        out_specs=whole,
        scratch_shapes=[
            pltpu.VMEM((256, theta), bf16),
            pltpu.VMEM((256, theta), bf16),
            pltpu.VMEM((degrees // 128, 8 * shells, 128), f32),
            pltpu.VMEM((degrees // 128, 8 * shells, 128), f32),
            pltpu.VMEM((8, shells, degrees), f32),
        ],
        out_shape=jax.ShapeDtypeStruct((owners, 4, 8, 128), f32),
        compiler_params=params(32),
        name="spectral",
    )(own, received, legendre, radial, factor)


def inverse_kernel(z_ref, table_ref, out_ref, gh, gl):
    owners = z_ref.shape[0] // 32
    rows = gh.shape[1]
    per = rows // 8
    both = table_ref.shape[1] // 2
    quarters = out_ref.shape[1]
    cols = table_ref.shape[2] // quarters
    tiles = cols // 128
    for par in range(2):
        halves = [[], []]
        for s in range(2):
            base = (par * 2 + s) * 8
            cos_u, sin_u = [], []
            for u in range(4):
                a = z_ref[pl.ds(base + 2 * u, owners, stride=32), :]
                b = z_ref[pl.ds(base + 2 * u + 1, owners, stride=32), :]
                first, second = swap_halves(a, b)
                cos_u.append(first)
                sin_u.append(second)
            halves[0].append(jnp.concatenate(cos_u, axis=1))
            halves[1].append(jnp.concatenate(sin_u, axis=1))
        for i in range(2):
            for s in range(2):
                h, l = split(halves[i][s].T)
                at = (2 * i + s) * owners
                gh[par, :, at : at + owners] = h
                gl[par, :, at : at + owners] = l

    for quarter in range(quarters):
        lanes = slice(quarter * cols, (quarter + 1) * cols)
        sums = []
        for par in range(2):
            th, tl = table_ref[par, :both, lanes], table_ref[par, both:, lanes]
            h, l = gh[par], gl[par]
            sums.append(dot_nn(h, th) + (dot_nn(h, tl) + dot_nn(l, th)))
        near = sums[0] + sums[1]
        far = sums[0] - sums[1]
        for t in range(8):
            for j in range(tiles):
                part = slice(j * 128, j * 128 + 128)
                strided = pl.ds(8 * j + t, per, stride=8 * tiles)
                out_ref[0, quarter, strided, :] = near[t * per : (t + 1) * per, part]
                out_ref[1, quarter, strided, :] = far[t * per : (t + 1) * per, part]


def inverse_stage(received, table, shells, az):
    owners, _, tb, _ = received.shape
    half_phi = table.shape[2]
    modes2 = table.shape[1] // 2
    flat = received.reshape(owners * 4 * tb, 128)
    cols = 2 * half_phi // az
    rows = shells * tb
    whole = pl.BlockSpec(memory_space=pltpu.VMEM)
    out = pl.pallas_call(
        inverse_kernel,
        in_specs=[whole, whole],
        out_specs=whole,
        out_shape=jax.ShapeDtypeStruct((2, az // 2, rows * cols // 128, 128), f32),
        scratch_shapes=[
            pltpu.VMEM((2, rows, modes2), bf16),
            pltpu.VMEM((2, rows, modes2), bf16),
        ],
        compiler_params=params(32),
        name="inverse",
    )(flat, table)
    return out.reshape(az, shells, cols // 128, tb, 128)


def gather_kernel(w_ref, out_ref):
    parts, shells = w_ref.shape[:2]
    for k in range(shells):
        for a in range(parts):
            for h in range(w_ref.shape[2]):
                out_ref[k, 8 * a : 8 * a + 8, 128 * h : 128 * h + 128] = w_ref[a, k, h]


def gather_stage(blocks):
    parts, shells, tiles, tb, _ = blocks.shape
    cols = tiles * 128
    kb = 16
    return pl.pallas_call(
        gather_kernel,
        grid=(shells // kb,),
        in_specs=[pl.BlockSpec((parts, kb, tiles, tb, 128), lambda i: (0, i, 0, 0, 0))],
        out_specs=pl.BlockSpec((kb, parts * tb, cols), lambda i: (i, 0, 0)),
        out_shape=jax.ShapeDtypeStruct((shells, parts * tb, cols), f32),
        compiler_params=params(16),
        name="gather",
    )(blocks)


def exchange(x, axes):
    return lax.all_to_all(x, axes, split_axis=0, concat_axis=0, tiled=True)


def body(phase_field, velocity, owned_modes, legendre, radial_inverse):
    shells, theta_local, phi_local = phase_field.shape
    az_count = lax.axis_size("az")
    col_count = lax.axis_size("col")
    az_here = lax.axis_index("az")
    col_here = lax.axis_index("col")
    phi_count = phi_local * az_count
    theta_count = theta_local * col_count
    degree_count = legendre.shape[2]
    radius = shell_radii(shells)

    weights = (colat_weights(theta_count) / phi_count).astype(np.float32)
    weights = jnp.asarray(np.repeat(weights[:, None], 128, axis=1))
    where = jnp.reshape(col_here, (1,)).astype(jnp.int32)

    west_out, east_out, north_out, south_out = edges_stage(phase_field)
    forward_az = [(i, (i + 1) % az_count) for i in range(az_count)]
    backward_az = [(target, source) for source, target in forward_az]
    forward_col = [(i, i + 1) for i in range(col_count - 1)]
    backward_col = [(target, source) for source, target in forward_col]
    west = lax.ppermute(east_out, "az", forward_az)
    east = lax.ppermute(west_out, "az", backward_az)
    north = lax.ppermute(south_out, "col", forward_col)
    south = lax.ppermute(north_out, "col", backward_col)

    here = az_here * col_count + col_here
    own = lax.dynamic_slice(owned_modes, (here, 0), (1, owned_modes.shape[1])).reshape(-1)
    degrees = np.arange(degree_count)
    factor = mobility_step * (degrees * (degrees + 1.0))[None, :] / (radius * radius)[:, None]
    factor = jnp.asarray(np.concatenate([factor, factor], axis=0).astype(np.float32))
    radial = jnp.transpose(radial_inverse, (1, 2, 0))
    table = wave_tables(owned_modes, phi_count)

    scale_phi = step_time * phi_count / (4.0 * math.pi)
    scale_theta = jnp.asarray((step_time * theta_count / (2.0 * math.pi) / radius).astype(np.float32))
    fields = stencil_stage(
        phase_field, velocity, weights, where, west, east, north, south, scale_phi, scale_theta
    )
    fields, table, own = lax.optimization_barrier((fields, table, own))
    received = exchange(fourier_stage(exchange(fields, "az"), table), everyone)
    synthesis = spectral_stage(
        received, legendre, radial, factor, own, az_count, col_count
    )
    grid_modes = exchange(synthesis, everyone)

    blocks = inverse_stage(grid_modes, table, shells, az_count)
    return gather_stage(exchange(blocks, "az"))


def solution(mesh):
    in_specs = (
        P(None, "col", "az"),
        P(None, None, "col", "az"),
        P(),
        P(("az", "col"), None, None),
        P(),
    )
    out_specs = P(None, "col", "az")
    return jax.shard_map(body, mesh=mesh, in_specs=in_specs, out_specs=out_specs, check_vma=False)
```

```python
import math

import jax
import jax.numpy as jnp
import numpy as np
from jax import lax
from jax.experimental import pallas as pl
from jax.experimental.pallas import tpu as pltpu
from jax.sharding import PartitionSpec as P

step_time = 0.002
mobility_step = 4e-06
f32 = jnp.float32
bf16 = jnp.bfloat16
everyone = ("az", "col")


def params(mib=48):
    return pltpu.CompilerParams(vmem_limit_bytes=mib * 1024 * 1024)


def colat_weights(count):
    theta = math.pi * (np.arange(count) + 0.5) / count
    waves = np.arange(1, count // 2 + 1)
    total = (np.cos(2.0 * waves[None, :] * theta[:, None]) / (4.0 * waves * waves - 1.0)).sum(1)
    return 2.0 / count * (1.0 - 2.0 * total)


def shell_radii(shells):
    return 0.75 + 0.25 * (np.arange(shells) + 0.5) / shells


def split(x):
    hi = x.astype(bf16)
    return hi, (x - hi.astype(f32)).astype(bf16)


def dot_nn(a, b):
    return lax.dot_general(a, b, (((1,), (0,)), ((), ())), preferred_element_type=f32)


def dot_nt(a, b):
    return lax.dot_general(a, b, (((1,), (1,)), ((), ())), preferred_element_type=f32)


def swap_halves(a, b):
    half = lax.broadcasted_iota(jnp.int32, a.shape, 1) < 64
    first = jnp.where(half, a, pltpu.roll(b, 64, 1))
    second = jnp.where(half, pltpu.roll(a, 64, 1), b)
    return first, second


def edges_kernel(where_ref, c_ref, az_even_ref, az_odd_ref, col_even_ref, col_odd_ref):
    shells, rows, cols = c_ref.shape
    lane = lax.broadcasted_iota(jnp.int32, (rows, 128), 1)
    low = jnp.zeros((rows, 128), f32)
    high = jnp.zeros((rows, 128), f32)
    for k in range(shells):
        low = jnp.where(lane == k, pltpu.roll(c_ref[k, :, :128], k, 1), low)
        high = jnp.where(lane == k, pltpu.roll(c_ref[k, :, cols - 128 :], k + 1, 1), high)
    odd = where_ref[0] % 2 == 1
    az_even_ref[...] = jnp.where(odd, low, high)
    az_odd_ref[...] = jnp.where(odd, high, low)
    low, high = c_ref[:, 0, :], c_ref[:, rows - 1, :]
    odd = where_ref[1] % 2 == 1
    col_even_ref[...] = jnp.where(odd, low, high)
    col_odd_ref[...] = jnp.where(odd, high, low)


def edges_stage(phase, where):
    shells, rows, cols = phase.shape
    whole = pl.BlockSpec(memory_space=pltpu.VMEM)
    return pl.pallas_call(
        edges_kernel,
        in_specs=[pl.BlockSpec(memory_space=pltpu.SMEM), whole],
        out_specs=[whole] * 4,
        out_shape=[
            jax.ShapeDtypeStruct((rows, 128), f32),
            jax.ShapeDtypeStruct((rows, 128), f32),
            jax.ShapeDtypeStruct((shells, cols), f32),
            jax.ShapeDtypeStruct((shells, cols), f32),
        ],
        compiler_params=params(32),
        name="edges",
    )(where, phase)


def stencil_kernel(scale_phi, where_ref, scale_ref, c_ref, v_ref, w_ref, az_even_ref, az_odd_ref, col_even_ref, col_odd_ref, out_ref):
    shells, rows, cols = c_ref.shape
    block = pl.program_id(0)
    weights = jnp.concatenate([w_ref[...]] * (cols // 128), axis=1)
    lane = lax.broadcasted_iota(jnp.int32, (rows, cols), 1)
    row = lax.broadcasted_iota(jnp.int32, (rows, cols), 0)
    turn = jnp.where(block == 0, 0, 128 - block * shells)
    odd = where_ref[0] % 2 == 1
    west_all = pltpu.roll(jnp.where(odd, az_even_ref[...], az_odd_ref[...]), turn, 1)
    east_all = pltpu.roll(jnp.where(odd, az_odd_ref[...], az_even_ref[...]), turn, 1)
    odd = where_ref[1] % 2 == 1
    north_all = jnp.where(odd, col_even_ref[...], col_odd_ref[...])
    south_all = jnp.where(odd, col_odd_ref[...], col_even_ref[...])
    for k in range(shells):
        x = c_ref[k]
        west_edge = jnp.broadcast_to(west_all[:, k : k + 1], (rows, cols))
        east_edge = jnp.broadcast_to(east_all[:, k : k + 1], (rows, cols))
        west = jnp.where(lane == 0, west_edge, pltpu.roll(x, 1, 1))
        east = jnp.where(lane == cols - 1, east_edge, pltpu.roll(x, cols - 1, 1))
        north = jnp.where(row == 0, north_all[k : k + 1, :], pltpu.roll(x, 1, 0))
        south = jnp.where(row == rows - 1, south_all[k : k + 1, :], pltpu.roll(x, rows - 1, 0))
        spin = v_ref[0, k].astype(f32)
        sweep = v_ref[1, k].astype(f32)
        scale_theta = scale_ref[block * shells + k]
        y = x - (spin * ((east - west) * scale_phi) + sweep * ((south - north) * scale_theta))
        y = y * weights
        z = (x * x * x - x) * weights
        for a in range(rows // 8):
            for h in range(cols // 128):
                out_ref[a, 0, k, h] = y[8 * a : 8 * a + 8, 128 * h : 128 * h + 128]
                out_ref[a, 1, k, h] = z[8 * a : 8 * a + 8, 128 * h : 128 * h + 128]


def stencil_stage(phase, velocity, weights, where, halos, scale_phi, scale_theta):
    shells, rows, cols = phase.shape
    kb = 16

    def kernel(*refs):
        stencil_kernel(scale_phi, *refs)

    return pl.pallas_call(
        kernel,
        grid_spec=pltpu.PrefetchScalarGridSpec(
            num_scalar_prefetch=1,
            grid=(shells // kb,),
            in_specs=[
                pl.BlockSpec(memory_space=pltpu.SMEM),
                pl.BlockSpec((kb, rows, cols), lambda i, s: (i, 0, 0)),
                pl.BlockSpec((2, kb, rows, cols), lambda i, s: (0, i, 0, 0)),
                pl.BlockSpec((rows, 128), lambda i, s: (s[1], 0)),
                pl.BlockSpec((rows, 128), lambda i, s: (0, 0)),
                pl.BlockSpec((rows, 128), lambda i, s: (0, 0)),
                pl.BlockSpec((kb, cols), lambda i, s: (i, 0)),
                pl.BlockSpec((kb, cols), lambda i, s: (i, 0)),
            ],
            out_specs=pl.BlockSpec((rows // 8, 2, kb, cols // 128, 8, 128), lambda i, s: (0, 0, i, 0, 0, 0)),
        ),
        out_shape=jax.ShapeDtypeStruct((rows // 8, 2, shells, cols // 128, 8, 128), f32),
        compiler_params=params(48),
        name="stencil",
    )(where, scale_theta, phase, velocity, weights, *halos)


def table_kernel(fine_ref, coarse_ref, out_ref):
    modes = fine_ref.shape[2]
    tiles = out_ref.shape[2] // 128
    fc, fs = fine_ref[0, 0], fine_ref[1, 0]
    coarse = [coarse_ref[i, 0].T for i in range(2)]
    for u in range(tiles):
        cc = jnp.broadcast_to(coarse[0][:, u : u + 1], (modes, 128))
        cs = jnp.broadcast_to(coarse[1][:, u : u + 1], (modes, 128))
        for i, value in enumerate((fc * cc - fs * cs, fs * cc + fc * cs)):
            h, l = split(value)
            lanes = slice(128 * u, 128 * u + 128)
            out_ref[0, i * modes : (i + 1) * modes, lanes] = h
            out_ref[0, (2 + i) * modes : (3 + i) * modes, lanes] = l


def wave_tables(owned_modes, phi_count):
    first_half = owned_modes[:, :2].T.reshape(-1)
    top = owned_modes.shape[0] * owned_modes.shape[1] - 1
    even = jnp.where(first_half % 2 == 0, first_half, top - first_half)
    modes = jnp.stack([even, top - even])
    count = modes.shape[1]
    half_phi = phi_count // 2

    quarter = jnp.arange(2, dtype=jnp.int32) * (phi_count // 4)

    def waves(turns):
        turns = (turns + quarter[:, None, None, None]) % phi_count
        return jnp.cos(turns.astype(f32) * (2.0 * math.pi / phi_count))

    lanes = jnp.arange(128, dtype=jnp.int32)
    tiles = jnp.arange(half_phi // 128, dtype=jnp.int32) * 128
    fine = waves(modes[None, :, :, None] * lanes)
    coarse = waves(modes[None, :, None, :] * tiles[:, None])

    return pl.pallas_call(
        table_kernel,
        grid=(2,),
        in_specs=[
            pl.BlockSpec((2, 1, count, 128), lambda i: (0, i, 0, 0)),
            pl.BlockSpec((2, 1, half_phi // 128, count), lambda i: (0, i, 0, 0)),
        ],
        out_specs=pl.BlockSpec((1, 4 * count, half_phi), lambda i: (i, 0, 0)),
        out_shape=jax.ShapeDtypeStruct((2, 4 * count, half_phi), bf16),
        compiler_params=params(40),
        name="table",
    )(fine, coarse)


def fourier_kernel(p_ref, table_ref, out_ref, xh, xl):
    parts, fields = p_ref.shape[:2]
    half = parts // 2
    per = xh.shape[1] // 8
    tiles = xh.shape[2] // half // 128
    both = table_ref.shape[1] // 2
    count = both // 2
    owners = count // 2
    stride = out_ref.shape[0] // owners

    def one(f, carry):
        for a in range(half):
            for t in range(8):
                for j in range(tiles):
                    strided = pl.ds(8 * j + t, per, stride=8 * tiles)
                    near, far = p_ref[a, f, strided, :], p_ref[a + half, f, strided, :]
                    lanes = slice((a * tiles + j) * 128, (a * tiles + j + 1) * 128)
                    for parity, x in enumerate((near + far, near - far)):
                        h, l = split(x)
                        xh[parity, t * per : (t + 1) * per, lanes] = h
                        xl[parity, t * per : (t + 1) * per, lanes] = l
        for parity in range(2):
            y = dot_nt(table_ref[parity], xh[parity])
            y = y[:both] + (y[both:] + dot_nt(table_ref[parity, :both], xl[parity]))
            for u in range(4):
                pair = swap_halves(y[:count, 128 * u : 128 * u + 128], y[count:, 128 * u : 128 * u + 128])
                for s in range(2):
                    for v in range(2):
                        at = f * (stride // fields) + (2 * parity + s) * 8 + 2 * u + v
                        out_ref[pl.ds(at, owners, stride=stride), :] = pair[v][s * owners : (s + 1) * owners]
        return carry

    lax.fori_loop(0, fields, one, 0)


def fourier_stage(rows_all, table):
    parts, fields, shells, tiles, tb, _ = rows_all.shape
    half_phi = table.shape[2]
    owners = table.shape[1] // 8
    flat = rows_all.reshape(parts, fields, shells * tiles * tb, 128)
    whole = pl.BlockSpec(memory_space=pltpu.VMEM)
    out = pl.pallas_call(
        fourier_kernel,
        in_specs=[whole, whole],
        out_specs=whole,
        out_shape=jax.ShapeDtypeStruct((owners * fields * 4 * 8, 128), f32),
        scratch_shapes=[
            pltpu.VMEM((2, shells * tb, half_phi), bf16),
            pltpu.VMEM((2, shells * tb, half_phi), bf16),
        ],
        compiler_params=params(32),
        name="fourier",
    )(flat, table)
    return out.reshape(owners, fields, 2, 2, 8, 128)


def spectral_kernel(az, col, mode_ref, r_ref, leg, rad, fac_ref, out_ref, xh, xl, rhs, sol, radf):
    degrees = leg.shape[2]
    shells = rad.shape[0]
    tb = az * 8
    tiles = degrees // 128
    for q in range(4):
        parity = mode_ref[q] % 2
        for f in range(2):
            x = jnp.concatenate(
                [r_ref[a * col + c, f, parity, q % 2] for c in range(col) for a in range(az)], axis=0
            )
            h, l = split(x.T)
            xh[f * 128 : (f + 1) * 128, :] = h
            xl[f * 128 : (f + 1) * 128, :] = l
        coef = dot_nn(xh[...], leg[q]) + dot_nn(xl[...], leg[q])
        right = coef[:128] - fac_ref[...] * coef[128:]
        for i in range(2):
            for lt in range(tiles):
                rhs[lt, pl.ds(2 * q + i, shells, stride=8), :] = right[
                    i * shells : (i + 1) * shells, lt * 128 : lt * 128 + 128
                ]

    rb = 8

    def outer(block, carry):
        radf[...] = rad[pl.ds(block * rb, rb)].astype(f32)
        for lt in range(tiles):
            lanes = slice(lt * 128, lt * 128 + 128)
            acc = [jnp.zeros((8, 128), f32) for _ in range(rb)]
            for s in range(shells):
                v = rhs[lt, 8 * s : 8 * s + 8, :]
                for r in range(rb):
                    acc[r] = acc[r] + radf[r, s : s + 1, lanes] * v
            for r in range(rb):
                sol[lt, pl.ds(pl.multiple_of((block * rb + r) * 8, 8), 8), :] = acc[r]
        return carry

    lax.fori_loop(0, shells // rb, outer, 0)

    for q in range(4):
        parity = mode_ref[q] % 2
        gain = jnp.where(mode_ref[q] == 0, 1.0, 2.0).astype(f32)
        x = jnp.concatenate(
            [
                jnp.concatenate([sol[lt, pl.ds(2 * q + i, shells, stride=8), :] for lt in range(tiles)], axis=1)
                for i in range(2)
            ],
            axis=0,
        )
        h, l = split(x * gain)
        y = dot_nt(leg[q], h) + dot_nt(leg[q], l)
        for c in range(col):
            for a in range(az):
                out_ref[a * col + c, 2 * parity + q % 2] = y[c * tb + a * 8 : c * tb + a * 8 + 8]


def spectral_stage(received, legendre, radial, factor, own, az, col):
    owners = received.shape[0]
    modes, theta, degrees = legendre.shape
    shells = radial.shape[0]

    def kernel(*refs):
        spectral_kernel(az, col, *refs)

    whole = pl.BlockSpec(memory_space=pltpu.VMEM)
    return pl.pallas_call(
        kernel,
        in_specs=[pl.BlockSpec(memory_space=pltpu.SMEM), whole, whole, whole, whole],
        out_specs=whole,
        scratch_shapes=[
            pltpu.VMEM((256, theta), bf16),
            pltpu.VMEM((256, theta), bf16),
            pltpu.VMEM((degrees // 128, 8 * shells, 128), f32),
            pltpu.VMEM((degrees // 128, 8 * shells, 128), f32),
            pltpu.VMEM((8, shells, degrees), f32),
        ],
        out_shape=jax.ShapeDtypeStruct((owners, 4, 8, 128), f32),
        compiler_params=params(32),
        name="spectral",
    )(own, received, legendre, radial, factor)


def inverse_kernel(z_ref, table_ref, out_ref, gh, gl):
    owners = z_ref.shape[0] // 32
    rows = gh.shape[1]
    per = rows // 8
    both = table_ref.shape[1] // 2
    quarters = out_ref.shape[1]
    cols = table_ref.shape[2] // quarters
    tiles = cols // 128
    for par in range(2):
        halves = [[], []]
        for s in range(2):
            base = (par * 2 + s) * 8
            cos_u, sin_u = [], []
            for u in range(4):
                a = z_ref[pl.ds(base + 2 * u, owners, stride=32), :]
                b = z_ref[pl.ds(base + 2 * u + 1, owners, stride=32), :]
                first, second = swap_halves(a, b)
                cos_u.append(first)
                sin_u.append(second)
            halves[0].append(jnp.concatenate(cos_u, axis=1))
            halves[1].append(jnp.concatenate(sin_u, axis=1))
        for i in range(2):
            for s in range(2):
                h, l = split(halves[i][s].T)
                at = (2 * i + s) * owners
                gh[par, :, at : at + owners] = h
                gl[par, :, at : at + owners] = l

    for quarter in range(quarters):
        lanes = slice(quarter * cols, (quarter + 1) * cols)
        sums = []
        for par in range(2):
            th, tl = table_ref[par, :both, lanes], table_ref[par, both:, lanes]
            h, l = gh[par], gl[par]
            sums.append(dot_nn(h, th) + (dot_nn(h, tl) + dot_nn(l, th)))
        near = sums[0] + sums[1]
        far = sums[0] - sums[1]
        for t in range(8):
            for j in range(tiles):
                part = slice(j * 128, j * 128 + 128)
                strided = pl.ds(8 * j + t, per, stride=8 * tiles)
                out_ref[0, quarter, strided, :] = near[t * per : (t + 1) * per, part]
                out_ref[1, quarter, strided, :] = far[t * per : (t + 1) * per, part]


def inverse_stage(received, table, shells, az):
    owners, _, tb, _ = received.shape
    half_phi = table.shape[2]
    modes2 = table.shape[1] // 2
    flat = received.reshape(owners * 4 * tb, 128)
    cols = 2 * half_phi // az
    rows = shells * tb
    whole = pl.BlockSpec(memory_space=pltpu.VMEM)
    out = pl.pallas_call(
        inverse_kernel,
        in_specs=[whole, whole],
        out_specs=whole,
        out_shape=jax.ShapeDtypeStruct((2, az // 2, rows * cols // 128, 128), f32),
        scratch_shapes=[
            pltpu.VMEM((2, rows, modes2), bf16),
            pltpu.VMEM((2, rows, modes2), bf16),
        ],
        compiler_params=params(32),
        name="inverse",
    )(flat, table)
    return out.reshape(az, shells, cols // 128, tb, 128)


def gather_kernel(w_ref, out_ref):
    parts, shells = w_ref.shape[:2]
    for k in range(shells):
        for a in range(parts):
            for h in range(w_ref.shape[2]):
                out_ref[k, 8 * a : 8 * a + 8, 128 * h : 128 * h + 128] = w_ref[a, k, h]


def gather_stage(blocks):
    parts, shells, tiles, tb, _ = blocks.shape
    cols = tiles * 128
    kb = 16
    return pl.pallas_call(
        gather_kernel,
        grid=(shells // kb,),
        in_specs=[pl.BlockSpec((parts, kb, tiles, tb, 128), lambda i: (0, i, 0, 0, 0))],
        out_specs=pl.BlockSpec((kb, parts * tb, cols), lambda i: (i, 0, 0)),
        out_shape=jax.ShapeDtypeStruct((shells, parts * tb, cols), f32),
        compiler_params=params(16),
        name="gather",
    )(blocks)


def exchange(x, axes):
    return lax.all_to_all(x, axes, split_axis=0, concat_axis=0, tiled=True)


def body(phase_field, velocity, owned_modes, legendre, radial_inverse):
    shells, theta_local, phi_local = phase_field.shape
    az_count = lax.axis_size("az")
    col_count = lax.axis_size("col")
    az_here = lax.axis_index("az")
    col_here = lax.axis_index("col")
    phi_count = phi_local * az_count
    theta_count = theta_local * col_count
    degree_count = legendre.shape[2]
    radius = shell_radii(shells)

    weights = (colat_weights(theta_count) / phi_count).astype(np.float32)
    weights = jnp.asarray(np.repeat(weights[:, None], 128, axis=1))
    where = jnp.stack([az_here, col_here]).astype(jnp.int32)

    az_even, az_odd, col_even, col_odd = edges_stage(phase_field, where)
    even_az = [(i, i ^ 1) for i in range(az_count)]
    odd_az = [(i, (i + 1 if i % 2 else i - 1) % az_count) for i in range(az_count)]
    even_col = [(i, i ^ 1) for i in range(col_count)]
    odd_col = [(i, i + 1 if i % 2 else i - 1) for i in range(1, col_count - 1)]
    halos = (
        lax.ppermute(az_even, "az", even_az),
        lax.ppermute(az_odd, "az", odd_az),
        lax.ppermute(col_even, "col", even_col),
        lax.ppermute(col_odd, "col", odd_col),
    )

    here = az_here * col_count + col_here
    own = lax.dynamic_slice(owned_modes, (here, 0), (1, owned_modes.shape[1])).reshape(-1)
    degrees = np.arange(degree_count)
    factor = mobility_step * (degrees * (degrees + 1.0))[None, :] / (radius * radius)[:, None]
    factor = jnp.asarray(np.concatenate([factor, factor], axis=0).astype(np.float32))
    radial = jnp.transpose(radial_inverse, (1, 2, 0))
    table = wave_tables(owned_modes, phi_count)

    scale_phi = step_time * phi_count / (4.0 * math.pi)
    scale_theta = jnp.asarray((step_time * theta_count / (2.0 * math.pi) / radius).astype(np.float32))
    fields = stencil_stage(
        phase_field, velocity, weights, where, halos, scale_phi, scale_theta
    )
    fields, table, own = lax.optimization_barrier((fields, table, own))
    received = exchange(fourier_stage(exchange(fields, "az"), table), everyone)
    synthesis = spectral_stage(
        received, legendre, radial, factor, own, az_count, col_count
    )
    grid_modes = exchange(synthesis, everyone)

    blocks = inverse_stage(grid_modes, table, shells, az_count)
    return gather_stage(exchange(blocks, "az"))


def solution(mesh):
    in_specs = (
        P(None, "col", "az"),
        P(None, None, "col", "az"),
        P(),
        P(("az", "col"), None, None),
        P(),
    )
    out_specs = P(None, "col", "az")
    return jax.shard_map(body, mesh=mesh, in_specs=in_specs, out_specs=out_specs, check_vma=False)
```

```python
import math

import jax
import jax.numpy as jnp
import numpy as np
from jax import lax
from jax.experimental import pallas as pl
from jax.experimental.pallas import tpu as pltpu
from jax.sharding import PartitionSpec as P

step_time = 0.002
mobility_step = 4e-06
f32 = jnp.float32
bf16 = jnp.bfloat16
everyone = ("az", "col")


def params(mib=48):
    return pltpu.CompilerParams(vmem_limit_bytes=mib * 1024 * 1024)


def colat_weights(count):
    theta = math.pi * (np.arange(count) + 0.5) / count
    waves = np.arange(1, count // 2 + 1)
    total = (np.cos(2.0 * waves[None, :] * theta[:, None]) / (4.0 * waves * waves - 1.0)).sum(1)
    return 2.0 / count * (1.0 - 2.0 * total)


def shell_radii(shells):
    return 0.75 + 0.25 * (np.arange(shells) + 0.5) / shells


def split(x):
    hi = x.astype(bf16)
    return hi, (x - hi.astype(f32)).astype(bf16)


def dot_nn(a, b):
    return lax.dot_general(a, b, (((1,), (0,)), ((), ())), preferred_element_type=f32)


def dot_nt(a, b):
    return lax.dot_general(a, b, (((1,), (1,)), ((), ())), preferred_element_type=f32)


def swap_halves(a, b):
    half = lax.broadcasted_iota(jnp.int32, a.shape, 1) < 64
    first = jnp.where(half, a, pltpu.roll(b, 64, 1))
    second = jnp.where(half, pltpu.roll(a, 64, 1), b)
    return first, second


def edges_kernel(where_ref, c_hbm, az_even_ref, az_odd_ref, col_even_ref, col_odd_ref, c_ref, sems):
    shells, rows, cols = c_ref.shape
    chunks = sems.shape[0]
    size = shells // chunks
    copies = [
        pltpu.make_async_copy(c_hbm.at[pl.ds(n * size, size)], c_ref.at[pl.ds(n * size, size)], sems.at[n])
        for n in range(chunks)
    ]
    for copy in copies:
        copy.start()
    lane = lax.broadcasted_iota(jnp.int32, (rows, 128), 1)
    low = jnp.zeros((rows, 128), f32)
    high = jnp.zeros((rows, 128), f32)
    for k in range(shells):
        if k % size == 0:
            copies[k // size].wait()
        low = jnp.where(lane == k, pltpu.roll(c_ref[k, :, :128], k, 1), low)
        high = jnp.where(lane == k, pltpu.roll(c_ref[k, :, cols - 128 :], k + 1, 1), high)
    odd = where_ref[0] % 2 == 1
    az_even_ref[...] = jnp.where(odd, low, high)
    az_odd_ref[...] = jnp.where(odd, high, low)
    low, high = c_ref[:, 0, :], c_ref[:, rows - 1, :]
    odd = where_ref[1] % 2 == 1
    col_even_ref[...] = jnp.where(odd, low, high)
    col_odd_ref[...] = jnp.where(odd, high, low)


def edges_stage(phase, where):
    shells, rows, cols = phase.shape
    whole = pl.BlockSpec(memory_space=pltpu.VMEM)
    return pl.pallas_call(
        edges_kernel,
        in_specs=[pl.BlockSpec(memory_space=pltpu.SMEM), pl.BlockSpec(memory_space=pl.ANY)],
        out_specs=[whole] * 4,
        out_shape=[
            jax.ShapeDtypeStruct((rows, 128), f32),
            jax.ShapeDtypeStruct((rows, 128), f32),
            jax.ShapeDtypeStruct((shells, cols), f32),
            jax.ShapeDtypeStruct((shells, cols), f32),
        ],
        scratch_shapes=[pltpu.VMEM(phase.shape, f32), pltpu.SemaphoreType.DMA((8,))],
        compiler_params=params(61),
        name="edges",
    )(where, phase)


def stencil_kernel(
    scale_phi, where_ref, scale_ref, c_ref, v_ref, w_ref, az_even_ref, az_odd_ref, col_even_ref, col_odd_ref, out_ref
):
    shells, rows, cols = c_ref.shape
    block = pl.program_id(0)
    tiles, strips = cols // 128, rows // 8
    lane = lax.broadcasted_iota(jnp.int32, (8, 128), 1)
    row = lax.broadcasted_iota(jnp.int32, (8, 128), 0)
    not_first, not_last = lane > 0, lane < 127
    not_top, not_bottom = row > 0, row < 7
    az_odd = where_ref[0] % 2 == 1
    col_odd = where_ref[1] % 2 == 1
    turn = jnp.where(block == 0, 0, 128 - block * shells)
    west_all = pltpu.roll(jnp.where(az_odd, az_even_ref[...], az_odd_ref[...]), turn, 1)
    east_all = pltpu.roll(jnp.where(az_odd, az_odd_ref[...], az_even_ref[...]), turn, 1)
    north_all = jnp.where(col_odd, col_even_ref[...], col_odd_ref[...])
    south_all = jnp.where(col_odd, col_odd_ref[...], col_even_ref[...])
    for k in range(shells):
        scale_theta = scale_ref[block * shells + k]
        above, below = [], []
        for h in range(tiles):
            lanes = slice(128 * h, 128 * h + 128)
            above.append(jnp.broadcast_to(north_all[k : k + 1, lanes], (8, 128)))
            below.append(jnp.broadcast_to(south_all[k : k + 1, lanes], (8, 128)))
        for r in range(strips):
            these = slice(8 * r, 8 * r + 8)
            x = [c_ref[k, these, 128 * h : 128 * h + 128] for h in range(tiles)]
            to_east = [pltpu.roll(t, 1, 1) for t in x]
            to_west = [pltpu.roll(t, 127, 1) for t in x]
            west_edge = jnp.broadcast_to(west_all[these, k : k + 1], (8, 128))
            east_edge = jnp.broadcast_to(east_all[these, k : k + 1], (8, 128))
            weights = w_ref[these, :]
            for h in range(tiles):
                lanes = slice(128 * h, 128 * h + 128)
                west = jnp.where(not_first, to_east[h], to_east[h - 1] if h else west_edge)
                east = jnp.where(not_last, to_west[h], to_west[h + 1] if h + 1 < tiles else east_edge)
                down = pltpu.roll(x[h], 1, 0)
                north = jnp.where(not_top, down, above[h])
                above[h] = down
                up = pltpu.roll(x[h], 7, 0)
                if r + 1 < strips:
                    following = pltpu.roll(c_ref[k, 8 * r + 8 : 8 * r + 16, lanes], 7, 0)
                else:
                    following = below[h]
                south = jnp.where(not_bottom, up, following)
                spin = v_ref[0, k, these, lanes].astype(f32)
                sweep = v_ref[1, k, these, lanes].astype(f32)
                y = x[h] - (spin * ((east - west) * scale_phi) + sweep * ((south - north) * scale_theta))
                out_ref[r, 0, k, h] = y * weights
                out_ref[r, 1, k, h] = (x[h] * x[h] * x[h] - x[h]) * weights


def stencil_stage(phase, velocity, weights, where, halos, scale_phi, scale_theta):
    shells, rows, cols = phase.shape
    kb = 16

    def kernel(*refs):
        stencil_kernel(scale_phi, *refs)

    return pl.pallas_call(
        kernel,
        grid_spec=pltpu.PrefetchScalarGridSpec(
            num_scalar_prefetch=1,
            grid=(shells // kb,),
            in_specs=[
                pl.BlockSpec(memory_space=pltpu.SMEM),
                pl.BlockSpec((kb, rows, cols), lambda i, s: (i, 0, 0)),
                pl.BlockSpec((2, kb, rows, cols), lambda i, s: (0, i, 0, 0)),
                pl.BlockSpec((rows, 128), lambda i, s: (s[1], 0)),
                pl.BlockSpec((rows, 128), lambda i, s: (0, 0)),
                pl.BlockSpec((rows, 128), lambda i, s: (0, 0)),
                pl.BlockSpec((kb, cols), lambda i, s: (i, 0)),
                pl.BlockSpec((kb, cols), lambda i, s: (i, 0)),
            ],
            out_specs=pl.BlockSpec((rows // 8, 2, kb, cols // 128, 8, 128), lambda i, s: (0, 0, i, 0, 0, 0)),
        ),
        out_shape=jax.ShapeDtypeStruct((rows // 8, 2, shells, cols // 128, 8, 128), f32),
        compiler_params=params(48),
        name="stencil",
    )(where, scale_theta, phase, velocity, weights, *halos)


def cos_and_minus_sin(turns, full):
    shift = (full // 4).bit_length() - 1
    quadrant = (turns + full // 8) >> shift
    rest = turns - (quadrant << shift)
    x = rest.astype(f32) * (2.0 * math.pi / full)
    q = quadrant & 3
    x2 = x * x
    cos = 1.0 + x2 * (-1.0 / 2 + x2 * (1.0 / 24 + x2 * (-1.0 / 720 + x2 * (1.0 / 40320))))
    sin = x + x * x2 * (-1.0 / 6 + x2 * (1.0 / 120 + x2 * (-1.0 / 5040 + x2 * (1.0 / 362880))))
    swap = (q & 1) == 1
    c = jnp.where(swap, sin, cos)
    s = jnp.where(swap, cos, sin)
    return jnp.where((q == 1) | (q == 2), -c, c), jnp.where(q >= 2, s, -s)


def table_kernel(mode_ref, out_ref):
    parities, modes, _ = mode_ref.shape
    half_phi = out_ref.shape[2]
    tiles = half_phi // 128
    lane = lax.broadcasted_iota(jnp.int32, (modes, 128), 1)
    for parity in range(parities):
        orders = mode_ref[parity]
        fc, fs = cos_and_minus_sin(orders * lane, 2 * half_phi)
        coarse_c, coarse_s = cos_and_minus_sin(orders * lane * 128, 2 * half_phi)
        for u in range(tiles):
            cc = jnp.broadcast_to(coarse_c[:, u : u + 1], (modes, 128))
            cs = jnp.broadcast_to(coarse_s[:, u : u + 1], (modes, 128))
            for i, value in enumerate((fc * cc - fs * cs, fs * cc + fc * cs)):
                h, l = split(value)
                lanes = slice(128 * u, 128 * u + 128)
                out_ref[parity, i * modes : (i + 1) * modes, lanes] = h
                out_ref[parity, (2 + i) * modes : (3 + i) * modes, lanes] = l


def wave_tables(owned_modes, phi_count):
    first_half = owned_modes[:, :2].T.reshape(-1)
    top = owned_modes.shape[0] * owned_modes.shape[1] - 1
    even = jnp.where(first_half % 2 == 0, first_half, top - first_half)
    modes = jnp.stack([even, top - even])
    count = modes.shape[1]
    whole = pl.BlockSpec(memory_space=pltpu.VMEM)
    return pl.pallas_call(
        table_kernel,
        in_specs=[whole],
        out_specs=whole,
        out_shape=jax.ShapeDtypeStruct((2, 4 * count, phi_count // 2), bf16),
        compiler_params=params(24),
        name="table",
    )(jnp.broadcast_to(modes[:, :, None], (2, count, 128)))


def fourier_kernel(p_ref, table_ref, out_ref, xh, xl):
    parts, fields = p_ref.shape[:2]
    half = parts // 2
    per = xh.shape[1] // 8
    tiles = xh.shape[2] // half // 128
    both = table_ref.shape[1] // 2
    count = both // 2
    owners = count // 2
    stride = out_ref.shape[0] // owners

    def one(f, carry):
        for a in range(half):
            for t in range(8):
                for j in range(tiles):
                    strided = pl.ds(8 * j + t, per, stride=8 * tiles)
                    near, far = p_ref[a, f, strided, :], p_ref[a + half, f, strided, :]
                    lanes = slice((a * tiles + j) * 128, (a * tiles + j + 1) * 128)
                    for parity, x in enumerate((near + far, near - far)):
                        h, l = split(x)
                        xh[parity, t * per : (t + 1) * per, lanes] = h
                        xl[parity, t * per : (t + 1) * per, lanes] = l
        for parity in range(2):
            y = dot_nt(table_ref[parity], xh[parity])
            y = y[:both] + (y[both:] + dot_nt(table_ref[parity, :both], xl[parity]))
            for u in range(4):
                pair = swap_halves(y[:count, 128 * u : 128 * u + 128], y[count:, 128 * u : 128 * u + 128])
                for s in range(2):
                    for v in range(2):
                        at = f * (stride // fields) + (2 * parity + s) * 8 + 2 * u + v
                        out_ref[pl.ds(at, owners, stride=stride), :] = pair[v][s * owners : (s + 1) * owners]
        return carry

    lax.fori_loop(0, fields, one, 0)


def fourier_stage(rows_all, table):
    parts, fields, shells, tiles, tb, _ = rows_all.shape
    half_phi = table.shape[2]
    owners = table.shape[1] // 8
    flat = rows_all.reshape(parts, fields, shells * tiles * tb, 128)
    whole = pl.BlockSpec(memory_space=pltpu.VMEM)
    out = pl.pallas_call(
        fourier_kernel,
        in_specs=[whole, whole],
        out_specs=whole,
        out_shape=jax.ShapeDtypeStruct((owners * fields * 4 * 8, 128), f32),
        scratch_shapes=[
            pltpu.VMEM((2, shells * tb, half_phi), bf16),
            pltpu.VMEM((2, shells * tb, half_phi), bf16),
        ],
        compiler_params=params(32),
        name="fourier",
    )(flat, table)
    return out.reshape(owners, fields, 2, 2, 8, 128)


def spectral_kernel(az, col, mode_ref, r_ref, leg, rad, fac_ref, out_ref, xh, xl, rhs, sol, radf):
    degrees = leg.shape[2]
    shells = rad.shape[0]
    tb = az * 8
    tiles = degrees // 128
    for q in range(4):
        parity = mode_ref[q] % 2
        for f in range(2):
            x = jnp.concatenate(
                [r_ref[a * col + c, f, parity, q % 2] for c in range(col) for a in range(az)], axis=0
            )
            h, l = split(x.T)
            xh[f * 128 : (f + 1) * 128, :] = h
            xl[f * 128 : (f + 1) * 128, :] = l
        coef = dot_nn(xh[...], leg[q]) + dot_nn(xl[...], leg[q])
        right = coef[:128] - fac_ref[...] * coef[128:]
        for i in range(2):
            for lt in range(tiles):
                rhs[lt, pl.ds(2 * q + i, shells, stride=8), :] = right[
                    i * shells : (i + 1) * shells, lt * 128 : lt * 128 + 128
                ]

    rb = 8

    def outer(block, carry):
        radf[...] = rad[pl.ds(block * rb, rb)].astype(f32)
        for lt in range(tiles):
            lanes = slice(lt * 128, lt * 128 + 128)
            acc = [jnp.zeros((8, 128), f32) for _ in range(rb)]
            for s in range(shells):
                v = rhs[lt, 8 * s : 8 * s + 8, :]
                for r in range(rb):
                    acc[r] = acc[r] + radf[r, s : s + 1, lanes] * v
            for r in range(rb):
                sol[lt, pl.ds(pl.multiple_of((block * rb + r) * 8, 8), 8), :] = acc[r]
        return carry

    lax.fori_loop(0, shells // rb, outer, 0)

    for q in range(4):
        parity = mode_ref[q] % 2
        gain = jnp.where(mode_ref[q] == 0, 1.0, 2.0).astype(f32)
        x = jnp.concatenate(
            [
                jnp.concatenate([sol[lt, pl.ds(2 * q + i, shells, stride=8), :] for lt in range(tiles)], axis=1)
                for i in range(2)
            ],
            axis=0,
        )
        h, l = split(x * gain)
        y = dot_nt(leg[q], h) + dot_nt(leg[q], l)
        for c in range(col):
            for a in range(az):
                out_ref[a * col + c, 2 * parity + q % 2] = y[c * tb + a * 8 : c * tb + a * 8 + 8]


def spectral_stage(received, legendre, radial, factor, own, az, col):
    owners = received.shape[0]
    modes, theta, degrees = legendre.shape
    shells = radial.shape[0]

    def kernel(*refs):
        spectral_kernel(az, col, *refs)

    whole = pl.BlockSpec(memory_space=pltpu.VMEM)
    return pl.pallas_call(
        kernel,
        in_specs=[pl.BlockSpec(memory_space=pltpu.SMEM), whole, whole, whole, whole],
        out_specs=whole,
        scratch_shapes=[
            pltpu.VMEM((256, theta), bf16),
            pltpu.VMEM((256, theta), bf16),
            pltpu.VMEM((degrees // 128, 8 * shells, 128), f32),
            pltpu.VMEM((degrees // 128, 8 * shells, 128), f32),
            pltpu.VMEM((8, shells, degrees), f32),
        ],
        out_shape=jax.ShapeDtypeStruct((owners, 4, 8, 128), f32),
        compiler_params=params(32),
        name="spectral",
    )(own, received, legendre, radial, factor)


def inverse_kernel(z_ref, table_ref, out_ref, gh, gl):
    owners = z_ref.shape[0] // 32
    rows = gh.shape[1]
    per = rows // 8
    both = table_ref.shape[1] // 2
    quarters = out_ref.shape[1]
    cols = table_ref.shape[2] // quarters
    tiles = cols // 128
    for par in range(2):
        halves = [[], []]
        for s in range(2):
            base = (par * 2 + s) * 8
            cos_u, sin_u = [], []
            for u in range(4):
                a = z_ref[pl.ds(base + 2 * u, owners, stride=32), :]
                b = z_ref[pl.ds(base + 2 * u + 1, owners, stride=32), :]
                first, second = swap_halves(a, b)
                cos_u.append(first)
                sin_u.append(second)
            halves[0].append(jnp.concatenate(cos_u, axis=1))
            halves[1].append(jnp.concatenate(sin_u, axis=1))
        for i in range(2):
            for s in range(2):
                h, l = split(halves[i][s].T)
                at = (2 * i + s) * owners
                gh[par, :, at : at + owners] = h
                gl[par, :, at : at + owners] = l

    for quarter in range(quarters):
        lanes = slice(quarter * cols, (quarter + 1) * cols)
        sums = []
        for par in range(2):
            th, tl = table_ref[par, :both, lanes], table_ref[par, both:, lanes]
            h, l = gh[par], gl[par]
            sums.append(dot_nn(h, th) + (dot_nn(h, tl) + dot_nn(l, th)))
        near = sums[0] + sums[1]
        far = sums[0] - sums[1]
        for t in range(8):
            for j in range(tiles):
                part = slice(j * 128, j * 128 + 128)
                strided = pl.ds(8 * j + t, per, stride=8 * tiles)
                out_ref[0, quarter, strided, :] = near[t * per : (t + 1) * per, part]
                out_ref[1, quarter, strided, :] = far[t * per : (t + 1) * per, part]


def inverse_stage(received, table, shells, az):
    owners, _, tb, _ = received.shape
    half_phi = table.shape[2]
    modes2 = table.shape[1] // 2
    flat = received.reshape(owners * 4 * tb, 128)
    cols = 2 * half_phi // az
    rows = shells * tb
    whole = pl.BlockSpec(memory_space=pltpu.VMEM)
    out = pl.pallas_call(
        inverse_kernel,
        in_specs=[whole, whole],
        out_specs=whole,
        out_shape=jax.ShapeDtypeStruct((2, az // 2, rows * cols // 128, 128), f32),
        scratch_shapes=[
            pltpu.VMEM((2, rows, modes2), bf16),
            pltpu.VMEM((2, rows, modes2), bf16),
        ],
        compiler_params=params(32),
        name="inverse",
    )(flat, table)
    return out.reshape(az, shells, cols // 128, tb, 128)


def gather_kernel(w_ref, out_ref, sem):
    parts, shells, tiles = w_ref.shape[:3]
    copies = []
    for a in range(parts):
        for h in range(tiles):
            copies.append(
                pltpu.make_async_copy(
                    w_ref.at[a, :, h],
                    out_ref.at[:, pl.ds(8 * a, 8), pl.ds(128 * h, 128)],
                    sem.at[a * tiles + h],
                )
            )
    for copy in copies:
        copy.start()
    for copy in copies:
        copy.wait()


def gather_stage(blocks):
    parts, shells, tiles, tb, _ = blocks.shape
    return pl.pallas_call(
        gather_kernel,
        in_specs=[pl.BlockSpec(memory_space=pltpu.VMEM)],
        out_specs=pl.BlockSpec(memory_space=pl.ANY),
        out_shape=jax.ShapeDtypeStruct((shells, parts * tb, tiles * 128), f32),
        scratch_shapes=[pltpu.SemaphoreType.DMA((parts * tiles,))],
        compiler_params=params(16),
        name="gather",
    )(blocks)


def exchange(x, axes):
    return lax.all_to_all(x, axes, split_axis=0, concat_axis=0, tiled=True)


def body(phase_field, velocity, owned_modes, legendre, radial_inverse):
    shells, theta_local, phi_local = phase_field.shape
    az_count = lax.axis_size("az")
    col_count = lax.axis_size("col")
    az_here = lax.axis_index("az")
    col_here = lax.axis_index("col")
    phi_count = phi_local * az_count
    theta_count = theta_local * col_count
    degree_count = legendre.shape[2]
    radius = shell_radii(shells)

    weights = (colat_weights(theta_count) / phi_count).astype(np.float32)
    weights = jnp.asarray(np.repeat(weights[:, None], 128, axis=1))
    where = jnp.stack([az_here, col_here]).astype(jnp.int32)

    az_even, az_odd, col_even, col_odd = edges_stage(phase_field, where)
    even_az = [(i, i ^ 1) for i in range(az_count)]
    odd_az = [(i, (i + 1 if i % 2 else i - 1) % az_count) for i in range(az_count)]
    even_col = [(i, i ^ 1) for i in range(col_count)]
    odd_col = [(i, i + 1 if i % 2 else i - 1) for i in range(1, col_count - 1)]
    halos = (
        lax.ppermute(az_even, "az", even_az),
        lax.ppermute(az_odd, "az", odd_az),
        lax.ppermute(col_even, "col", even_col),
        lax.ppermute(col_odd, "col", odd_col),
    )

    here = az_here * col_count + col_here
    own = lax.dynamic_slice(owned_modes, (here, 0), (1, owned_modes.shape[1])).reshape(-1)
    degrees = np.arange(degree_count)
    factor = mobility_step * (degrees * (degrees + 1.0))[None, :] / (radius * radius)[:, None]
    factor = jnp.asarray(np.concatenate([factor, factor], axis=0).astype(np.float32))
    radial = jnp.transpose(radial_inverse, (1, 2, 0))
    table = wave_tables(owned_modes, phi_count)

    scale_phi = step_time * phi_count / (4.0 * math.pi)
    scale_theta = jnp.asarray((step_time * theta_count / (2.0 * math.pi) / radius).astype(np.float32))
    fields = stencil_stage(
        phase_field, velocity, weights, where, halos, scale_phi, scale_theta
    )
    fields, table, own = lax.optimization_barrier((fields, table, own))
    received = exchange(fourier_stage(exchange(fields, "az"), table), everyone)
    synthesis = spectral_stage(
        received, legendre, radial, factor, own, az_count, col_count
    )
    grid_modes = exchange(synthesis, everyone)

    blocks = inverse_stage(grid_modes, table, shells, az_count)
    return gather_stage(exchange(blocks, "az"))


def solution(mesh):
    in_specs = (
        P(None, "col", "az"),
        P(None, None, "col", "az"),
        P(),
        P(("az", "col"), None, None),
        P(),
    )
    out_specs = P(None, "col", "az")
    return jax.shard_map(body, mesh=mesh, in_specs=in_specs, out_specs=out_specs, check_vma=False)
```

```python
import math

import jax
import jax.numpy as jnp
import numpy as np
from jax import lax
from jax.experimental import pallas as pl
from jax.experimental.pallas import tpu as pltpu
from jax.sharding import PartitionSpec as P

step_time = 0.002
mobility_step = 4e-06
f32 = jnp.float32
bf16 = jnp.bfloat16
everyone = ("az", "col")


def params(mib=48):
    return pltpu.CompilerParams(vmem_limit_bytes=mib * 1024 * 1024)


def colat_weights(count):
    theta = math.pi * (np.arange(count) + 0.5) / count
    waves = np.arange(1, count // 2 + 1)
    total = (np.cos(2.0 * waves[None, :] * theta[:, None]) / (4.0 * waves * waves - 1.0)).sum(1)
    return 2.0 / count * (1.0 - 2.0 * total)


def shell_radii(shells):
    return 0.75 + 0.25 * (np.arange(shells) + 0.5) / shells


def split(x):
    hi = x.astype(bf16)
    return hi, (x - hi.astype(f32)).astype(bf16)


def dot_nn(a, b):
    return lax.dot_general(a, b, (((1,), (0,)), ((), ())), preferred_element_type=f32)


def dot_nt(a, b):
    return lax.dot_general(a, b, (((1,), (1,)), ((), ())), preferred_element_type=f32)


def swap_halves(a, b):
    half = lax.broadcasted_iota(jnp.int32, a.shape, 1) < 64
    first = jnp.where(half, a, pltpu.roll(b, 64, 1))
    second = jnp.where(half, pltpu.roll(a, 64, 1), b)
    return first, second


def edges_kernel(c_hbm, az_even_ref, az_odd_ref, col_even_ref, col_odd_ref, c_ref, sems):
    shells, rows, cols = c_ref.shape
    chunks = sems.shape[0]
    size = shells // chunks
    copies = [
        pltpu.make_async_copy(c_hbm.at[pl.ds(n * size, size)], c_ref.at[pl.ds(n * size, size)], sems.at[n])
        for n in range(chunks)
    ]
    for copy in copies:
        copy.start()
    lane = lax.broadcasted_iota(jnp.int32, (rows, 128), 1)
    low = jnp.zeros((rows, 128), f32)
    high = jnp.zeros((rows, 128), f32)
    for k in range(shells):
        if k % size == 0:
            copies[k // size].wait()
        low = jnp.where(lane == k, pltpu.roll(c_ref[k, :, :128], k, 1), low)
        high = jnp.where(lane == k, pltpu.roll(c_ref[k, :, cols - 128 :], k + 1, 1), high)
    odd = lax.axis_index("az") % 2 == 1
    az_even_ref[...] = jnp.where(odd, low, high)
    az_odd_ref[...] = jnp.where(odd, high, low)
    low, high = c_ref[:, 0, :], c_ref[:, rows - 1, :]
    odd = lax.axis_index("col") % 2 == 1
    col_even_ref[...] = jnp.where(odd, low, high)
    col_odd_ref[...] = jnp.where(odd, high, low)


def edges_stage(phase):
    shells, rows, cols = phase.shape
    whole = pl.BlockSpec(memory_space=pltpu.VMEM)
    return pl.pallas_call(
        edges_kernel,
        in_specs=[pl.BlockSpec(memory_space=pl.ANY)],
        out_specs=[whole] * 4,
        out_shape=[
            jax.ShapeDtypeStruct((rows, 128), f32),
            jax.ShapeDtypeStruct((rows, 128), f32),
            jax.ShapeDtypeStruct((shells, cols), f32),
            jax.ShapeDtypeStruct((shells, cols), f32),
        ],
        scratch_shapes=[pltpu.VMEM(phase.shape, f32), pltpu.SemaphoreType.DMA((8,))],
        compiler_params=params(52),
        name="edges",
    )(phase)


def stencil_kernel(
    scale_phi, scale_ref, c_ref, v_ref, w_ref, az_even_ref, az_odd_ref, col_even_ref, col_odd_ref, out_ref
):
    shells, rows, cols = c_ref.shape
    block = pl.program_id(0)
    tiles, strips = cols // 128, rows // 8
    lane = lax.broadcasted_iota(jnp.int32, (8, 128), 1)
    row = lax.broadcasted_iota(jnp.int32, (8, 128), 0)
    not_first, not_last = lane > 0, lane < 127
    not_top, not_bottom = row > 0, row < 7
    az_odd = lax.axis_index("az") % 2 == 1
    col_here = lax.axis_index("col")
    col_odd = col_here % 2 == 1
    turn = jnp.where(block == 0, 0, 128 - block * shells)
    west_all = pltpu.roll(jnp.where(az_odd, az_even_ref[...], az_odd_ref[...]), turn, 1)
    east_all = pltpu.roll(jnp.where(az_odd, az_odd_ref[...], az_even_ref[...]), turn, 1)
    north_all = jnp.where(col_odd, col_even_ref[...], col_odd_ref[...])
    south_all = jnp.where(col_odd, col_odd_ref[...], col_even_ref[...])
    for k in range(shells):
        scale_theta = scale_ref[block * shells + k]
        above, below = [], []
        for h in range(tiles):
            lanes = slice(128 * h, 128 * h + 128)
            above.append(jnp.broadcast_to(north_all[k : k + 1, lanes], (8, 128)))
            below.append(jnp.broadcast_to(south_all[k : k + 1, lanes], (8, 128)))
        for r in range(strips):
            these = slice(8 * r, 8 * r + 8)
            x = [c_ref[k, these, 128 * h : 128 * h + 128] for h in range(tiles)]
            to_east = [pltpu.roll(t, 1, 1) for t in x]
            to_west = [pltpu.roll(t, 127, 1) for t in x]
            west_edge = jnp.broadcast_to(west_all[these, k : k + 1], (8, 128))
            east_edge = jnp.broadcast_to(east_all[these, k : k + 1], (8, 128))
            weights = w_ref[pl.ds(pl.multiple_of(col_here * rows + 8 * r, 8), 8), :]
            for h in range(tiles):
                lanes = slice(128 * h, 128 * h + 128)
                west = jnp.where(not_first, to_east[h], to_east[h - 1] if h else west_edge)
                east = jnp.where(not_last, to_west[h], to_west[h + 1] if h + 1 < tiles else east_edge)
                down = pltpu.roll(x[h], 1, 0)
                north = jnp.where(not_top, down, above[h])
                above[h] = down
                up = pltpu.roll(x[h], 7, 0)
                if r + 1 < strips:
                    following = pltpu.roll(c_ref[k, 8 * r + 8 : 8 * r + 16, lanes], 7, 0)
                else:
                    following = below[h]
                south = jnp.where(not_bottom, up, following)
                spin = v_ref[0, k, these, lanes].astype(f32)
                sweep = v_ref[1, k, these, lanes].astype(f32)
                y = x[h] - (spin * ((east - west) * scale_phi) + sweep * ((south - north) * scale_theta))
                out_ref[r, 0, k, h] = y * weights
                out_ref[r, 1, k, h] = (x[h] * x[h] * x[h] - x[h]) * weights


def stencil_stage(phase, velocity, weights, halos, scale_phi, scale_theta):
    shells, rows, cols = phase.shape
    kb = 16

    def kernel(*refs):
        stencil_kernel(scale_phi, *refs)

    return pl.pallas_call(
        kernel,
        grid=(shells // kb,),
        in_specs=[
            pl.BlockSpec(memory_space=pltpu.SMEM),
            pl.BlockSpec((kb, rows, cols), lambda i: (i, 0, 0)),
            pl.BlockSpec((2, kb, rows, cols), lambda i: (0, i, 0, 0)),
            pl.BlockSpec(weights.shape, lambda i: (0, 0)),
            pl.BlockSpec((rows, 128), lambda i: (0, 0)),
            pl.BlockSpec((rows, 128), lambda i: (0, 0)),
            pl.BlockSpec((kb, cols), lambda i: (i, 0)),
            pl.BlockSpec((kb, cols), lambda i: (i, 0)),
        ],
        out_specs=pl.BlockSpec((rows // 8, 2, kb, cols // 128, 8, 128), lambda i: (0, 0, i, 0, 0, 0)),
        out_shape=jax.ShapeDtypeStruct((rows // 8, 2, shells, cols // 128, 8, 128), f32),
        compiler_params=params(48),
        name="stencil",
    )(scale_theta, phase, velocity, weights, *halos)


def cos_and_minus_sin(turns, full):
    shift = (full // 4).bit_length() - 1
    quadrant = (turns + full // 8) >> shift
    rest = turns - (quadrant << shift)
    x = rest.astype(f32) * (2.0 * math.pi / full)
    q = quadrant & 3
    x2 = x * x
    cos = 1.0 + x2 * (-1.0 / 2 + x2 * (1.0 / 24 + x2 * (-1.0 / 720 + x2 * (1.0 / 40320))))
    sin = x + x * x2 * (-1.0 / 6 + x2 * (1.0 / 120 + x2 * (-1.0 / 5040 + x2 * (1.0 / 362880))))
    swap = (q & 1) == 1
    c = jnp.where(swap, sin, cos)
    s = jnp.where(swap, cos, sin)
    return jnp.where((q == 1) | (q == 2), -c, c), jnp.where(q >= 2, s, -s)


def table_kernel(mode_ref, out_ref):
    parities, modes, _ = mode_ref.shape
    half_phi = out_ref.shape[2]
    tiles = half_phi // 128
    lane = lax.broadcasted_iota(jnp.int32, (modes, 128), 1)
    for parity in range(parities):
        orders = mode_ref[parity]
        fc, fs = cos_and_minus_sin(orders * lane, 2 * half_phi)
        coarse_c, coarse_s = cos_and_minus_sin(orders * lane * 128, 2 * half_phi)
        for u in range(tiles):
            cc = jnp.broadcast_to(coarse_c[:, u : u + 1], (modes, 128))
            cs = jnp.broadcast_to(coarse_s[:, u : u + 1], (modes, 128))
            for i, value in enumerate((fc * cc - fs * cs, fs * cc + fc * cs)):
                h, l = split(value)
                lanes = slice(128 * u, 128 * u + 128)
                out_ref[parity, i * modes : (i + 1) * modes, lanes] = h
                out_ref[parity, (2 + i) * modes : (3 + i) * modes, lanes] = l


def wave_tables(owned_modes, phi_count):
    first_half = owned_modes[:, :2].T.reshape(-1)
    top = owned_modes.shape[0] * owned_modes.shape[1] - 1
    even = jnp.where(first_half % 2 == 0, first_half, top - first_half)
    modes = jnp.stack([even, top - even])
    count = modes.shape[1]
    whole = pl.BlockSpec(memory_space=pltpu.VMEM)
    return pl.pallas_call(
        table_kernel,
        in_specs=[whole],
        out_specs=whole,
        out_shape=jax.ShapeDtypeStruct((2, 4 * count, phi_count // 2), bf16),
        compiler_params=params(24),
        name="table",
    )(jnp.broadcast_to(modes[:, :, None], (2, count, 128)))


def fourier_kernel(p_ref, table_ref, out_ref, xh, xl):
    parts, fields = p_ref.shape[:2]
    half = parts // 2
    per = xh.shape[1] // 8
    tiles = xh.shape[2] // half // 128
    both = table_ref.shape[1] // 2
    count = both // 2
    owners = count // 2
    stride = out_ref.shape[0] // owners

    def one(f, carry):
        for a in range(half):
            for t in range(8):
                for j in range(tiles):
                    strided = pl.ds(8 * j + t, per, stride=8 * tiles)
                    near, far = p_ref[a, f, strided, :], p_ref[a + half, f, strided, :]
                    lanes = slice((a * tiles + j) * 128, (a * tiles + j + 1) * 128)
                    for parity, x in enumerate((near + far, near - far)):
                        h, l = split(x)
                        xh[parity, t * per : (t + 1) * per, lanes] = h
                        xl[parity, t * per : (t + 1) * per, lanes] = l
        for parity in range(2):
            y = dot_nt(table_ref[parity], xh[parity])
            y = y[:both] + (y[both:] + dot_nt(table_ref[parity, :both], xl[parity]))
            for u in range(4):
                pair = swap_halves(y[:count, 128 * u : 128 * u + 128], y[count:, 128 * u : 128 * u + 128])
                for s in range(2):
                    for v in range(2):
                        at = f * (stride // fields) + (2 * parity + s) * 8 + 2 * u + v
                        out_ref[pl.ds(at, owners, stride=stride), :] = pair[v][s * owners : (s + 1) * owners]
        return carry

    lax.fori_loop(0, fields, one, 0)


def fourier_stage(rows_all, table):
    parts, fields, shells, tiles, tb, _ = rows_all.shape
    half_phi = table.shape[2]
    owners = table.shape[1] // 8
    flat = rows_all.reshape(parts, fields, shells * tiles * tb, 128)
    whole = pl.BlockSpec(memory_space=pltpu.VMEM)
    out = pl.pallas_call(
        fourier_kernel,
        in_specs=[whole, whole],
        out_specs=whole,
        out_shape=jax.ShapeDtypeStruct((owners * fields * 4 * 8, 128), f32),
        scratch_shapes=[
            pltpu.VMEM((2, shells * tb, half_phi), bf16),
            pltpu.VMEM((2, shells * tb, half_phi), bf16),
        ],
        compiler_params=params(32),
        name="fourier",
    )(flat, table)
    return out.reshape(owners, fields, 2, 2, 8, 128)


def spectral_kernel(az, col, mode_ref, r_ref, leg, rad, fac_ref, out_ref, xh, xl, rhs, sol, radf):
    degrees = leg.shape[2]
    shells = rad.shape[0]
    tb = az * 8
    tiles = degrees // 128
    half = degrees // 2
    for q in range(4):
        parity = mode_ref[q] % 2
        for f in range(2):
            x = jnp.concatenate(
                [r_ref[a * col + c, f, parity, q % 2] for c in range(col) for a in range(az)], axis=0
            )
            h, l = split(x.T)
            xh[q, f * 128 : (f + 1) * 128, :] = h
            xl[q, f * 128 : (f + 1) * 128, :] = l

    def right_side(q, lanes):
        coef = dot_nn(xh[q], leg[q, :, lanes]) + dot_nn(xl[q], leg[q, :, lanes])
        return coef[:128] - fac_ref[:, lanes] * coef[128:]

    def put(q, first, right):
        for i in range(2):
            for n in range(tiles // 2):
                rhs[first + n, pl.ds(2 * q + i, shells, stride=8), :] = right[
                    i * shells : (i + 1) * shells, n * 128 : n * 128 + 128
                ]

    for q in range(4):
        put(q, tiles // 2, right_side(q, slice(half, degrees)))
    low = [jnp.where(mode_ref[s] < half, s, s + 2) for s in range(2)]
    high = [jnp.where(mode_ref[s] < half, s + 2, s) for s in range(2)]
    for s in range(2):
        put(low[s], 0, right_side(low[s], slice(0, half)))
        put(high[s], 0, jnp.zeros((2 * shells, half), f32))

    rb = 8

    def outer(block, carry):
        radf[...] = rad[pl.ds(block * rb, rb)].astype(f32)
        for lt in range(tiles):
            lanes = slice(lt * 128, lt * 128 + 128)
            acc = [jnp.zeros((8, 128), f32) for _ in range(rb)]
            for s in range(shells):
                v = rhs[lt, 8 * s : 8 * s + 8, :]
                for r in range(rb):
                    acc[r] = acc[r] + radf[r, s : s + 1, lanes] * v
            for r in range(rb):
                sol[lt, pl.ds(pl.multiple_of((block * rb + r) * 8, 8), 8), :] = acc[r]
        return carry

    lax.fori_loop(0, shells // rb, outer, 0)

    for s in range(2):
        for q, first in ((low[s], 0), (high[s], tiles // 2)):
            gain = jnp.where(mode_ref[q] == 0, 1.0, 2.0).astype(f32)
            x = jnp.concatenate(
                [
                    jnp.concatenate(
                        [sol[lt, pl.ds(2 * q + i, shells, stride=8), :] for lt in range(first, tiles)], axis=1
                    )
                    for i in range(2)
                ],
                axis=0,
            )
            h, l = split(x * gain)
            matrix = leg[q, :, first * 128 :]
            y = dot_nt(matrix, h) + dot_nt(matrix, l)
            slot = 2 * (mode_ref[q] % 2) + s
            for c in range(col):
                for a in range(az):
                    out_ref[a * col + c, slot] = y[c * tb + a * 8 : c * tb + a * 8 + 8]


def spectral_stage(received, legendre, radial, factor, own, az, col):
    owners = received.shape[0]
    modes, theta, degrees = legendre.shape
    shells = radial.shape[0]

    def kernel(*refs):
        spectral_kernel(az, col, *refs)

    whole = pl.BlockSpec(memory_space=pltpu.VMEM)
    return pl.pallas_call(
        kernel,
        in_specs=[pl.BlockSpec(memory_space=pltpu.SMEM), whole, whole, whole, whole],
        out_specs=whole,
        scratch_shapes=[
            pltpu.VMEM((4, 256, theta), bf16),
            pltpu.VMEM((4, 256, theta), bf16),
            pltpu.VMEM((degrees // 128, 8 * shells, 128), f32),
            pltpu.VMEM((degrees // 128, 8 * shells, 128), f32),
            pltpu.VMEM((8, shells, degrees), f32),
        ],
        out_shape=jax.ShapeDtypeStruct((owners, 4, 8, 128), f32),
        compiler_params=params(32),
        name="spectral",
    )(own, received, legendre, radial, factor)


def inverse_kernel(z_ref, table_ref, out_ref, gh, gl):
    owners = z_ref.shape[0] // 32
    rows = gh.shape[1]
    per = rows // 8
    both = table_ref.shape[1] // 2
    quarters = out_ref.shape[1]
    cols = table_ref.shape[2] // quarters
    tiles = cols // 128
    for par in range(2):
        halves = [[], []]
        for s in range(2):
            base = (par * 2 + s) * 8
            cos_u, sin_u = [], []
            for u in range(4):
                a = z_ref[pl.ds(base + 2 * u, owners, stride=32), :]
                b = z_ref[pl.ds(base + 2 * u + 1, owners, stride=32), :]
                first, second = swap_halves(a, b)
                cos_u.append(first)
                sin_u.append(second)
            halves[0].append(jnp.concatenate(cos_u, axis=1))
            halves[1].append(jnp.concatenate(sin_u, axis=1))
        for i in range(2):
            for s in range(2):
                h, l = split(halves[i][s].T)
                at = (2 * i + s) * owners
                gh[par, :, at : at + owners] = h
                gh[par, :, both + at : both + at + owners] = h
                gl[par, :, at : at + owners] = l

    for quarter in range(quarters):
        lanes = slice(quarter * cols, (quarter + 1) * cols)
        sums = []
        for par in range(2):
            sums.append(dot_nn(gh[par], table_ref[par, :, lanes]) + dot_nn(gl[par], table_ref[par, :both, lanes]))
        near = sums[0] + sums[1]
        far = sums[0] - sums[1]
        for t in range(8):
            for j in range(tiles):
                part = slice(j * 128, j * 128 + 128)
                strided = pl.ds(8 * j + t, per, stride=8 * tiles)
                out_ref[0, quarter, strided, :] = near[t * per : (t + 1) * per, part]
                out_ref[1, quarter, strided, :] = far[t * per : (t + 1) * per, part]


def inverse_stage(received, table, shells, az):
    owners, _, tb, _ = received.shape
    half_phi = table.shape[2]
    modes2 = table.shape[1] // 2
    flat = received.reshape(owners * 4 * tb, 128)
    cols = 2 * half_phi // az
    rows = shells * tb
    whole = pl.BlockSpec(memory_space=pltpu.VMEM)
    out = pl.pallas_call(
        inverse_kernel,
        in_specs=[whole, whole],
        out_specs=whole,
        out_shape=jax.ShapeDtypeStruct((2, az // 2, rows * cols // 128, 128), f32),
        scratch_shapes=[
            pltpu.VMEM((2, rows, 2 * modes2), bf16),
            pltpu.VMEM((2, rows, modes2), bf16),
        ],
        compiler_params=params(32),
        name="inverse",
    )(flat, table)
    return out.reshape(az, shells, cols // 128, tb, 128)


def gather_kernel(w_ref, out_ref, sem):
    parts, shells, tiles = w_ref.shape[:3]
    copies = []
    for a in range(parts):
        for h in range(tiles):
            copies.append(
                pltpu.make_async_copy(
                    w_ref.at[a, :, h],
                    out_ref.at[:, pl.ds(8 * a, 8), pl.ds(128 * h, 128)],
                    sem.at[a * tiles + h],
                )
            )
    for copy in copies:
        copy.start()
    for copy in copies:
        copy.wait()


def gather_stage(blocks):
    parts, shells, tiles, tb, _ = blocks.shape
    return pl.pallas_call(
        gather_kernel,
        in_specs=[pl.BlockSpec(memory_space=pltpu.VMEM)],
        out_specs=pl.BlockSpec(memory_space=pl.ANY),
        out_shape=jax.ShapeDtypeStruct((shells, parts * tb, tiles * 128), f32),
        scratch_shapes=[pltpu.SemaphoreType.DMA((parts * tiles,))],
        compiler_params=params(16),
        name="gather",
    )(blocks)


def exchange(x, axes):
    return lax.all_to_all(x, axes, split_axis=0, concat_axis=0, tiled=True)


def body(phase_field, velocity, owned_modes, legendre, radial_inverse):
    shells, theta_local, phi_local = phase_field.shape
    az_count = lax.axis_size("az")
    col_count = lax.axis_size("col")
    az_here = lax.axis_index("az")
    col_here = lax.axis_index("col")
    phi_count = phi_local * az_count
    theta_count = theta_local * col_count
    degree_count = legendre.shape[2]
    radius = shell_radii(shells)

    weights = (colat_weights(theta_count) / phi_count).astype(np.float32)
    weights = jnp.asarray(np.repeat(weights[:, None], 128, axis=1))

    az_even, az_odd, col_even, col_odd = edges_stage(phase_field)
    even_az = [(i, i ^ 1) for i in range(az_count)]
    odd_az = [(i, (i + 1 if i % 2 else i - 1) % az_count) for i in range(az_count)]
    even_col = [(i, i ^ 1) for i in range(col_count)]
    odd_col = [(i, i + 1 if i % 2 else i - 1) for i in range(1, col_count - 1)]
    halos = (
        lax.ppermute(az_even, "az", even_az),
        lax.ppermute(az_odd, "az", odd_az),
        lax.ppermute(col_even, "col", even_col),
        lax.ppermute(col_odd, "col", odd_col),
    )

    here = az_here * col_count + col_here
    own = lax.dynamic_slice(owned_modes, (here, 0), (1, owned_modes.shape[1])).reshape(-1)
    degrees = np.arange(degree_count)
    factor = mobility_step * (degrees * (degrees + 1.0))[None, :] / (radius * radius)[:, None]
    factor = jnp.asarray(np.concatenate([factor, factor], axis=0).astype(np.float32))
    radial = jnp.transpose(radial_inverse, (1, 2, 0))
    table = wave_tables(owned_modes, phi_count)

    scale_phi = step_time * phi_count / (4.0 * math.pi)
    scale_theta = jnp.asarray((step_time * theta_count / (2.0 * math.pi) / radius).astype(np.float32))
    fields = stencil_stage(
        phase_field, velocity, weights, halos, scale_phi, scale_theta
    )
    fields, table, own = lax.optimization_barrier((fields, table, own))
    received = exchange(fourier_stage(exchange(fields, "az"), table), everyone)
    synthesis = spectral_stage(
        received, legendre, radial, factor, own, az_count, col_count
    )
    grid_modes = exchange(synthesis, everyone)

    blocks = inverse_stage(grid_modes, table, shells, az_count)
    return gather_stage(exchange(blocks, "az"))


def solution(mesh):
    in_specs = (
        P(None, "col", "az"),
        P(None, None, "col", "az"),
        P(),
        P(("az", "col"), None, None),
        P(),
    )
    out_specs = P(None, "col", "az")
    return jax.shard_map(body, mesh=mesh, in_specs=in_specs, out_specs=out_specs, check_vma=False)
```

```python
import math

import jax
import jax.numpy as jnp
import numpy as np
from jax import lax
from jax.experimental import pallas as pl
from jax.experimental.pallas import tpu as pltpu
from jax.sharding import PartitionSpec as P

step_time = 0.002
mobility_step = 4e-06
f32 = jnp.float32
bf16 = jnp.bfloat16
everyone = ("az", "col")


def params(mib=48):
    return pltpu.CompilerParams(vmem_limit_bytes=mib * 1024 * 1024)


def colat_weights(count):
    theta = math.pi * (np.arange(count) + 0.5) / count
    waves = np.arange(1, count // 2 + 1)
    total = (np.cos(2.0 * waves[None, :] * theta[:, None]) / (4.0 * waves * waves - 1.0)).sum(1)
    return 2.0 / count * (1.0 - 2.0 * total)


def shell_radii(shells):
    return 0.75 + 0.25 * (np.arange(shells) + 0.5) / shells


def split(x):
    hi = x.astype(bf16)
    return hi, (x - hi.astype(f32)).astype(bf16)


def dot_nn(a, b):
    return lax.dot_general(a, b, (((1,), (0,)), ((), ())), preferred_element_type=f32)


def dot_nt(a, b):
    return lax.dot_general(a, b, (((1,), (1,)), ((), ())), preferred_element_type=f32)


def swap_halves(a, b):
    half = lax.broadcasted_iota(jnp.int32, a.shape, 1) < 64
    first = jnp.where(half, a, pltpu.roll(b, 64, 1))
    second = jnp.where(half, pltpu.roll(a, 64, 1), b)
    return first, second


def row_edges_kernel(c_hbm, even_ref, odd_ref, top_ref, bottom_ref, sems):
    rows = c_hbm.shape[1]
    copies = [
        pltpu.make_async_copy(c_hbm.at[:, pl.ds(0, 8)], top_ref, sems.at[0]),
        pltpu.make_async_copy(c_hbm.at[:, pl.ds(rows - 8, 8)], bottom_ref, sems.at[1]),
    ]
    for copy in copies:
        copy.start()
    for copy in copies:
        copy.wait()
    low, high = top_ref[:, 0, :], bottom_ref[:, 7, :]
    odd = lax.axis_index("col") % 2 == 1
    even_ref[...] = jnp.where(odd, low, high)
    odd_ref[...] = jnp.where(odd, high, low)


def row_edges_stage(phase):
    shells, _, cols = phase.shape
    whole = pl.BlockSpec(memory_space=pltpu.VMEM)
    return pl.pallas_call(
        row_edges_kernel,
        in_specs=[pl.BlockSpec(memory_space=pl.ANY)],
        out_specs=[whole] * 2,
        out_shape=[jax.ShapeDtypeStruct((shells, cols), f32)] * 2,
        scratch_shapes=[
            pltpu.VMEM((shells, 8, cols), f32),
            pltpu.VMEM((shells, 8, cols), f32),
            pltpu.SemaphoreType.DMA((2,)),
        ],
        compiler_params=params(52),
        name="row_edges",
    )(phase)


def column_edges_kernel(c_hbm, even_ref, odd_ref, c_ref, sems):
    shells, rows, cols = c_ref.shape
    chunks = sems.shape[0]
    size = shells // chunks
    copies = [
        pltpu.make_async_copy(c_hbm.at[pl.ds(n * size, size)], c_ref.at[pl.ds(n * size, size)], sems.at[n])
        for n in range(chunks)
    ]
    for copy in copies:
        copy.start()
    lane = lax.broadcasted_iota(jnp.int32, (rows, 128), 1)
    low = jnp.zeros((rows, 128), f32)
    high = jnp.zeros((rows, 128), f32)
    for k in range(shells):
        if k % size == 0:
            copies[k // size].wait()
        low = jnp.where(lane == k, pltpu.roll(c_ref[k, :, :128], k, 1), low)
        high = jnp.where(lane == k, pltpu.roll(c_ref[k, :, cols - 128 :], k + 1, 1), high)
    odd = lax.axis_index("az") % 2 == 1
    even_ref[...] = jnp.where(odd, low, high)
    odd_ref[...] = jnp.where(odd, high, low)


def column_edges_stage(phase):
    _, rows, _ = phase.shape
    whole = pl.BlockSpec(memory_space=pltpu.VMEM)
    return pl.pallas_call(
        column_edges_kernel,
        in_specs=[pl.BlockSpec(memory_space=pl.ANY)],
        out_specs=[whole] * 2,
        out_shape=[jax.ShapeDtypeStruct((rows, 128), f32)] * 2,
        scratch_shapes=[pltpu.VMEM(phase.shape, f32), pltpu.SemaphoreType.DMA((8,))],
        compiler_params=params(52),
        name="column_edges",
    )(phase)


def stencil_kernel(
    scale_phi, scale_ref, c_ref, v_ref, w_ref, az_even_ref, az_odd_ref, col_even_ref, col_odd_ref, out_ref
):
    shells, rows, cols = c_ref.shape
    block = pl.program_id(0)
    tiles, strips = cols // 128, rows // 8
    lane = lax.broadcasted_iota(jnp.int32, (8, 128), 1)
    row = lax.broadcasted_iota(jnp.int32, (8, 128), 0)
    not_first, not_last = lane > 0, lane < 127
    not_top, not_bottom = row > 0, row < 7
    az_odd = lax.axis_index("az") % 2 == 1
    col_here = lax.axis_index("col")
    col_odd = col_here % 2 == 1
    turn = jnp.where(block == 0, 0, 128 - block * shells)
    west_all = pltpu.roll(jnp.where(az_odd, az_even_ref[...], az_odd_ref[...]), turn, 1)
    east_all = pltpu.roll(jnp.where(az_odd, az_odd_ref[...], az_even_ref[...]), turn, 1)
    north_all = jnp.where(col_odd, col_even_ref[...], col_odd_ref[...])
    south_all = jnp.where(col_odd, col_odd_ref[...], col_even_ref[...])
    for k in range(shells):
        scale_theta = scale_ref[block * shells + k]
        above, below = [], []
        for h in range(tiles):
            lanes = slice(128 * h, 128 * h + 128)
            above.append(jnp.broadcast_to(north_all[k : k + 1, lanes], (8, 128)))
            below.append(jnp.broadcast_to(south_all[k : k + 1, lanes], (8, 128)))
        for r in range(strips):
            these = slice(8 * r, 8 * r + 8)
            x = [c_ref[k, these, 128 * h : 128 * h + 128] for h in range(tiles)]
            to_east = [pltpu.roll(t, 1, 1) for t in x]
            to_west = [pltpu.roll(t, 127, 1) for t in x]
            west_edge = jnp.broadcast_to(west_all[these, k : k + 1], (8, 128))
            east_edge = jnp.broadcast_to(east_all[these, k : k + 1], (8, 128))
            weights = w_ref[pl.ds(pl.multiple_of(col_here * rows + 8 * r, 8), 8), :]
            for h in range(tiles):
                lanes = slice(128 * h, 128 * h + 128)
                west = jnp.where(not_first, to_east[h], to_east[h - 1] if h else west_edge)
                east = jnp.where(not_last, to_west[h], to_west[h + 1] if h + 1 < tiles else east_edge)
                down = pltpu.roll(x[h], 1, 0)
                north = jnp.where(not_top, down, above[h])
                above[h] = down
                up = pltpu.roll(x[h], 7, 0)
                if r + 1 < strips:
                    following = pltpu.roll(c_ref[k, 8 * r + 8 : 8 * r + 16, lanes], 7, 0)
                else:
                    following = below[h]
                south = jnp.where(not_bottom, up, following)
                spin = v_ref[0, k, these, lanes].astype(f32)
                sweep = v_ref[1, k, these, lanes].astype(f32)
                y = x[h] - (spin * ((east - west) * scale_phi) + sweep * ((south - north) * scale_theta))
                out_ref[r, 0, k, h] = y * weights
                out_ref[r, 1, k, h] = (x[h] * x[h] * x[h] - x[h]) * weights


def stencil_stage(phase, velocity, weights, halos, scale_phi, scale_theta):
    shells, rows, cols = phase.shape
    kb = 16

    def kernel(*refs):
        stencil_kernel(scale_phi, *refs)

    return pl.pallas_call(
        kernel,
        grid=(shells // kb,),
        in_specs=[
            pl.BlockSpec(memory_space=pltpu.SMEM),
            pl.BlockSpec((kb, rows, cols), lambda i: (i, 0, 0)),
            pl.BlockSpec((2, kb, rows, cols), lambda i: (0, i, 0, 0)),
            pl.BlockSpec(weights.shape, lambda i: (0, 0)),
            pl.BlockSpec((rows, 128), lambda i: (0, 0)),
            pl.BlockSpec((rows, 128), lambda i: (0, 0)),
            pl.BlockSpec((kb, cols), lambda i: (i, 0)),
            pl.BlockSpec((kb, cols), lambda i: (i, 0)),
        ],
        out_specs=pl.BlockSpec((rows // 8, 2, kb, cols // 128, 8, 128), lambda i: (0, 0, i, 0, 0, 0)),
        out_shape=jax.ShapeDtypeStruct((rows // 8, 2, shells, cols // 128, 8, 128), f32),
        compiler_params=params(48),
        name="stencil",
    )(scale_theta, phase, velocity, weights, *halos)


def cos_and_minus_sin(turns, full):
    shift = (full // 4).bit_length() - 1
    quadrant = (turns + full // 8) >> shift
    rest = turns - (quadrant << shift)
    x = rest.astype(f32) * (2.0 * math.pi / full)
    q = quadrant & 3
    x2 = x * x
    cos = 1.0 + x2 * (-1.0 / 2 + x2 * (1.0 / 24 + x2 * (-1.0 / 720 + x2 * (1.0 / 40320))))
    sin = x + x * x2 * (-1.0 / 6 + x2 * (1.0 / 120 + x2 * (-1.0 / 5040 + x2 * (1.0 / 362880))))
    swap = (q & 1) == 1
    c = jnp.where(swap, sin, cos)
    s = jnp.where(swap, cos, sin)
    return jnp.where((q == 1) | (q == 2), -c, c), jnp.where(q >= 2, s, -s)


def table_kernel(mode_ref, out_ref):
    parities, modes, _ = mode_ref.shape
    half_phi = out_ref.shape[2]
    tiles = half_phi // 128
    lane = lax.broadcasted_iota(jnp.int32, (modes, 128), 1)
    for parity in range(parities):
        orders = mode_ref[parity]
        fc, fs = cos_and_minus_sin(orders * lane, 2 * half_phi)
        coarse_c, coarse_s = cos_and_minus_sin(orders * lane * 128, 2 * half_phi)
        for u in range(tiles):
            cc = jnp.broadcast_to(coarse_c[:, u : u + 1], (modes, 128))
            cs = jnp.broadcast_to(coarse_s[:, u : u + 1], (modes, 128))
            for i, value in enumerate((fc * cc - fs * cs, fs * cc + fc * cs)):
                h, l = split(value)
                lanes = slice(128 * u, 128 * u + 128)
                out_ref[parity, i * modes : (i + 1) * modes, lanes] = h
                out_ref[parity, (2 + i) * modes : (3 + i) * modes, lanes] = l


def wave_tables(owned_modes, phi_count):
    first_half = owned_modes[:, :2].T.reshape(-1)
    top = owned_modes.shape[0] * owned_modes.shape[1] - 1
    even = jnp.where(first_half % 2 == 0, first_half, top - first_half)
    modes = jnp.stack([even, top - even])
    count = modes.shape[1]
    whole = pl.BlockSpec(memory_space=pltpu.VMEM)
    return pl.pallas_call(
        table_kernel,
        in_specs=[whole],
        out_specs=whole,
        out_shape=jax.ShapeDtypeStruct((2, 4 * count, phi_count // 2), bf16),
        compiler_params=params(24),
        name="table",
    )(jnp.broadcast_to(modes[:, :, None], (2, count, 128)))


def fourier_kernel(p_ref, table_ref, out_ref, xh, xl):
    parts, fields = p_ref.shape[:2]
    half = parts // 2
    per = xh.shape[1] // 8
    tiles = xh.shape[2] // half // 128
    both = table_ref.shape[1] // 2
    count = both // 2
    owners = count // 2
    stride = out_ref.shape[0] // owners

    def one(f, carry):
        for a in range(half):
            for t in range(8):
                for j in range(tiles):
                    strided = pl.ds(8 * j + t, per, stride=8 * tiles)
                    near, far = p_ref[a, f, strided, :], p_ref[a + half, f, strided, :]
                    lanes = slice((a * tiles + j) * 128, (a * tiles + j + 1) * 128)
                    for parity, x in enumerate((near + far, near - far)):
                        h, l = split(x)
                        xh[parity, t * per : (t + 1) * per, lanes] = h
                        xl[parity, t * per : (t + 1) * per, lanes] = l
        for parity in range(2):
            y = dot_nt(table_ref[parity], xh[parity])
            y = y[:both] + (y[both:] + dot_nt(table_ref[parity, :both], xl[parity]))
            for u in range(4):
                pair = swap_halves(y[:count, 128 * u : 128 * u + 128], y[count:, 128 * u : 128 * u + 128])
                for s in range(2):
                    for v in range(2):
                        at = f * (stride // fields) + (2 * parity + s) * 8 + 2 * u + v
                        out_ref[pl.ds(at, owners, stride=stride), :] = pair[v][s * owners : (s + 1) * owners]
        return carry

    lax.fori_loop(0, fields, one, 0)


def fourier_stage(rows_all, table):
    parts, fields, shells, tiles, tb, _ = rows_all.shape
    half_phi = table.shape[2]
    owners = table.shape[1] // 8
    flat = rows_all.reshape(parts, fields, shells * tiles * tb, 128)
    whole = pl.BlockSpec(memory_space=pltpu.VMEM)
    out = pl.pallas_call(
        fourier_kernel,
        in_specs=[whole, whole],
        out_specs=whole,
        out_shape=jax.ShapeDtypeStruct((owners * fields * 4 * 8, 128), f32),
        scratch_shapes=[
            pltpu.VMEM((2, shells * tb, half_phi), bf16),
            pltpu.VMEM((2, shells * tb, half_phi), bf16),
        ],
        compiler_params=params(32),
        name="fourier",
    )(flat, table)
    return out.reshape(owners, fields, 2, 2, 8, 128)


def spectral_kernel(az, col, mode_ref, r_ref, leg, rad, fac_ref, out_ref, xh, xl, rhs, sol, radf):
    degrees = leg.shape[2]
    shells = rad.shape[0]
    tb = az * 8
    tiles = degrees // 128
    half = degrees // 2
    for q in range(4):
        parity = mode_ref[q] % 2
        for f in range(2):
            x = jnp.concatenate(
                [r_ref[a * col + c, f, parity, q % 2] for c in range(col) for a in range(az)], axis=0
            )
            h, l = split(x.T)
            xh[q, f * 128 : (f + 1) * 128, :] = h
            xl[q, f * 128 : (f + 1) * 128, :] = l

    def right_side(q, lanes):
        coef = dot_nn(xh[q], leg[q, :, lanes]) + dot_nn(xl[q], leg[q, :, lanes])
        return coef[:128] - fac_ref[:, lanes] * coef[128:]

    def put(q, first, right):
        for i in range(2):
            for n in range(tiles // 2):
                rhs[first + n, pl.ds(2 * q + i, shells, stride=8), :] = right[
                    i * shells : (i + 1) * shells, n * 128 : n * 128 + 128
                ]

    for q in range(4):
        put(q, tiles // 2, right_side(q, slice(half, degrees)))
    low = [jnp.where(mode_ref[s] < half, s, s + 2) for s in range(2)]
    high = [jnp.where(mode_ref[s] < half, s + 2, s) for s in range(2)]
    for s in range(2):
        put(low[s], 0, right_side(low[s], slice(0, half)))
        put(high[s], 0, jnp.zeros((2 * shells, half), f32))

    rb = 8

    def outer(block, carry):
        radf[...] = rad[pl.ds(block * rb, rb)].astype(f32)
        for lt in range(tiles):
            lanes = slice(lt * 128, lt * 128 + 128)
            acc = [jnp.zeros((8, 128), f32) for _ in range(rb)]
            for s in range(shells):
                v = rhs[lt, 8 * s : 8 * s + 8, :]
                for r in range(rb):
                    acc[r] = acc[r] + radf[r, s : s + 1, lanes] * v
            for r in range(rb):
                sol[lt, pl.ds(pl.multiple_of((block * rb + r) * 8, 8), 8), :] = acc[r]
        return carry

    lax.fori_loop(0, shells // rb, outer, 0)

    for s in range(2):
        for q, first in ((low[s], 0), (high[s], tiles // 2)):
            gain = jnp.where(mode_ref[q] == 0, 1.0, 2.0).astype(f32)
            x = jnp.concatenate(
                [
                    jnp.concatenate(
                        [sol[lt, pl.ds(2 * q + i, shells, stride=8), :] for lt in range(first, tiles)], axis=1
                    )
                    for i in range(2)
                ],
                axis=0,
            )
            h, l = split(x * gain)
            matrix = leg[q, :, first * 128 :]
            y = dot_nt(matrix, h) + dot_nt(matrix, l)
            slot = 2 * (mode_ref[q] % 2) + s
            for c in range(col):
                for a in range(az):
                    out_ref[a * col + c, slot] = y[c * tb + a * 8 : c * tb + a * 8 + 8]


def spectral_stage(received, legendre, radial, factor, own, az, col):
    owners = received.shape[0]
    modes, theta, degrees = legendre.shape
    shells = radial.shape[0]

    def kernel(*refs):
        spectral_kernel(az, col, *refs)

    whole = pl.BlockSpec(memory_space=pltpu.VMEM)
    return pl.pallas_call(
        kernel,
        in_specs=[pl.BlockSpec(memory_space=pltpu.SMEM), whole, whole, whole, whole],
        out_specs=whole,
        scratch_shapes=[
            pltpu.VMEM((4, 256, theta), bf16),
            pltpu.VMEM((4, 256, theta), bf16),
            pltpu.VMEM((degrees // 128, 8 * shells, 128), f32),
            pltpu.VMEM((degrees // 128, 8 * shells, 128), f32),
            pltpu.VMEM((8, shells, degrees), f32),
        ],
        out_shape=jax.ShapeDtypeStruct((owners, 4, 8, 128), f32),
        compiler_params=params(32),
        name="spectral",
    )(own, received, legendre, radial, factor)


def inverse_kernel(z_ref, table_ref, out_ref, gh, gl):
    owners = z_ref.shape[0] // 32
    rows = gh.shape[1]
    per = rows // 8
    both = table_ref.shape[1] // 2
    quarters = out_ref.shape[1]
    cols = table_ref.shape[2] // quarters
    tiles = cols // 128
    for par in range(2):
        halves = [[], []]
        for s in range(2):
            base = (par * 2 + s) * 8
            cos_u, sin_u = [], []
            for u in range(4):
                a = z_ref[pl.ds(base + 2 * u, owners, stride=32), :]
                b = z_ref[pl.ds(base + 2 * u + 1, owners, stride=32), :]
                first, second = swap_halves(a, b)
                cos_u.append(first)
                sin_u.append(second)
            halves[0].append(jnp.concatenate(cos_u, axis=1))
            halves[1].append(jnp.concatenate(sin_u, axis=1))
        for i in range(2):
            for s in range(2):
                h, l = split(halves[i][s].T)
                at = (2 * i + s) * owners
                gh[par, :, at : at + owners] = h
                gh[par, :, both + at : both + at + owners] = h
                gl[par, :, at : at + owners] = l

    for quarter in range(quarters):
        lanes = slice(quarter * cols, (quarter + 1) * cols)
        sums = []
        for par in range(2):
            sums.append(dot_nn(gh[par], table_ref[par, :, lanes]) + dot_nn(gl[par], table_ref[par, :both, lanes]))
        near = sums[0] + sums[1]
        far = sums[0] - sums[1]
        for t in range(8):
            for j in range(tiles):
                part = slice(j * 128, j * 128 + 128)
                strided = pl.ds(8 * j + t, per, stride=8 * tiles)
                out_ref[0, quarter, strided, :] = near[t * per : (t + 1) * per, part]
                out_ref[1, quarter, strided, :] = far[t * per : (t + 1) * per, part]


def inverse_stage(received, table, shells, az):
    owners, _, tb, _ = received.shape
    half_phi = table.shape[2]
    modes2 = table.shape[1] // 2
    flat = received.reshape(owners * 4 * tb, 128)
    cols = 2 * half_phi // az
    rows = shells * tb
    whole = pl.BlockSpec(memory_space=pltpu.VMEM)
    out = pl.pallas_call(
        inverse_kernel,
        in_specs=[whole, whole],
        out_specs=whole,
        out_shape=jax.ShapeDtypeStruct((2, az // 2, rows * cols // 128, 128), f32),
        scratch_shapes=[
            pltpu.VMEM((2, rows, 2 * modes2), bf16),
            pltpu.VMEM((2, rows, modes2), bf16),
        ],
        compiler_params=params(32),
        name="inverse",
    )(flat, table)
    return out.reshape(az, shells, cols // 128, tb, 128)


def gather_kernel(w_ref, out_ref, sem):
    parts, shells, tiles = w_ref.shape[:3]
    copies = []
    for a in range(parts):
        for h in range(tiles):
            copies.append(
                pltpu.make_async_copy(
                    w_ref.at[a, :, h],
                    out_ref.at[:, pl.ds(8 * a, 8), pl.ds(128 * h, 128)],
                    sem.at[a * tiles + h],
                )
            )
    for copy in copies:
        copy.start()
    for copy in copies:
        copy.wait()


def gather_stage(blocks):
    parts, shells, tiles, tb, _ = blocks.shape
    return pl.pallas_call(
        gather_kernel,
        in_specs=[pl.BlockSpec(memory_space=pltpu.VMEM)],
        out_specs=pl.BlockSpec(memory_space=pl.ANY),
        out_shape=jax.ShapeDtypeStruct((shells, parts * tb, tiles * 128), f32),
        scratch_shapes=[pltpu.SemaphoreType.DMA((parts * tiles,))],
        compiler_params=params(16),
        name="gather",
    )(blocks)


def exchange(x, axes):
    return lax.all_to_all(x, axes, split_axis=0, concat_axis=0, tiled=True)


def body(phase_field, velocity, owned_modes, legendre, radial_inverse):
    shells, theta_local, phi_local = phase_field.shape
    az_count = lax.axis_size("az")
    col_count = lax.axis_size("col")
    az_here = lax.axis_index("az")
    col_here = lax.axis_index("col")
    phi_count = phi_local * az_count
    theta_count = theta_local * col_count
    degree_count = legendre.shape[2]
    radius = shell_radii(shells)

    weights = (colat_weights(theta_count) / phi_count).astype(np.float32)
    weights = jnp.asarray(np.repeat(weights[:, None], 128, axis=1))

    even_az = [(i, i ^ 1) for i in range(az_count)]
    odd_az = [(i, (i + 1 if i % 2 else i - 1) % az_count) for i in range(az_count)]
    even_col = [(i, i ^ 1) for i in range(col_count)]
    odd_col = [(i, i + 1 if i % 2 else i - 1) for i in range(1, col_count - 1)]
    col_even, col_odd = row_edges_stage(phase_field)
    col_halos = (lax.ppermute(col_even, "col", even_col), lax.ppermute(col_odd, "col", odd_col))
    field, _ = lax.optimization_barrier((phase_field, col_odd))
    az_even, az_odd = column_edges_stage(field)
    az_halos = (lax.ppermute(az_even, "az", even_az), lax.ppermute(az_odd, "az", odd_az))
    halos = az_halos + col_halos

    here = az_here * col_count + col_here
    own = lax.dynamic_slice(owned_modes, (here, 0), (1, owned_modes.shape[1])).reshape(-1)
    degrees = np.arange(degree_count)
    factor = mobility_step * (degrees * (degrees + 1.0))[None, :] / (radius * radius)[:, None]
    factor = jnp.asarray(np.concatenate([factor, factor], axis=0).astype(np.float32))
    radial = jnp.transpose(radial_inverse, (1, 2, 0))
    table = wave_tables(owned_modes, phi_count)

    scale_phi = step_time * phi_count / (4.0 * math.pi)
    scale_theta = jnp.asarray((step_time * theta_count / (2.0 * math.pi) / radius).astype(np.float32))
    fields = stencil_stage(
        phase_field, velocity, weights, halos, scale_phi, scale_theta
    )
    fields, table, own = lax.optimization_barrier((fields, table, own))
    received = exchange(fourier_stage(exchange(fields, "az"), table), everyone)
    synthesis = spectral_stage(
        received, legendre, radial, factor, own, az_count, col_count
    )
    grid_modes = exchange(synthesis, everyone)

    blocks = inverse_stage(grid_modes, table, shells, az_count)
    return gather_stage(exchange(blocks, "az"))


def solution(mesh):
    in_specs = (
        P(None, "col", "az"),
        P(None, None, "col", "az"),
        P(),
        P(("az", "col"), None, None),
        P(),
    )
    out_specs = P(None, "col", "az")
    return jax.shard_map(body, mesh=mesh, in_specs=in_specs, out_specs=out_specs, check_vma=False)
```

```python
import math

import jax
import jax.numpy as jnp
import numpy as np
from jax import lax
from jax.experimental import pallas as pl
from jax.experimental.pallas import tpu as pltpu
from jax.sharding import PartitionSpec as P

step_time = 0.002
mobility_step = 4e-06
f32 = jnp.float32
bf16 = jnp.bfloat16
everyone = ("az", "col")


def params(mib=48):
    return pltpu.CompilerParams(vmem_limit_bytes=mib * 1024 * 1024)


def colat_weights(count):
    theta = math.pi * (np.arange(count) + 0.5) / count
    waves = np.arange(1, count // 2 + 1)
    total = (np.cos(2.0 * waves[None, :] * theta[:, None]) / (4.0 * waves * waves - 1.0)).sum(1)
    return 2.0 / count * (1.0 - 2.0 * total)


def shell_radii(shells):
    return 0.75 + 0.25 * (np.arange(shells) + 0.5) / shells


def split(x):
    hi = x.astype(bf16)
    return hi, (x - hi.astype(f32)).astype(bf16)


def dot_nn(a, b):
    return lax.dot_general(a, b, (((1,), (0,)), ((), ())), preferred_element_type=f32)


def dot_nt(a, b):
    return lax.dot_general(a, b, (((1,), (1,)), ((), ())), preferred_element_type=f32)


def swap_halves(a, b):
    half = lax.broadcasted_iota(jnp.int32, a.shape, 1) < 64
    first = jnp.where(half, a, pltpu.roll(b, 64, 1))
    second = jnp.where(half, pltpu.roll(a, 64, 1), b)
    return first, second


def edges_kernel(c_hbm, az_even_ref, az_odd_ref, col_even_ref, col_odd_ref, c_ref, sems):
    shells, rows, cols = c_ref.shape
    chunks = sems.shape[0]
    size = shells // chunks
    copies = [
        pltpu.make_async_copy(c_hbm.at[pl.ds(n * size, size)], c_ref.at[pl.ds(n * size, size)], sems.at[n])
        for n in range(chunks)
    ]
    for copy in copies:
        copy.start()
    lane = lax.broadcasted_iota(jnp.int32, (rows, 128), 1)
    low = jnp.zeros((rows, 128), f32)
    high = jnp.zeros((rows, 128), f32)
    for k in range(shells):
        if k % size == 0:
            copies[k // size].wait()
        low = jnp.where(lane == k, pltpu.roll(c_ref[k, :, :128], k, 1), low)
        high = jnp.where(lane == k, pltpu.roll(c_ref[k, :, cols - 128 :], k + 1, 1), high)
    odd = lax.axis_index("az") % 2 == 1
    az_even_ref[...] = jnp.where(odd, low, high)
    az_odd_ref[...] = jnp.where(odd, high, low)
    low, high = c_ref[:, 0, :], c_ref[:, rows - 1, :]
    odd = lax.axis_index("col") % 2 == 1
    col_even_ref[...] = jnp.where(odd, low, high)
    col_odd_ref[...] = jnp.where(odd, high, low)


def edges_stage(phase):
    shells, rows, cols = phase.shape
    whole = pl.BlockSpec(memory_space=pltpu.VMEM)
    return pl.pallas_call(
        edges_kernel,
        in_specs=[pl.BlockSpec(memory_space=pl.ANY)],
        out_specs=[whole] * 4,
        out_shape=[
            jax.ShapeDtypeStruct((rows, 128), f32),
            jax.ShapeDtypeStruct((rows, 128), f32),
            jax.ShapeDtypeStruct((shells, cols), f32),
            jax.ShapeDtypeStruct((shells, cols), f32),
        ],
        scratch_shapes=[pltpu.VMEM(phase.shape, f32), pltpu.SemaphoreType.DMA((8,))],
        compiler_params=params(52),
        name="edges",
    )(phase)


def stencil_kernel(
    scale_phi, scale_ref, c_ref, v_ref, w_ref, col_odd_ref, az_odd_ref, az_even_ref, col_even_ref, out_ref
):
    shells, rows, cols = c_ref.shape
    block = pl.program_id(0)
    tiles, strips = cols // 128, rows // 8
    lane = lax.broadcasted_iota(jnp.int32, (8, 128), 1)
    row = lax.broadcasted_iota(jnp.int32, (8, 128), 0)
    not_first, not_last = lane > 0, lane < 127
    not_top, not_bottom = row > 0, row < 7
    az_odd = lax.axis_index("az") % 2 == 1
    col_here = lax.axis_index("col")
    col_odd = col_here % 2 == 1
    turn = jnp.where(block == 0, 0, 128 - block * shells)
    west_all = pltpu.roll(jnp.where(az_odd, az_even_ref[...], az_odd_ref[...]), turn, 1)
    east_all = pltpu.roll(jnp.where(az_odd, az_odd_ref[...], az_even_ref[...]), turn, 1)
    north_all = jnp.where(col_odd, col_even_ref[...], col_odd_ref[...])
    south_all = jnp.where(col_odd, col_odd_ref[...], col_even_ref[...])
    for k in range(shells):
        scale_theta = scale_ref[block * shells + k]
        above, below = [], []
        for h in range(tiles):
            lanes = slice(128 * h, 128 * h + 128)
            above.append(jnp.broadcast_to(north_all[k : k + 1, lanes], (8, 128)))
            below.append(jnp.broadcast_to(south_all[k : k + 1, lanes], (8, 128)))
        for r in range(strips):
            these = slice(8 * r, 8 * r + 8)
            x = [c_ref[k, these, 128 * h : 128 * h + 128] for h in range(tiles)]
            to_east = [pltpu.roll(t, 1, 1) for t in x]
            to_west = [pltpu.roll(t, 127, 1) for t in x]
            west_edge = jnp.broadcast_to(west_all[these, k : k + 1], (8, 128))
            east_edge = jnp.broadcast_to(east_all[these, k : k + 1], (8, 128))
            weights = w_ref[pl.ds(pl.multiple_of(col_here * rows + 8 * r, 8), 8), :]
            for h in range(tiles):
                lanes = slice(128 * h, 128 * h + 128)
                west = jnp.where(not_first, to_east[h], to_east[h - 1] if h else west_edge)
                east = jnp.where(not_last, to_west[h], to_west[h + 1] if h + 1 < tiles else east_edge)
                down = pltpu.roll(x[h], 1, 0)
                north = jnp.where(not_top, down, above[h])
                above[h] = down
                up = pltpu.roll(x[h], 7, 0)
                if r + 1 < strips:
                    following = pltpu.roll(c_ref[k, 8 * r + 8 : 8 * r + 16, lanes], 7, 0)
                else:
                    following = below[h]
                south = jnp.where(not_bottom, up, following)
                spin = v_ref[0, k, these, lanes].astype(f32)
                sweep = v_ref[1, k, these, lanes].astype(f32)
                y = x[h] - (spin * ((east - west) * scale_phi) + sweep * ((south - north) * scale_theta))
                out_ref[r, 0, k, h] = y * weights
                out_ref[r, 1, k, h] = (x[h] * x[h] * x[h] - x[h]) * weights


def stencil_stage(phase, velocity, weights, halos, scale_phi, scale_theta):
    shells, rows, cols = phase.shape
    kb = 16

    def kernel(*refs):
        stencil_kernel(scale_phi, *refs)

    return pl.pallas_call(
        kernel,
        grid=(shells // kb,),
        in_specs=[
            pl.BlockSpec(memory_space=pltpu.SMEM),
            pl.BlockSpec((kb, rows, cols), lambda i: (i, 0, 0)),
            pl.BlockSpec((2, kb, rows, cols), lambda i: (0, i, 0, 0)),
            pl.BlockSpec(weights.shape, lambda i: (0, 0)),
            pl.BlockSpec((kb, cols), lambda i: (i, 0)),
            pl.BlockSpec((rows, 128), lambda i: (0, 0)),
            pl.BlockSpec((rows, 128), lambda i: (0, 0)),
            pl.BlockSpec((kb, cols), lambda i: (i, 0)),
        ],
        out_specs=pl.BlockSpec((rows // 8, 2, kb, cols // 128, 8, 128), lambda i: (0, 0, i, 0, 0, 0)),
        out_shape=jax.ShapeDtypeStruct((rows // 8, 2, shells, cols // 128, 8, 128), f32),
        compiler_params=params(48),
        name="stencil",
    )(scale_theta, phase, velocity, weights, *halos)


def cos_and_minus_sin(turns, full):
    shift = (full // 4).bit_length() - 1
    quadrant = (turns + full // 8) >> shift
    rest = turns - (quadrant << shift)
    x = rest.astype(f32) * (2.0 * math.pi / full)
    q = quadrant & 3
    x2 = x * x
    cos = 1.0 + x2 * (-1.0 / 2 + x2 * (1.0 / 24 + x2 * (-1.0 / 720 + x2 * (1.0 / 40320))))
    sin = x + x * x2 * (-1.0 / 6 + x2 * (1.0 / 120 + x2 * (-1.0 / 5040 + x2 * (1.0 / 362880))))
    swap = (q & 1) == 1
    c = jnp.where(swap, sin, cos)
    s = jnp.where(swap, cos, sin)
    return jnp.where((q == 1) | (q == 2), -c, c), jnp.where(q >= 2, s, -s)


def table_kernel(mode_ref, out_ref):
    parities, modes, _ = mode_ref.shape
    half_phi = out_ref.shape[2]
    tiles = half_phi // 128
    lane = lax.broadcasted_iota(jnp.int32, (modes, 128), 1)
    for parity in range(parities):
        orders = mode_ref[parity]
        fc, fs = cos_and_minus_sin(orders * lane, 2 * half_phi)
        coarse_c, coarse_s = cos_and_minus_sin(orders * lane * 128, 2 * half_phi)
        for u in range(tiles):
            cc = jnp.broadcast_to(coarse_c[:, u : u + 1], (modes, 128))
            cs = jnp.broadcast_to(coarse_s[:, u : u + 1], (modes, 128))
            for i, value in enumerate((fc * cc - fs * cs, fs * cc + fc * cs)):
                h, l = split(value)
                lanes = slice(128 * u, 128 * u + 128)
                out_ref[parity, i * modes : (i + 1) * modes, lanes] = h
                out_ref[parity, (2 + i) * modes : (3 + i) * modes, lanes] = l


def wave_tables(owned_modes, phi_count):
    first_half = owned_modes[:, :2].T.reshape(-1)
    top = owned_modes.shape[0] * owned_modes.shape[1] - 1
    even = jnp.where(first_half % 2 == 0, first_half, top - first_half)
    modes = jnp.stack([even, top - even])
    count = modes.shape[1]
    whole = pl.BlockSpec(memory_space=pltpu.VMEM)
    return pl.pallas_call(
        table_kernel,
        in_specs=[whole],
        out_specs=whole,
        out_shape=jax.ShapeDtypeStruct((2, 4 * count, phi_count // 2), bf16),
        compiler_params=params(24),
        name="table",
    )(jnp.broadcast_to(modes[:, :, None], (2, count, 128)))


def fourier_kernel(p_ref, table_ref, out_ref, xh, xl):
    parts, fields = p_ref.shape[:2]
    half = parts // 2
    per = xh.shape[1] // 8
    tiles = xh.shape[2] // half // 128
    both = table_ref.shape[1] // 2
    count = both // 2
    owners = count // 2
    stride = out_ref.shape[0] // owners

    def one(f, carry):
        for a in range(half):
            for t in range(8):
                for j in range(tiles):
                    strided = pl.ds(8 * j + t, per, stride=8 * tiles)
                    near, far = p_ref[a, f, strided, :], p_ref[a + half, f, strided, :]
                    lanes = slice((a * tiles + j) * 128, (a * tiles + j + 1) * 128)
                    for parity, x in enumerate((near + far, near - far)):
                        h, l = split(x)
                        xh[parity, t * per : (t + 1) * per, lanes] = h
                        xl[parity, t * per : (t + 1) * per, lanes] = l
        for parity in range(2):
            y = dot_nt(table_ref[parity], xh[parity])
            y = y[:both] + (y[both:] + dot_nt(table_ref[parity, :both], xl[parity]))
            for u in range(4):
                pair = swap_halves(y[:count, 128 * u : 128 * u + 128], y[count:, 128 * u : 128 * u + 128])
                for s in range(2):
                    for v in range(2):
                        at = f * (stride // fields) + (2 * parity + s) * 8 + 2 * u + v
                        out_ref[pl.ds(at, owners, stride=stride), :] = pair[v][s * owners : (s + 1) * owners]
        return carry

    lax.fori_loop(0, fields, one, 0)


def fourier_stage(rows_all, table):
    parts, fields, shells, tiles, tb, _ = rows_all.shape
    half_phi = table.shape[2]
    owners = table.shape[1] // 8
    flat = rows_all.reshape(parts, fields, shells * tiles * tb, 128)
    whole = pl.BlockSpec(memory_space=pltpu.VMEM)
    out = pl.pallas_call(
        fourier_kernel,
        in_specs=[whole, whole],
        out_specs=whole,
        out_shape=jax.ShapeDtypeStruct((owners * fields * 4 * 8, 128), f32),
        scratch_shapes=[
            pltpu.VMEM((2, shells * tb, half_phi), bf16),
            pltpu.VMEM((2, shells * tb, half_phi), bf16),
        ],
        compiler_params=params(32),
        name="fourier",
    )(flat, table)
    return out.reshape(owners, fields, 2, 2, 8, 128)


def spectral_kernel(az, col, mode_ref, r_ref, leg, rad, fac_ref, out_ref, xh, xl, rhs, sol, radf):
    degrees = leg.shape[2]
    shells = rad.shape[0]
    tb = az * 8
    tiles = degrees // 128
    half = degrees // 2
    for q in range(4):
        parity = mode_ref[q] % 2
        for f in range(2):
            x = jnp.concatenate(
                [r_ref[a * col + c, f, parity, q % 2] for c in range(col) for a in range(az)], axis=0
            )
            h, l = split(x.T)
            xh[q, f * 128 : (f + 1) * 128, :] = h
            xl[q, f * 128 : (f + 1) * 128, :] = l

    def right_side(q, lanes):
        coef = dot_nn(xh[q], leg[q, :, lanes]) + dot_nn(xl[q], leg[q, :, lanes])
        return coef[:128] - fac_ref[:, lanes] * coef[128:]

    def put(q, first, right):
        for i in range(2):
            for n in range(tiles // 2):
                rhs[first + n, pl.ds(2 * q + i, shells, stride=8), :] = right[
                    i * shells : (i + 1) * shells, n * 128 : n * 128 + 128
                ]

    for q in range(4):
        put(q, tiles // 2, right_side(q, slice(half, degrees)))
    low = [jnp.where(mode_ref[s] < half, s, s + 2) for s in range(2)]
    high = [jnp.where(mode_ref[s] < half, s + 2, s) for s in range(2)]
    for s in range(2):
        put(low[s], 0, right_side(low[s], slice(0, half)))
        put(high[s], 0, jnp.zeros((2 * shells, half), f32))

    rb = 8

    def outer(block, carry):
        radf[...] = rad[pl.ds(block * rb, rb)].astype(f32)
        for lt in range(tiles):
            lanes = slice(lt * 128, lt * 128 + 128)
            acc = [jnp.zeros((8, 128), f32) for _ in range(rb)]
            for s in range(shells):
                v = rhs[lt, 8 * s : 8 * s + 8, :]
                for r in range(rb):
                    acc[r] = acc[r] + radf[r, s : s + 1, lanes] * v
            for r in range(rb):
                sol[lt, pl.ds(pl.multiple_of((block * rb + r) * 8, 8), 8), :] = acc[r]
        return carry

    lax.fori_loop(0, shells // rb, outer, 0)

    for s in range(2):
        for q, first in ((low[s], 0), (high[s], tiles // 2)):
            gain = jnp.where(mode_ref[q] == 0, 1.0, 2.0).astype(f32)
            x = jnp.concatenate(
                [
                    jnp.concatenate(
                        [sol[lt, pl.ds(2 * q + i, shells, stride=8), :] for lt in range(first, tiles)], axis=1
                    )
                    for i in range(2)
                ],
                axis=0,
            )
            h, l = split(x * gain)
            matrix = leg[q, :, first * 128 :]
            y = dot_nt(matrix, h) + dot_nt(matrix, l)
            slot = 2 * (mode_ref[q] % 2) + s
            for c in range(col):
                for a in range(az):
                    out_ref[a * col + c, slot] = y[c * tb + a * 8 : c * tb + a * 8 + 8]


def spectral_stage(received, legendre, radial, factor, own, az, col):
    owners = received.shape[0]
    modes, theta, degrees = legendre.shape
    shells = radial.shape[0]

    def kernel(*refs):
        spectral_kernel(az, col, *refs)

    whole = pl.BlockSpec(memory_space=pltpu.VMEM)
    return pl.pallas_call(
        kernel,
        in_specs=[pl.BlockSpec(memory_space=pltpu.SMEM), whole, whole, whole, whole],
        out_specs=whole,
        scratch_shapes=[
            pltpu.VMEM((4, 256, theta), bf16),
            pltpu.VMEM((4, 256, theta), bf16),
            pltpu.VMEM((degrees // 128, 8 * shells, 128), f32),
            pltpu.VMEM((degrees // 128, 8 * shells, 128), f32),
            pltpu.VMEM((8, shells, degrees), f32),
        ],
        out_shape=jax.ShapeDtypeStruct((owners, 4, 8, 128), f32),
        compiler_params=params(32),
        name="spectral",
    )(own, received, legendre, radial, factor)


def inverse_kernel(z_ref, table_ref, out_ref, gh, gl):
    owners = z_ref.shape[0] // 32
    rows = gh.shape[1]
    per = rows // 8
    both = table_ref.shape[1] // 2
    quarters = out_ref.shape[1]
    cols = table_ref.shape[2] // quarters
    tiles = cols // 128
    for par in range(2):
        halves = [[], []]
        for s in range(2):
            base = (par * 2 + s) * 8
            cos_u, sin_u = [], []
            for u in range(4):
                a = z_ref[pl.ds(base + 2 * u, owners, stride=32), :]
                b = z_ref[pl.ds(base + 2 * u + 1, owners, stride=32), :]
                first, second = swap_halves(a, b)
                cos_u.append(first)
                sin_u.append(second)
            halves[0].append(jnp.concatenate(cos_u, axis=1))
            halves[1].append(jnp.concatenate(sin_u, axis=1))
        for i in range(2):
            for s in range(2):
                h, l = split(halves[i][s].T)
                at = (2 * i + s) * owners
                gh[par, :, at : at + owners] = h
                gh[par, :, both + at : both + at + owners] = h
                gl[par, :, at : at + owners] = l

    for quarter in range(quarters):
        lanes = slice(quarter * cols, (quarter + 1) * cols)
        sums = []
        for par in range(2):
            sums.append(dot_nn(gh[par], table_ref[par, :, lanes]) + dot_nn(gl[par], table_ref[par, :both, lanes]))
        near = sums[0] + sums[1]
        far = sums[0] - sums[1]
        for t in range(8):
            for j in range(tiles):
                part = slice(j * 128, j * 128 + 128)
                strided = pl.ds(8 * j + t, per, stride=8 * tiles)
                out_ref[0, quarter, strided, :] = near[t * per : (t + 1) * per, part]
                out_ref[1, quarter, strided, :] = far[t * per : (t + 1) * per, part]


def inverse_stage(received, table, shells, az):
    owners, _, tb, _ = received.shape
    half_phi = table.shape[2]
    modes2 = table.shape[1] // 2
    flat = received.reshape(owners * 4 * tb, 128)
    cols = 2 * half_phi // az
    rows = shells * tb
    whole = pl.BlockSpec(memory_space=pltpu.VMEM)
    out = pl.pallas_call(
        inverse_kernel,
        in_specs=[whole, whole],
        out_specs=whole,
        out_shape=jax.ShapeDtypeStruct((2, az // 2, rows * cols // 128, 128), f32),
        scratch_shapes=[
            pltpu.VMEM((2, rows, 2 * modes2), bf16),
            pltpu.VMEM((2, rows, modes2), bf16),
        ],
        compiler_params=params(32),
        name="inverse",
    )(flat, table)
    return out.reshape(az, shells, cols // 128, tb, 128)


def gather_kernel(w_ref, out_ref, sem):
    parts, shells, tiles = w_ref.shape[:3]
    copies = []
    for a in range(parts):
        for h in range(tiles):
            copies.append(
                pltpu.make_async_copy(
                    w_ref.at[a, :, h],
                    out_ref.at[:, pl.ds(8 * a, 8), pl.ds(128 * h, 128)],
                    sem.at[a * tiles + h],
                )
            )
    for copy in copies:
        copy.start()
    for copy in copies:
        copy.wait()


def gather_stage(blocks):
    parts, shells, tiles, tb, _ = blocks.shape
    return pl.pallas_call(
        gather_kernel,
        in_specs=[pl.BlockSpec(memory_space=pltpu.VMEM)],
        out_specs=pl.BlockSpec(memory_space=pl.ANY),
        out_shape=jax.ShapeDtypeStruct((shells, parts * tb, tiles * 128), f32),
        scratch_shapes=[pltpu.SemaphoreType.DMA((parts * tiles,))],
        compiler_params=params(16),
        name="gather",
    )(blocks)


def exchange(x, axes):
    return lax.all_to_all(x, axes, split_axis=0, concat_axis=0, tiled=True)


def body(phase_field, velocity, owned_modes, legendre, radial_inverse):
    shells, theta_local, phi_local = phase_field.shape
    az_count = lax.axis_size("az")
    col_count = lax.axis_size("col")
    az_here = lax.axis_index("az")
    col_here = lax.axis_index("col")
    phi_count = phi_local * az_count
    theta_count = theta_local * col_count
    degree_count = legendre.shape[2]
    radius = shell_radii(shells)

    weights = (colat_weights(theta_count) / phi_count).astype(np.float32)
    weights = jnp.asarray(np.repeat(weights[:, None], 128, axis=1))

    az_even, az_odd, col_even, col_odd = edges_stage(phase_field)
    even_az = [(i, i ^ 1) for i in range(az_count)]
    odd_az = [(i, (i + 1 if i % 2 else i - 1) % az_count) for i in range(az_count)]
    even_col = [(i, i ^ 1) for i in range(col_count)]
    odd_col = [(i, i + 1 if i % 2 else i - 1) for i in range(1, col_count - 1)]
    halos = (
        lax.ppermute(col_odd, "col", odd_col),
        lax.ppermute(az_odd, "az", odd_az),
        lax.ppermute(az_even, "az", even_az),
        lax.ppermute(col_even, "col", even_col),
    )

    here = az_here * col_count + col_here
    own = lax.dynamic_slice(owned_modes, (here, 0), (1, owned_modes.shape[1])).reshape(-1)
    degrees = np.arange(degree_count)
    factor = mobility_step * (degrees * (degrees + 1.0))[None, :] / (radius * radius)[:, None]
    factor = jnp.asarray(np.concatenate([factor, factor], axis=0).astype(np.float32))
    radial = jnp.transpose(radial_inverse, (1, 2, 0))
    table = wave_tables(owned_modes, phi_count)

    scale_phi = step_time * phi_count / (4.0 * math.pi)
    scale_theta = jnp.asarray((step_time * theta_count / (2.0 * math.pi) / radius).astype(np.float32))
    fields = stencil_stage(
        phase_field, velocity, weights, halos, scale_phi, scale_theta
    )
    fields, table, own = lax.optimization_barrier((fields, table, own))
    received = exchange(fourier_stage(exchange(fields, "az"), table), everyone)
    synthesis = spectral_stage(
        received, legendre, radial, factor, own, az_count, col_count
    )
    grid_modes = exchange(synthesis, everyone)

    blocks = inverse_stage(grid_modes, table, shells, az_count)
    return gather_stage(exchange(blocks, "az"))


def solution(mesh):
    in_specs = (
        P(None, "col", "az"),
        P(None, None, "col", "az"),
        P(),
        P(("az", "col"), None, None),
        P(),
    )
    out_specs = P(None, "col", "az")
    return jax.shard_map(body, mesh=mesh, in_specs=in_specs, out_specs=out_specs, check_vma=False)
```

```python
import math

import jax
import jax.numpy as jnp
import numpy as np
from jax import lax
from jax.experimental import pallas as pl
from jax.experimental.pallas import tpu as pltpu
from jax.sharding import PartitionSpec as P

step_time = 0.002
mobility_step = 4e-06
f32 = jnp.float32
bf16 = jnp.bfloat16
everyone = ("az", "col")


def params(mib=48):
    return pltpu.CompilerParams(vmem_limit_bytes=mib * 1024 * 1024)


def colat_weights(count):
    theta = math.pi * (np.arange(count) + 0.5) / count
    waves = np.arange(1, count // 2 + 1)
    total = (np.cos(2.0 * waves[None, :] * theta[:, None]) / (4.0 * waves * waves - 1.0)).sum(1)
    return 2.0 / count * (1.0 - 2.0 * total)


def shell_radii(shells):
    return 0.75 + 0.25 * (np.arange(shells) + 0.5) / shells


def split(x):
    hi = x.astype(bf16)
    return hi, (x - hi.astype(f32)).astype(bf16)


def dot_nn(a, b):
    return lax.dot_general(a, b, (((1,), (0,)), ((), ())), preferred_element_type=f32)


def dot_nt(a, b):
    return lax.dot_general(a, b, (((1,), (1,)), ((), ())), preferred_element_type=f32)


def swap_halves(a, b):
    half = lax.broadcasted_iota(jnp.int32, a.shape, 1) < 64
    first = jnp.where(half, a, pltpu.roll(b, 64, 1))
    second = jnp.where(half, pltpu.roll(a, 64, 1), b)
    return first, second


def edges_kernel(c_hbm, az_even_ref, az_odd_ref, col_even_ref, col_odd_ref, c_ref, sems):
    shells, rows, cols = c_ref.shape
    chunks = sems.shape[0]
    size = shells // chunks
    copies = [
        pltpu.make_async_copy(c_hbm.at[pl.ds(n * size, size)], c_ref.at[pl.ds(n * size, size)], sems.at[n])
        for n in range(chunks)
    ]
    for copy in copies:
        copy.start()
    lane = lax.broadcasted_iota(jnp.int32, (rows, 128), 1)
    low = jnp.zeros((rows, 128), f32)
    high = jnp.zeros((rows, 128), f32)
    for k in range(shells):
        if k % size == 0:
            copies[k // size].wait()
        low = jnp.where(lane == k, pltpu.roll(c_ref[k, :, :128], k, 1), low)
        high = jnp.where(lane == k, pltpu.roll(c_ref[k, :, cols - 128 :], k + 1, 1), high)
    odd = lax.axis_index("az") % 2 == 1
    az_even_ref[...] = jnp.where(odd, low, high)
    az_odd_ref[...] = jnp.where(odd, high, low)
    low, high = c_ref[:, 0, :], c_ref[:, rows - 1, :]
    odd = lax.axis_index("col") % 2 == 1
    col_even_ref[...] = jnp.where(odd, low, high)
    col_odd_ref[...] = jnp.where(odd, high, low)


def edges_stage(phase):
    shells, rows, cols = phase.shape
    whole = pl.BlockSpec(memory_space=pltpu.VMEM)
    return pl.pallas_call(
        edges_kernel,
        in_specs=[pl.BlockSpec(memory_space=pl.ANY)],
        out_specs=[whole] * 4,
        out_shape=[
            jax.ShapeDtypeStruct((rows, 128), f32),
            jax.ShapeDtypeStruct((rows, 128), f32),
            jax.ShapeDtypeStruct((shells, cols), f32),
            jax.ShapeDtypeStruct((shells, cols), f32),
        ],
        scratch_shapes=[pltpu.VMEM(phase.shape, f32), pltpu.SemaphoreType.DMA((8,))],
        compiler_params=params(52),
        name="edges",
    )(phase)


def stencil_kernel(
    scale_phi, scale_ref, c_ref, v_ref, w_ref, col_odd_ref, az_odd_ref, az_even_ref, col_even_ref, out_ref
):
    shells, rows, cols = c_ref.shape
    block = pl.program_id(0)
    tiles, strips = cols // 128, rows // 8
    lane = lax.broadcasted_iota(jnp.int32, (8, 128), 1)
    row = lax.broadcasted_iota(jnp.int32, (8, 128), 0)
    not_first, not_last = lane > 0, lane < 127
    not_top, not_bottom = row > 0, row < 7
    az_odd = lax.axis_index("az") % 2 == 1
    col_here = lax.axis_index("col")
    col_odd = col_here % 2 == 1
    turn = jnp.where(block == 0, 0, 128 - block * shells)
    west_all = pltpu.roll(jnp.where(az_odd, az_even_ref[...], az_odd_ref[...]), turn, 1)
    east_all = pltpu.roll(jnp.where(az_odd, az_odd_ref[...], az_even_ref[...]), turn, 1)
    north_all = jnp.where(col_odd, col_even_ref[...], col_odd_ref[...])
    south_all = jnp.where(col_odd, col_odd_ref[...], col_even_ref[...])
    for k in range(shells):
        scale_theta = scale_ref[block * shells + k]
        above, below = [], []
        for h in range(tiles):
            lanes = slice(128 * h, 128 * h + 128)
            above.append(jnp.broadcast_to(north_all[k : k + 1, lanes], (8, 128)))
            below.append(jnp.broadcast_to(south_all[k : k + 1, lanes], (8, 128)))
        for r in range(strips):
            these = slice(8 * r, 8 * r + 8)
            x = [c_ref[k, these, 128 * h : 128 * h + 128] for h in range(tiles)]
            to_east = [pltpu.roll(t, 1, 1) for t in x]
            to_west = [pltpu.roll(t, 127, 1) for t in x]
            west_edge = jnp.broadcast_to(west_all[these, k : k + 1], (8, 128))
            east_edge = jnp.broadcast_to(east_all[these, k : k + 1], (8, 128))
            weights = w_ref[pl.ds(pl.multiple_of(col_here * rows + 8 * r, 8), 8), :]
            for h in range(tiles):
                lanes = slice(128 * h, 128 * h + 128)
                west = jnp.where(not_first, to_east[h], to_east[h - 1] if h else west_edge)
                east = jnp.where(not_last, to_west[h], to_west[h + 1] if h + 1 < tiles else east_edge)
                down = pltpu.roll(x[h], 1, 0)
                north = jnp.where(not_top, down, above[h])
                above[h] = down
                up = pltpu.roll(x[h], 7, 0)
                if r + 1 < strips:
                    following = pltpu.roll(c_ref[k, 8 * r + 8 : 8 * r + 16, lanes], 7, 0)
                else:
                    following = below[h]
                south = jnp.where(not_bottom, up, following)
                spin = v_ref[0, k, these, lanes].astype(f32)
                sweep = v_ref[1, k, these, lanes].astype(f32)
                y = x[h] - (spin * ((east - west) * scale_phi) + sweep * ((south - north) * scale_theta))
                out_ref[r, 0, k, h] = y * weights
                out_ref[r, 1, k, h] = (x[h] * x[h] * x[h] - x[h]) * weights


def stencil_stage(phase, velocity, weights, halos, scale_phi, scale_theta):
    shells, rows, cols = phase.shape
    kb = 32

    def kernel(*refs):
        stencil_kernel(scale_phi, *refs)

    return pl.pallas_call(
        kernel,
        grid=(shells // kb,),
        in_specs=[
            pl.BlockSpec(memory_space=pltpu.SMEM),
            pl.BlockSpec((kb, rows, cols), lambda i: (i, 0, 0)),
            pl.BlockSpec((2, kb, rows, cols), lambda i: (0, i, 0, 0)),
            pl.BlockSpec(weights.shape, lambda i: (0, 0)),
            pl.BlockSpec((kb, cols), lambda i: (i, 0)),
            pl.BlockSpec((rows, 128), lambda i: (0, 0)),
            pl.BlockSpec((rows, 128), lambda i: (0, 0)),
            pl.BlockSpec((kb, cols), lambda i: (i, 0)),
        ],
        out_specs=pl.BlockSpec((rows // 8, 2, kb, cols // 128, 8, 128), lambda i: (0, 0, i, 0, 0, 0)),
        out_shape=jax.ShapeDtypeStruct((rows // 8, 2, shells, cols // 128, 8, 128), f32),
        compiler_params=params(48),
        name="stencil",
    )(scale_theta, phase, velocity, weights, *halos)


def cos_and_minus_sin(turns, full):
    shift = (full // 4).bit_length() - 1
    quadrant = (turns + full // 8) >> shift
    rest = turns - (quadrant << shift)
    x = rest.astype(f32) * (2.0 * math.pi / full)
    q = quadrant & 3
    x2 = x * x
    cos = 1.0 + x2 * (-1.0 / 2 + x2 * (1.0 / 24 + x2 * (-1.0 / 720 + x2 * (1.0 / 40320))))
    sin = x + x * x2 * (-1.0 / 6 + x2 * (1.0 / 120 + x2 * (-1.0 / 5040 + x2 * (1.0 / 362880))))
    swap = (q & 1) == 1
    c = jnp.where(swap, sin, cos)
    s = jnp.where(swap, cos, sin)
    return jnp.where((q == 1) | (q == 2), -c, c), jnp.where(q >= 2, s, -s)


def table_kernel(mode_ref, out_ref):
    parities, modes, _ = mode_ref.shape
    half_phi = out_ref.shape[2]
    tiles = half_phi // 128
    lane = lax.broadcasted_iota(jnp.int32, (modes, 128), 1)
    for parity in range(parities):
        orders = mode_ref[parity]
        fc, fs = cos_and_minus_sin(orders * lane, 2 * half_phi)
        coarse_c, coarse_s = cos_and_minus_sin(orders * lane * 128, 2 * half_phi)
        for u in range(tiles):
            cc = jnp.broadcast_to(coarse_c[:, u : u + 1], (modes, 128))
            cs = jnp.broadcast_to(coarse_s[:, u : u + 1], (modes, 128))
            for i, value in enumerate((fc * cc - fs * cs, fs * cc + fc * cs)):
                h, l = split(value)
                lanes = slice(128 * u, 128 * u + 128)
                out_ref[parity, i * modes : (i + 1) * modes, lanes] = h
                out_ref[parity, (2 + i) * modes : (3 + i) * modes, lanes] = l


def wave_tables(owned_modes, phi_count):
    first_half = owned_modes[:, :2].T.reshape(-1)
    top = owned_modes.shape[0] * owned_modes.shape[1] - 1
    even = jnp.where(first_half % 2 == 0, first_half, top - first_half)
    modes = jnp.stack([even, top - even])
    count = modes.shape[1]
    whole = pl.BlockSpec(memory_space=pltpu.VMEM)
    return pl.pallas_call(
        table_kernel,
        in_specs=[whole],
        out_specs=whole,
        out_shape=jax.ShapeDtypeStruct((2, 4 * count, phi_count // 2), bf16),
        compiler_params=params(24),
        name="table",
    )(jnp.broadcast_to(modes[:, :, None], (2, count, 128)))


def fourier_kernel(p_ref, table_ref, out_ref, xh, xl):
    parts, fields = p_ref.shape[:2]
    half = parts // 2
    per = xh.shape[1] // 8
    tiles = xh.shape[2] // half // 128
    both = table_ref.shape[1] // 2
    count = both // 2
    owners = count // 2
    stride = out_ref.shape[0] // owners

    def one(f, carry):
        for a in range(half):
            for t in range(8):
                for j in range(tiles):
                    strided = pl.ds(8 * j + t, per, stride=8 * tiles)
                    near, far = p_ref[a, f, strided, :], p_ref[a + half, f, strided, :]
                    lanes = slice((a * tiles + j) * 128, (a * tiles + j + 1) * 128)
                    for parity, x in enumerate((near + far, near - far)):
                        h, l = split(x)
                        xh[parity, t * per : (t + 1) * per, lanes] = h
                        xl[parity, t * per : (t + 1) * per, lanes] = l
        for parity in range(2):
            y = dot_nt(table_ref[parity], xh[parity])
            y = y[:both] + (y[both:] + dot_nt(table_ref[parity, :both], xl[parity]))
            for u in range(4):
                pair = swap_halves(y[:count, 128 * u : 128 * u + 128], y[count:, 128 * u : 128 * u + 128])
                for s in range(2):
                    for v in range(2):
                        at = f * (stride // fields) + (2 * parity + s) * 8 + 2 * u + v
                        out_ref[pl.ds(at, owners, stride=stride), :] = pair[v][s * owners : (s + 1) * owners]
        return carry

    lax.fori_loop(0, fields, one, 0)


def fourier_stage(rows_all, table):
    parts, fields, shells, tiles, tb, _ = rows_all.shape
    half_phi = table.shape[2]
    owners = table.shape[1] // 8
    flat = rows_all.reshape(parts, fields, shells * tiles * tb, 128)
    whole = pl.BlockSpec(memory_space=pltpu.VMEM)
    out = pl.pallas_call(
        fourier_kernel,
        in_specs=[whole, whole],
        out_specs=whole,
        out_shape=jax.ShapeDtypeStruct((owners * fields * 4 * 8, 128), f32),
        scratch_shapes=[
            pltpu.VMEM((2, shells * tb, half_phi), bf16),
            pltpu.VMEM((2, shells * tb, half_phi), bf16),
        ],
        compiler_params=params(32),
        name="fourier",
    )(flat, table)
    return out.reshape(owners, fields, 2, 2, 8, 128)


def spectral_kernel(az, col, mode_ref, r_ref, leg, rad, fac_ref, out_ref, xh, xl, rhs, sol, radf):
    degrees = leg.shape[2]
    shells = rad.shape[0]
    tb = az * 8
    tiles = degrees // 128
    half = degrees // 2
    for q in range(4):
        parity = mode_ref[q] % 2
        for f in range(2):
            x = jnp.concatenate(
                [r_ref[a * col + c, f, parity, q % 2] for c in range(col) for a in range(az)], axis=0
            )
            h, l = split(x.T)
            xh[q, f * 128 : (f + 1) * 128, :] = h
            xl[q, f * 128 : (f + 1) * 128, :] = l

    def right_side(q, lanes):
        coef = dot_nn(xh[q], leg[q, :, lanes]) + dot_nn(xl[q], leg[q, :, lanes])
        return coef[:128] - fac_ref[:, lanes] * coef[128:]

    def put(q, first, right):
        for i in range(2):
            for n in range(tiles // 2):
                rhs[first + n, pl.ds(2 * q + i, shells, stride=8), :] = right[
                    i * shells : (i + 1) * shells, n * 128 : n * 128 + 128
                ]

    for q in range(4):
        put(q, tiles // 2, right_side(q, slice(half, degrees)))
    low = [jnp.where(mode_ref[s] < half, s, s + 2) for s in range(2)]
    high = [jnp.where(mode_ref[s] < half, s + 2, s) for s in range(2)]
    for s in range(2):
        put(low[s], 0, right_side(low[s], slice(0, half)))
        put(high[s], 0, jnp.zeros((2 * shells, half), f32))

    rb = 8

    def outer(block, carry):
        radf[...] = rad[pl.ds(block * rb, rb)].astype(f32)
        for lt in range(tiles):
            lanes = slice(lt * 128, lt * 128 + 128)
            acc = [jnp.zeros((8, 128), f32) for _ in range(rb)]
            for s in range(shells):
                v = rhs[lt, 8 * s : 8 * s + 8, :]
                for r in range(rb):
                    acc[r] = acc[r] + radf[r, s : s + 1, lanes] * v
            for r in range(rb):
                sol[lt, pl.ds(pl.multiple_of((block * rb + r) * 8, 8), 8), :] = acc[r]
        return carry

    lax.fori_loop(0, shells // rb, outer, 0)

    for s in range(2):
        for q, first in ((low[s], 0), (high[s], tiles // 2)):
            gain = jnp.where(mode_ref[q] == 0, 1.0, 2.0).astype(f32)
            x = jnp.concatenate(
                [
                    jnp.concatenate(
                        [sol[lt, pl.ds(2 * q + i, shells, stride=8), :] for lt in range(first, tiles)], axis=1
                    )
                    for i in range(2)
                ],
                axis=0,
            )
            h, l = split(x * gain)
            matrix = leg[q, :, first * 128 :]
            y = dot_nt(matrix, h) + dot_nt(matrix, l)
            slot = 2 * (mode_ref[q] % 2) + s
            for c in range(col):
                for a in range(az):
                    out_ref[a * col + c, slot] = y[c * tb + a * 8 : c * tb + a * 8 + 8]


def spectral_stage(received, legendre, radial, factor, own, az, col):
    owners = received.shape[0]
    modes, theta, degrees = legendre.shape
    shells = radial.shape[0]

    def kernel(*refs):
        spectral_kernel(az, col, *refs)

    whole = pl.BlockSpec(memory_space=pltpu.VMEM)
    return pl.pallas_call(
        kernel,
        in_specs=[pl.BlockSpec(memory_space=pltpu.SMEM), whole, whole, whole, whole],
        out_specs=whole,
        scratch_shapes=[
            pltpu.VMEM((4, 256, theta), bf16),
            pltpu.VMEM((4, 256, theta), bf16),
            pltpu.VMEM((degrees // 128, 8 * shells, 128), f32),
            pltpu.VMEM((degrees // 128, 8 * shells, 128), f32),
            pltpu.VMEM((8, shells, degrees), f32),
        ],
        out_shape=jax.ShapeDtypeStruct((owners, 4, 8, 128), f32),
        compiler_params=params(32),
        name="spectral",
    )(own, received, legendre, radial, factor)


def inverse_kernel(z_ref, table_ref, out_ref, gh, gl):
    owners = z_ref.shape[0] // 32
    rows = gh.shape[1]
    per = rows // 8
    both = table_ref.shape[1] // 2
    quarters = out_ref.shape[1]
    cols = table_ref.shape[2] // quarters
    tiles = cols // 128
    for par in range(2):
        halves = [[], []]
        for s in range(2):
            base = (par * 2 + s) * 8
            cos_u, sin_u = [], []
            for u in range(4):
                a = z_ref[pl.ds(base + 2 * u, owners, stride=32), :]
                b = z_ref[pl.ds(base + 2 * u + 1, owners, stride=32), :]
                first, second = swap_halves(a, b)
                cos_u.append(first)
                sin_u.append(second)
            halves[0].append(jnp.concatenate(cos_u, axis=1))
            halves[1].append(jnp.concatenate(sin_u, axis=1))
        for i in range(2):
            for s in range(2):
                h, l = split(halves[i][s].T)
                at = (2 * i + s) * owners
                gh[par, :, at : at + owners] = h
                gh[par, :, both + at : both + at + owners] = h
                gl[par, :, at : at + owners] = l

    for quarter in range(quarters):
        lanes = slice(quarter * cols, (quarter + 1) * cols)
        sums = []
        for par in range(2):
            sums.append(dot_nn(gh[par], table_ref[par, :, lanes]) + dot_nn(gl[par], table_ref[par, :both, lanes]))
        near = sums[0] + sums[1]
        far = sums[0] - sums[1]
        for t in range(8):
            for j in range(tiles):
                part = slice(j * 128, j * 128 + 128)
                strided = pl.ds(8 * j + t, per, stride=8 * tiles)
                out_ref[0, quarter, strided, :] = near[t * per : (t + 1) * per, part]
                out_ref[1, quarter, strided, :] = far[t * per : (t + 1) * per, part]


def inverse_stage(received, table, shells, az):
    owners, _, tb, _ = received.shape
    half_phi = table.shape[2]
    modes2 = table.shape[1] // 2
    flat = received.reshape(owners * 4 * tb, 128)
    cols = 2 * half_phi // az
    rows = shells * tb
    whole = pl.BlockSpec(memory_space=pltpu.VMEM)
    out = pl.pallas_call(
        inverse_kernel,
        in_specs=[whole, whole],
        out_specs=whole,
        out_shape=jax.ShapeDtypeStruct((2, az // 2, rows * cols // 128, 128), f32),
        scratch_shapes=[
            pltpu.VMEM((2, rows, 2 * modes2), bf16),
            pltpu.VMEM((2, rows, modes2), bf16),
        ],
        compiler_params=params(32),
        name="inverse",
    )(flat, table)
    return out.reshape(az, shells, cols // 128, tb, 128)


def gather_kernel(w_ref, out_ref, sem):
    parts, shells, tiles = w_ref.shape[:3]
    copies = []
    for a in range(parts):
        for h in range(tiles):
            copies.append(
                pltpu.make_async_copy(
                    w_ref.at[a, :, h],
                    out_ref.at[:, pl.ds(8 * a, 8), pl.ds(128 * h, 128)],
                    sem.at[a * tiles + h],
                )
            )
    for copy in copies:
        copy.start()
    for copy in copies:
        copy.wait()


def gather_stage(blocks):
    parts, shells, tiles, tb, _ = blocks.shape
    return pl.pallas_call(
        gather_kernel,
        in_specs=[pl.BlockSpec(memory_space=pltpu.VMEM)],
        out_specs=pl.BlockSpec(memory_space=pl.ANY),
        out_shape=jax.ShapeDtypeStruct((shells, parts * tb, tiles * 128), f32),
        scratch_shapes=[pltpu.SemaphoreType.DMA((parts * tiles,))],
        compiler_params=params(16),
        name="gather",
    )(blocks)


def exchange(x, axes):
    return lax.all_to_all(x, axes, split_axis=0, concat_axis=0, tiled=True)


def body(phase_field, velocity, owned_modes, legendre, radial_inverse):
    shells, theta_local, phi_local = phase_field.shape
    az_count = lax.axis_size("az")
    col_count = lax.axis_size("col")
    az_here = lax.axis_index("az")
    col_here = lax.axis_index("col")
    phi_count = phi_local * az_count
    theta_count = theta_local * col_count
    degree_count = legendre.shape[2]
    radius = shell_radii(shells)

    weights = (colat_weights(theta_count) / phi_count).astype(np.float32)
    weights = jnp.asarray(np.repeat(weights[:, None], 128, axis=1))

    az_even, az_odd, col_even, col_odd = edges_stage(phase_field)
    even_az = [(i, i ^ 1) for i in range(az_count)]
    odd_az = [(i, (i + 1 if i % 2 else i - 1) % az_count) for i in range(az_count)]
    even_col = [(i, i ^ 1) for i in range(col_count)]
    odd_col = [(i, i + 1 if i % 2 else i - 1) for i in range(1, col_count - 1)]
    halos = (
        lax.ppermute(col_odd, "col", odd_col),
        lax.ppermute(az_odd, "az", odd_az),
        lax.ppermute(az_even, "az", even_az),
        lax.ppermute(col_even, "col", even_col),
    )

    here = az_here * col_count + col_here
    own = lax.dynamic_slice(owned_modes, (here, 0), (1, owned_modes.shape[1])).reshape(-1)
    degrees = np.arange(degree_count)
    factor = mobility_step * (degrees * (degrees + 1.0))[None, :] / (radius * radius)[:, None]
    factor = jnp.asarray(np.concatenate([factor, factor], axis=0).astype(np.float32))
    radial = jnp.transpose(radial_inverse, (1, 2, 0))
    table = wave_tables(owned_modes, phi_count)

    scale_phi = step_time * phi_count / (4.0 * math.pi)
    scale_theta = jnp.asarray((step_time * theta_count / (2.0 * math.pi) / radius).astype(np.float32))
    fields = stencil_stage(
        phase_field, velocity, weights, halos, scale_phi, scale_theta
    )
    fields, table, own = lax.optimization_barrier((fields, table, own))
    received = exchange(fourier_stage(exchange(fields, "az"), table), everyone)
    synthesis = spectral_stage(
        received, legendre, radial, factor, own, az_count, col_count
    )
    grid_modes = exchange(synthesis, everyone)

    blocks = inverse_stage(grid_modes, table, shells, az_count)
    return gather_stage(exchange(blocks, "az"))


def solution(mesh):
    in_specs = (
        P(None, "col", "az"),
        P(None, None, "col", "az"),
        P(),
        P(("az", "col"), None, None),
        P(),
    )
    out_specs = P(None, "col", "az")
    return jax.shard_map(body, mesh=mesh, in_specs=in_specs, out_specs=out_specs, check_vma=False)
```
